32 devices in a mesh: dp: 4 (over z), tensor: 4 (over y, x), section: 2 (over core).
Axes of the slice: x: 2, y: 2, z: 4, core: 2. Of those that a mesh axis runs over, the one named last changes fastest.
Arguments:
- grads: bfloat16 [4, 2, 768, 768], P('dp', 'section', 'tensor'), may hold values from -6 to 6
- errors: float32 [4, 2, 768, 768], P('dp', 'section', 'tensor'), may hold values from -3 to 3
- q_prev: float32 [2, 768, 32], P('section'), may hold values from -0.21875 to 0.21875
- p_root: float32 [2, 32, 32], P('section')
- q_root: float32 [2, 32, 32], P('section')
- momentum: float32 [2, 768, 768], P('section', 'tensor')
- weights: float32 [2, 768, 768], P('section', 'tensor'), may hold values from -0.21875 to 0.21875
- vec_grads: float32 [4, 2, 3, 768], P('dp', 'section', None, 'tensor'), may hold values from -6 to 6
- vec_momentum: float32 [2, 3, 768], P('section', None, 'tensor'), may hold values from -6 to 6
- vec_params: float32 [2, 3, 768], P('section', None, 'tensor'), may hold values from -3 to 3
Outputs:
- errors_out: float32 [4, 2, 768, 768], P('dp', 'section', 'tensor')
- p_factor: float32 [2, 768, 32], P('section', 'tensor')
- q_factor: float32 [2, 768, 32], P('section')
- momentum_out: float32 [2, 768, 768], P('section', 'tensor')
- weights_out: float32 [2, 768, 768], P('section', 'tensor')
- vec_momentum_out: float32 [2, 3, 768], P('section', None, 'tensor')
- vec_params_out: float32 [2, 3, 768], P('section', None, 'tensor')
The draws below stay inside these ranges and needn't reach their ends.
All inputs are finite; a program needn't handle non-finite values.
Results may differ from the reference program's by a relative error of at most 0.0003.
Values sent between devices are 32-bit elements; how exact they have to be, the bound alone decides.
A program may use at most 64 MiB of HBM per device.

```python
import math
import jax
import jax.numpy as jnp
from jax import lax

D = 768
R = 32
REPLICAS = 4
TENSOR_WAYS = 4


def make_root(key, factor):
    key_diag, key_off = jax.random.split(key)
    diag_part = jax.random.uniform(key_diag, (2, R, R), jnp.float32, 1.0, 2.0)
    off_part = jnp.clip(0.1 * jax.random.normal(key_off, (2, R, R), jnp.float32), -0.4, 0.4)
    eye_mask = jnp.eye(R, dtype=jnp.float32)[None]
    return (eye_mask * diag_part + (1.0 - eye_mask) * off_part) * factor


def draw_p_root(key, part):
    return make_root(jax.random.fold_in(key, 11), 1.0 / math.sqrt(REPLICAS))


def draw_q_root(key, part):
    return make_root(jax.random.fold_in(key, 23), 2.0 / math.sqrt(REPLICAS * D))


def draw_momentum(key, part):
    key = jax.random.fold_in(key, 37)
    key_base, key_rows, key_cols = jax.random.split(key, 3)
    rows_factor = jnp.exp(jax.random.uniform(key_rows, (2, D, 1), jnp.float32) * math.log(10.0))
    cols_factor = jnp.exp(jax.random.uniform(key_cols, (2, 1, D), jnp.float32) * math.log(10.0))
    row_index = jnp.arange(D, dtype=jnp.int32)[None, :, None]
    section_index = jnp.arange(2, dtype=jnp.int32)[:, None, None]
    position = (2 * (row_index // (D // TENSOR_WAYS)) + section_index).astype(jnp.float32)
    base = jnp.clip(jax.random.normal(key_base, (2, D, D), jnp.float32), -6.0, 6.0)
    trend = jnp.exp(math.log(3.0) * position / (2 * TENSOR_WAYS - 1))
    return 0.1 * base * rows_factor * cols_factor * trend


def steps_of(own_key, dims, cuts, smallest, largest):
    level = 1.0
    for dim, blocks in cuts:
        steps = jax.random.uniform(jax.random.fold_in(jax.random.fold_in(own_key, 6), dim), (blocks,), jnp.float32, smallest / len(cuts), largest / len(cuts))
        level = level * jnp.repeat(jnp.exp(steps), dims[dim] // blocks).reshape((-1,) + (1,) * (len(dims) - 1 - dim))
    return level


def scatter_about(stream_key, shape, width, bound, cuts=(), kind=jnp.bfloat16):
    array = width * jax.random.normal(stream_key, shape, jnp.float32)
    if cuts:
        array = array * steps_of(stream_key, shape, cuts, -0.22, 0.18)
    return jnp.clip(array, -bound, bound).astype(kind)


def setup_inputs(seed: int = 0) -> dict:
    key_list = jax.random.split(jax.random.key(seed), 11)
    return {
        "grads": scatter_about(key_list[0], (REPLICAS, 2, D, D), 1.0, 6.0, ((0, 4), (1, 2), (2, 4))),
        "errors": scatter_about(key_list[1], (REPLICAS, 2, D, D), 0.5, 3.0, ((0, 4), (1, 2), (2, 4)), jnp.float32),
        "q_prev": scatter_about(key_list[2], (2, D, R), D ** -0.5, 0.21875, ((0, 2),), jnp.float32),
        "p_root": draw_p_root(jax.random.fold_in(key_list[10], 71), 0),
        "q_root": draw_q_root(jax.random.fold_in(key_list[10], 71), 0),
        "momentum": draw_momentum(jax.random.fold_in(key_list[10], 71), 0),
        "weights": scatter_about(key_list[6], (2, D, D), D ** -0.5, 0.21875, ((0, 2), (1, 4)), jnp.float32),
        "vec_grads": scatter_about(key_list[7], (REPLICAS, 2, 3, D), 1.0, 6.0, ((0, 4), (1, 2), (3, 4)), jnp.float32),
        "vec_momentum": scatter_about(key_list[8], (2, 3, D), 1.0, 6.0, ((0, 2), (2, 4)), jnp.float32),
        "vec_params": scatter_about(key_list[9], (2, 3, D), 0.5, 3.0, ((0, 2), (2, 4)), jnp.float32),
    }


HIGH = lax.Precision.HIGHEST

def reference(grads, errors, q_prev, p_root, q_root, momentum, weights, vec_grads, vec_momentum, vec_params):
    merged = grads.astype(jnp.float32) + errors
    p_sum = jnp.einsum('nsdc,sck->sdk', merged, q_prev, precision=HIGH)
    p_factor = jnp.einsum('sdk,skj->sdj', p_sum, p_root, precision=HIGH)
    q_sum = jnp.einsum('nsdc,sdk->sck', merged, p_factor, precision=HIGH)
    q_factor = jnp.einsum('sck,skj->scj', q_sum, q_root, precision=HIGH)
    approx = jnp.einsum('sdk,sck->sdc', p_factor, q_factor, precision=HIGH) / REPLICAS
    errors_out = merged - approx[None]
    vec_mean = lax.optimization_barrier(jnp.sum(vec_grads, axis=0)) / REPLICAS
    momentum_out = 0.9 * momentum + approx
    vec_momentum_out = 0.9 * vec_momentum + vec_mean
    total = jnp.sum(momentum_out * momentum_out) + jnp.sum(vec_momentum_out * vec_momentum_out)
    scale = 0.05 / jnp.sqrt(total / (2 * D * D + 6 * D) + 1e-06)
    weights_out = weights - scale * momentum_out
    vec_params_out = vec_params - scale * vec_momentum_out
    return (errors_out, p_factor, q_factor, momentum_out, weights_out, vec_momentum_out, vec_params_out)
```

```python
import functools

import jax
import jax.numpy as jnp
from jax import lax
from jax.experimental import pallas as pl
from jax.experimental.pallas import tpu as pltpu
from jax.sharding import PartitionSpec as P

F32 = jnp.float32
BF16 = jnp.bfloat16
MESH = pl.DeviceIdType.MESH
LANES = 128
UNROLL = 16
WRITES = 4


def split(x):
    high = x.astype(BF16)
    return high, (x - high.astype(F32)).astype(BF16)


def mm(a, b, dims=((1,), (0,))):
    return lax.dot_general(a, b, (dims, ((), ())), preferred_element_type=F32)


def left_parts(x):
    high, low = split(x)
    return jnp.concatenate([high, high, low], axis=1)


def right_parts(x):
    high, low = split(x)
    return jnp.concatenate([high, low, high], axis=0)


def each(count, body):
    if count <= UNROLL:
        for i in range(count):
            body(i)
    else:
        lax.fori_loop(0, count, lambda i, c: (body(i), c)[1], 0)


def total_of(ref, count):
    if count <= UNROLL:
        total = ref[0]
        for i in range(1, count):
            total = total + ref[i]
        return total
    return lax.fori_loop(1, count, lambda i, acc: acc + ref[i], ref[0])


def row_blocks(rows):
    return [(r, min(LANES, rows - r)) for r in range(0, rows, LANES)]


def packed_rows(rank, rows):
    return rank * rows // LANES


def pack(part):
    rank, size = part.shape
    count = LANES // size
    step = rank // count
    return jnp.concatenate([part[i * step : (i + 1) * step] for i in range(count)], axis=1)


def unpack(x, rank, rows):
    parts = []
    for start, size in row_blocks(rows):
        count = LANES // size
        step = rank // count
        block = x[rank * start // LANES :][:step]
        parts.append(
            jnp.concatenate([block[:, i * size : (i + 1) * size] for i in range(count)], axis=0)
        )
    return jnp.concatenate(parts, axis=1)


class Owners:
    def __init__(self, n_dp, n_t, width):
        self.count = width // LANES
        self.planes = -(-self.count // n_t)
        self.per_plane = -(-self.count // self.planes)
        self.first = (n_dp - self.planes) // 2

    def dp(self, k):
        return self.first + k // self.per_plane

    def tensor(self, k):
        return k % self.per_plane


def kernel(
    sizes,
    g_hbm, e_hbm, qt_hbm, pr_hbm, qr_hbm, m_hbm, w_hbm, vg_hbm, vm_hbm, vp_hbm,
    eo_v, pf_v, qf_v, mo_v, w_v, vmo_v, vp_v, tot_v,
    g_v, e_v, qt_v, pr_v, qr_v, m_v, vm_v,
    hi_v, lo_v, pbuf, vbuf, lbuf, vsq, mbuf, qpart, rbuf, qfull, left_v, tiles,
    in_sem, psend, precv, vsend, vrecv, lsend, lrecv, xsend, xrecv, msend, mrecv,
    rsend, rrecv, asend, arecv, tsend, trecv,
):
    n_dp, n_t, n_s = sizes
    n = n_dp * n_t
    group = n_t * n_s
    dp, tn, sc = lax.axis_index("dp"), lax.axis_index("tensor"), lax.axis_index("section")
    me = dp * n_t + tn
    rank, width = qt_v.shape
    rows = e_v.shape[0]
    own = Owners(n_dp, n_t, width)
    chunks, per_plane, planes = own.count, own.per_plane, own.planes
    plane = dp - own.first
    mine = plane * per_plane + tn
    owns = jnp.logical_and(
        jnp.logical_and(plane >= 0, plane < planes),
        jnp.logical_and(tn < per_plane, mine < chunks),
    )
    upper = 2 * dp < n_dp

    def load(i, src, dst):
        copy = pltpu.make_async_copy(src, dst, in_sem.at[i])
        copy.start()
        return copy

    blocks = row_blocks(rows)
    in_q = load(0, qt_hbm, qt_v)
    in_pr = load(1, pr_hbm, pr_v)
    in_g, in_e = [], []
    for b, (start, size) in enumerate(blocks):
        at = pl.ds(start, size)
        in_g.append(load(9 + 2 * b, g_hbm.at[at], g_v.at[at]))
        in_e.append(load(10 + 2 * b, e_hbm.at[at], e_v.at[at]))
    in_vg = load(2, vg_hbm, vbuf.at[dp])
    in_qr = load(3, qr_hbm, qr_v)
    in_vm = load(4, vm_hbm, vm_v)
    in_m = load(5, m_hbm, m_v)
    in_vp = load(6, vp_hbm, vp_v)
    in_w = load(7, w_hbm, w_v)

    barrier = pltpu.get_barrier_semaphore()
    slot = sc * n_t + tn

    def line_peer(i):
        up, down = n_dp - 1 - i, i
        return jnp.where(
            upper, jnp.where(up > dp, up, up - 1), jnp.where(down < dp, down, down + 1)
        )

    def greet_line(i):
        pl.semaphore_signal(
            barrier, inc=1, device_id=(line_peer(i), tn, sc), device_id_type=MESH
        )

    def greet_plane(i):
        peer = lax.rem(slot + 1 + i, group)
        pl.semaphore_signal(
            barrier, inc=1, device_id=(dp, lax.rem(peer, n_t), peer // n_t), device_id_type=MESH
        )

    each(n_dp - 1, greet_line)
    each(group - 1, greet_plane)

    in_q.wait()
    in_pr.wait()
    q_hi, q_lo = split(mm(left_parts(pr_v[...].T), right_parts(qt_v[...])))
    q_both = jnp.concatenate([q_hi, q_lo], axis=0)
    span = per_plane * LANES
    for b, (start, size) in enumerate(blocks):
        at = pl.ds(start, size)
        in_g[b].wait()
        in_e[b].wait()
        merged = g_v[at, :].astype(F32) + e_v[at, :]
        e_v[at, :] = merged
        m_hi, m_lo = split(merged)
        for p in range(planes):
            hi_v[p, at, :] = m_hi[:, p * span : (p + 1) * span]
            lo_v[p, at, :] = m_lo[:, p * span : (p + 1) * span]
        first = mm(q_both, m_hi, ((1,), (1,)))
        second = mm(q_hi, m_lo, ((1,), (1,)))
        pbuf[dp, pl.ds(rank * start // LANES, rank * size // LANES), :] = pack(
            first[:rank] + first[rank:] + second
        )

    pl.semaphore_wait(barrier, n_dp - 1 + group - 1)

    def send_p(i):
        pltpu.make_async_remote_copy(
            pbuf.at[dp], pbuf.at[dp], psend, precv,
            device_id=(line_peer(i), tn, sc), device_id_type=MESH,
        ).start()

    def send_v(i):
        pltpu.make_async_remote_copy(
            vbuf.at[dp], vbuf.at[dp], vsend, vrecv,
            device_id=(line_peer(i), tn, sc), device_id_type=MESH,
        ).start()

    each(n_dp - 1, send_p)
    in_vg.wait()
    each(n_dp - 1, send_v)

    def to_owner(k, src, dst, send, recv):
        return pltpu.make_async_remote_copy(
            src, dst, send.at[k], recv,
            device_id=(own.dp(k), own.tensor(k), sc), device_id_type=MESH,
        )

    def beside(k):
        return jnp.logical_and(dp == own.dp(k), tn != own.tensor(k))

    def columns(k):
        return m_v.at[:, pl.ds(k * LANES, LANES)]

    in_m.wait()
    for k in range(chunks):

        @pl.when(beside(k))
        def _():
            to_owner(k, columns(k), mbuf.at[tn], msend, mrecv).start()

        @pl.when(jnp.logical_and(owns, mine == k))
        def _():
            mbuf[tn] = columns(k)[...]

    in_qr.wait()
    in_vm.wait()
    q_root_left = left_parts(qr_v[...])

    others = pl.ds(0, n_dp - 1)
    pltpu.make_async_copy(pbuf.at[others], pbuf.at[others], precv).wait()
    pf = unpack(total_of(pbuf, n_dp), rank, rows)
    pf_hi, pf_lo = split(pf)
    pf_both = jnp.concatenate([pf_hi, pf_lo], axis=0)

    for i in range(planes):
        p = jnp.where(upper, planes - 1 - i, i)
        first = mm(pf_both, hi_v[p])
        second = mm(pf_hi, lo_v[p])
        part = first[:rank] + first[rank:] + second
        for j in range(per_plane):
            k = p * per_plane + j
            block = part[:, j * LANES : (j + 1) * LANES]
            here = jnp.logical_and(owns, mine == k)

            @pl.when(here)
            def _():
                rbuf[me] = block

            @pl.when(jnp.logical_not(here))
            def _():
                qpart[k] = block
                pltpu.make_async_remote_copy(
                    qpart.at[k], rbuf.at[me], rsend, rrecv,
                    device_id=(own.first + p, j, sc), device_id_type=MESH,
                ).start()

    pf_v[...] = pf
    left_t = mm(q_root_left, right_parts(pf)) / n_dp
    for start, size in blocks:
        lbuf[tn, pl.ds(rank * start // LANES, rank * size // LANES), :] = pack(
            left_t[:, start : start + size]
        )
    left = left_parts(left_t.T)
    pltpu.make_async_copy(vbuf.at[others], vbuf.at[others], vrecv).wait()
    v_new = 0.9 * vm_v[...] + total_of(vbuf, n_dp) / n_dp
    vmo_v[...] = v_new
    v_square = jnp.sum(v_new * v_new)
    lane = lax.broadcasted_iota(jnp.int32, (1, LANES), 1)
    vsq[tn] = jnp.where(lane == 0, v_square, 0.0)
    for k in range(chunks):

        @pl.when(beside(k))
        def _():
            to_owner(k, lbuf.at[tn], lbuf.at[tn], lsend, lrecv).start()
            to_owner(k, vsq.at[tn], vsq.at[tn], xsend, xrecv).start()

    half = 2 if n_t % 2 == 0 else 1

    def far_tensor(j):
        outer = lax.rem(n_t // half - 1 - tn // half + j // half + n_t, n_t // half)
        inner = lax.rem(half - 1 - lax.rem(tn, half) + j % half + half, half)
        return outer * half + inner

    def far_dp(i):
        return jnp.where(upper, n_dp - 1 - i, i)

    @pl.when(owns)
    def _():
        rest = pl.ds(0, n_t - 1)
        pltpu.make_async_copy(lbuf.at[rest], lbuf.at[rest], lrecv).wait()
        pltpu.make_async_copy(vsq.at[rest], vsq.at[rest], xrecv).wait()
        for t in range(n_t):
            left_v[t] = left_parts(unpack(lbuf[t], rank, rows).T)
        pltpu.make_async_copy(mbuf.at[rest], mbuf.at[rest], mrecv).wait()
        v_squares = total_of(vsq, n_t)

        whole = pl.ds(0, n - 1)
        pltpu.make_async_copy(rbuf.at[whole], rbuf.at[whole], rrecv).wait()
        q_sum = total_of(rbuf, n)
        qfull[mine] = q_sum

        def send_sum(i):
            to_dp = far_dp(i // n_t)
            to_tensor = far_tensor(i % n_t)

            @pl.when(to_dp * n_t + to_tensor != me)
            def _():
                pltpu.make_async_remote_copy(
                    qfull.at[mine], qfull.at[mine], asend, arecv,
                    device_id=(to_dp, to_tensor, sc), device_id_type=MESH,
                ).start()

        each(n, send_sum)

        right = right_parts(q_sum)
        squares = jnp.zeros((8, LANES), F32)
        for t in range(n_t):
            new = 0.9 * mbuf[t] + mm(left_v[t], right)
            squares = squares + jnp.sum((new * new).reshape(rows // 8, 8, LANES), axis=0)
        row = jnp.sum(squares, axis=0, keepdims=True) + jnp.where(mine == 0, v_squares, 0.0)
        at = sc * chunks + mine
        tiles[at] = row

        def send_row(i):
            to_dp = far_dp(i // group)
            to_tensor = far_tensor((i // n_s) % n_t)
            to_section = lax.rem(sc + 1 + i % n_s, n_s)

            @pl.when(jnp.logical_or(to_dp * n_t + to_tensor != me, to_section != sc))
            def _():
                pltpu.make_async_remote_copy(
                    tiles.at[at], tiles.at[at], tsend, trecv,
                    device_id=(to_dp, to_tensor, to_section), device_id_type=MESH,
                ).start()

        if n * n_s <= 2 * UNROLL:
            for i in range(n * n_s):
                send_row(i)
        else:
            each(n * n_s, send_row)
        got = pl.ds(0, chunks - 1)
        pltpu.make_async_copy(qfull.at[got], qfull.at[got], arecv).wait()

    @pl.when(jnp.logical_not(owns))
    def _():
        pltpu.make_async_copy(qfull, qfull, arecv).wait()

    q_root_t = left_parts(qr_v[...].T)
    block = 2
    for c in range(0, chunks, block):
        cols = pl.ds(c * LANES, block * LANES)
        right = right_parts(jnp.concatenate([qfull[c + j] for j in range(block)], axis=1))
        approx = mm(left, right)
        mo_v[:, cols] = 0.9 * m_v[:, cols] + approx
        eo_v[:, cols] = e_v[:, cols] - approx
        qf_v[:, cols] = mm(q_root_t, right)
    in_w.wait()
    in_vp.wait()

    count = n_s * chunks

    @pl.when(owns)
    def _():
        got = pl.ds(0, count - 1)
        pltpu.make_async_copy(tiles.at[got], tiles.at[got], trecv).wait()

    @pl.when(jnp.logical_not(owns))
    def _():
        got = pl.ds(0, count)
        pltpu.make_async_copy(tiles.at[got], tiles.at[got], trecv).wait()

    tot_v[...] = total_of(tiles, count)

    pltpu.make_async_copy(pbuf.at[others], pbuf.at[others], psend).wait()
    pltpu.make_async_copy(vbuf.at[others], vbuf.at[others], vsend).wait()
    for k in range(chunks):

        @pl.when(beside(k))
        def _():
            to_owner(k, columns(k), mbuf.at[tn], msend, mrecv).wait_send()
            to_owner(k, lbuf.at[tn], lbuf.at[tn], lsend, lrecv).wait_send()
            to_owner(k, vsq.at[tn], vsq.at[tn], xsend, xrecv).wait_send()

    @pl.when(owns)
    def _():
        got = pl.ds(0, chunks - 1)
        pltpu.make_async_copy(qfull.at[got], qfull.at[got], rsend).wait()
        whole = pl.ds(0, n - 1)
        pltpu.make_async_copy(rbuf.at[whole], rbuf.at[whole], asend).wait()
        sent = tiles.at[pl.ds(0, n * n_s - 1)]
        pltpu.make_async_copy(sent, sent, tsend).wait()

    @pl.when(jnp.logical_not(owns))
    def _():
        pltpu.make_async_copy(qfull, qfull, rsend).wait()


def finish(
    entries,
    eo_v, pf_v, qf_v, mo_v, w_v, vmo_v, vp_v, tot_v,
    eo_hbm, pf_hbm, qf_hbm, mo_hbm, wo_hbm, vmo_hbm, vpo_hbm,
    wo_v, vpo_v, sems,
):
    copies = []

    def write(src, dst):
        copy = pltpu.make_async_copy(src, dst, sems.at[len(copies)])
        copy.start()
        copies.append(copy)

    write(eo_v, eo_hbm)
    write(mo_v, mo_hbm)
    write(qf_v, qf_hbm)
    write(pf_v, pf_hbm)
    write(vmo_v, vmo_hbm)
    total = jnp.sum(tot_v[...], axis=1, keepdims=True)
    scale = 0.05 / jnp.sqrt(total / entries + 1e-06)
    rows = w_v.shape[0]
    step = rows // WRITES
    for i in range(WRITES):
        at = pl.ds(i * step, step)
        wo_v[at, :] = w_v[at, :] - scale * mo_v[at, :]
        write(wo_v.at[at], wo_hbm.at[at])
    vpo_v[...] = vp_v[...] - scale.reshape(1, 1, 1) * vmo_v[...]
    write(vpo_v, vpo_hbm)
    for copy in copies:
        copy.wait()


def shards(
    sizes,
    grads, errors, q_prev, p_root, q_root, momentum, weights, vec_grads, vec_momentum, vec_params,
):
    n_dp, n_t, n_s = sizes
    rows, width = errors.shape[2:]
    rank = q_prev.shape[2]
    vecs, entries = vec_params.shape[1:]
    n = n_dp * n_t
    own = Owners(n_dp, n_t, width)
    span = own.per_plane * LANES
    n_blocks = len(row_blocks(rows))
    big = (rows, width)
    vec = (vecs, 1, entries)
    packed = (packed_rows(rank, rows), LANES)
    chunk = (rank, LANES)
    any_space = pl.BlockSpec(memory_space=pl.ANY)
    in_vmem = pl.BlockSpec(memory_space=pltpu.VMEM)
    dma = pltpu.SemaphoreType.DMA
    vmem = pltpu.VMEM
    args = (
        grads[0, 0],
        errors[0, 0],
        q_prev[0].T,
        p_root[0],
        q_root[0],
        momentum[0],
        weights[0],
        vec_grads[0, 0][:, None, :],
        vec_momentum[0][:, None, :],
        vec_params[0][:, None, :],
    )
    shapes = (big, (rank, rows), (rank, width), big, big, vec, vec)
    outs = pl.pallas_call(
        functools.partial(kernel, sizes),
        out_shape=tuple(vmem(shape, F32) for shape in shapes + ((1, LANES),)),
        in_specs=[any_space] * 10,
        out_specs=(in_vmem,) * 8,
        scratch_shapes=[
            vmem(big, BF16),
            vmem(big, F32),
            vmem((rank, width), F32),
            vmem((rank, rank), F32),
            vmem((rank, rank), F32),
            vmem(big, F32),
            vmem(vec, F32),
            vmem((own.planes, rows, span), BF16),
            vmem((own.planes, rows, span), BF16),
            vmem((n_dp,) + packed, F32),
            vmem((n_dp,) + vec, F32),
            vmem((n_t,) + packed, F32),
            vmem((n_t, 1, LANES), F32),
            vmem((n_t, rows, LANES), F32),
            vmem((own.count,) + chunk, F32),
            vmem((n,) + chunk, F32),
            vmem((own.count,) + chunk, F32),
            vmem((n_t, rows, 3 * rank), BF16),
            vmem((n * n_s, 1, LANES), F32),
            dma((9 + 2 * n_blocks,)),
            dma(()), dma(()), dma(()), dma(()),
            dma((own.count,)), dma(()), dma((own.count,)), dma(()), dma((own.count,)), dma(()),
            dma(()), dma(()), dma(()), dma(()), dma(()), dma(()),
        ],
        compiler_params=pltpu.CompilerParams(
            collective_id=0, has_side_effects=True, vmem_limit_bytes=48 * 1024 * 1024
        ),
    )(*(pltpu.with_memory_space_constraint(arg, pltpu.HBM) for arg in args))
    outs = pl.pallas_call(
        functools.partial(finish, n_s * (width * width + vecs * width)),
        out_shape=tuple(pltpu.HBM(shape, F32) for shape in shapes),
        in_specs=[in_vmem] * 8,
        out_specs=(any_space,) * 7,
        scratch_shapes=[vmem(big, F32), vmem(vec, F32), dma((6 + WRITES,))],
    )(*(pltpu.with_memory_space_constraint(out, pltpu.VMEM) for out in outs))
    errors_out, p_factor, q_factor, momentum_out, weights_out, vec_momentum_out, vec_params_out = outs
    return (
        errors_out[None, None],
        p_factor.T[None],
        q_factor.T[None],
        momentum_out[None],
        weights_out[None],
        vec_momentum_out[:, 0][None],
        vec_params_out[:, 0][None],
    )


def solution(mesh):
    sizes = (mesh.shape["dp"], mesh.shape["tensor"], mesh.shape["section"])
    in_specs = (
        P("dp", "section", "tensor", None),
        P("dp", "section", "tensor", None),
        P("section", None, None),
        P("section", None, None),
        P("section", None, None),
        P("section", "tensor", None),
        P("section", "tensor", None),
        P("dp", "section", None, "tensor"),
        P("section", None, "tensor"),
        P("section", None, "tensor"),
    )
    out_specs = (
        P("dp", "section", "tensor", None),
        P("section", "tensor", None),
        P("section", None, None),
        P("section", "tensor", None),
        P("section", "tensor", None),
        P("section", None, "tensor"),
        P("section", None, "tensor"),
    )
    return jax.shard_map(
        functools.partial(shards, sizes),
        mesh=mesh, in_specs=in_specs, out_specs=out_specs, check_vma=False,
    )
```

```python
import functools

import jax
import jax.numpy as jnp
from jax import lax
from jax.experimental import pallas as pl
from jax.experimental.pallas import tpu as pltpu
from jax.sharding import PartitionSpec as P

F32 = jnp.float32
BF16 = jnp.bfloat16
MESH = pl.DeviceIdType.MESH
LANES = 128
UNROLL = 16
WRITES = 4


def split(x):
    high = x.astype(BF16)
    return high, (x - high.astype(F32)).astype(BF16)


def mm(a, b, dims=((1,), (0,))):
    return lax.dot_general(a, b, (dims, ((), ())), preferred_element_type=F32)


def left_parts(x):
    high, low = split(x)
    return jnp.concatenate([high, high, low], axis=1)


def right_parts(x):
    high, low = split(x)
    return jnp.concatenate([high, low, high], axis=0)


def each(count, body):
    if count <= UNROLL:
        for i in range(count):
            body(i)
    else:
        lax.fori_loop(0, count, lambda i, c: (body(i), c)[1], 0)


def total_of(ref, count):
    if count <= UNROLL:
        total = ref[0]
        for i in range(1, count):
            total = total + ref[i]
        return total
    return lax.fori_loop(1, count, lambda i, acc: acc + ref[i], ref[0])


def row_blocks(rows):
    return [(r, min(LANES, rows - r)) for r in range(0, rows, LANES)]


def packed_rows(rank, rows):
    return rank * rows // LANES


def pack(part):
    rank, size = part.shape
    count = LANES // size
    step = rank // count
    return jnp.concatenate([part[i * step : (i + 1) * step] for i in range(count)], axis=1)


def unpack(x, rank, rows):
    parts = []
    for start, size in row_blocks(rows):
        count = LANES // size
        step = rank // count
        block = x[rank * start // LANES :][:step]
        parts.append(
            jnp.concatenate([block[:, i * size : (i + 1) * size] for i in range(count)], axis=0)
        )
    return jnp.concatenate(parts, axis=1)


class Owners:
    def __init__(self, n_dp, n_t, width):
        self.count = width // LANES
        self.planes = -(-self.count // n_t)
        self.per_plane = self.count // self.planes
        self.first = (n_dp - self.planes) // 2


def kernel(
    sizes,
    g_hbm, e_hbm, qt_hbm, pr_hbm, qr_hbm, m_hbm, w_hbm, vg_hbm, vm_hbm, vp_hbm,
    eo_v, pf_v, qf_v, mo_v, w_v, vmo_v, vp_v, tot_v,
    g_v, e_v, qt_v, pr_v, qr_v, m_v, vm_v,
    hi_v, lo_v, mhi_v, mlo_v, msq_v, pbuf, vbuf, gbuf, wsend, wbuf, gl_v, qpart, rbuf, qfull, tiles,
    in_sem, psend, precv, vsend, vrecv, gsend_sem, grecv, wsend_sem, wrecv,
    rsend, rrecv, asend, arecv, tsend, trecv,
):
    n_dp, n_t, n_s = sizes
    n = n_dp * n_t
    group = n_t * n_s
    dp, tn, sc = lax.axis_index("dp"), lax.axis_index("tensor"), lax.axis_index("section")
    me = dp * n_t + tn
    rank, width = qt_v.shape
    rows = e_v.shape[0]
    own = Owners(n_dp, n_t, width)
    chunks, per_plane, planes = own.count, own.per_plane, own.planes
    span = per_plane * LANES
    gram_rows = packed_rows(rank, rank)
    plane = dp - own.first
    mine = plane * per_plane + tn
    in_plane = jnp.logical_and(plane >= 0, plane < planes)
    owns = jnp.logical_and(in_plane, tn < per_plane)
    upper = 2 * dp < n_dp

    def load(i, src, dst):
        copy = pltpu.make_async_copy(src, dst, in_sem.at[i])
        copy.start()
        return copy

    blocks = row_blocks(rows)
    in_q = load(0, qt_hbm, qt_v)
    in_pr = load(1, pr_hbm, pr_v)
    in_g, in_e = [], []
    for b, (start, size) in enumerate(blocks):
        at = pl.ds(start, size)
        in_g.append(load(9 + 2 * b, g_hbm.at[at], g_v.at[at]))
        in_e.append(load(10 + 2 * b, e_hbm.at[at], e_v.at[at]))
    in_vg = load(2, vg_hbm, vbuf.at[dp])
    in_qr = load(3, qr_hbm, qr_v)
    in_vm = load(4, vm_hbm, vm_v)
    in_m = load(5, m_hbm, m_v)
    in_vp = load(6, vp_hbm, vp_v)
    in_w = load(7, w_hbm, w_v)

    barrier = pltpu.get_barrier_semaphore()
    slot = sc * n_t + tn

    def line_peer(i):
        up, down = n_dp - 1 - i, i
        return jnp.where(
            upper, jnp.where(up > dp, up, up - 1), jnp.where(down < dp, down, down + 1)
        )

    def greet_line(i):
        pl.semaphore_signal(
            barrier, inc=1, device_id=(line_peer(i), tn, sc), device_id_type=MESH
        )

    def greet_plane(i):
        peer = lax.rem(slot + 1 + i, group)
        pl.semaphore_signal(
            barrier, inc=1, device_id=(dp, lax.rem(peer, n_t), peer // n_t), device_id_type=MESH
        )

    each(n_dp - 1, greet_line)
    each(group - 1, greet_plane)

    in_q.wait()
    in_pr.wait()
    q_hi, q_lo = split(mm(left_parts(pr_v[...].T), right_parts(qt_v[...])))
    q_both = jnp.concatenate([q_hi, q_lo], axis=0)
    for b, (start, size) in enumerate(blocks):
        at = pl.ds(start, size)
        in_g[b].wait()
        in_e[b].wait()
        merged = g_v[at, :].astype(F32) + e_v[at, :]
        e_v[at, :] = merged
        m_hi, m_lo = split(merged)
        for p in range(planes):
            hi_v[p, at, :] = m_hi[:, p * span : (p + 1) * span]
            lo_v[p, at, :] = m_lo[:, p * span : (p + 1) * span]
        first = mm(q_both, m_hi, ((1,), (1,)))
        second = mm(q_hi, m_lo, ((1,), (1,)))
        pbuf[dp, pl.ds(rank * start // LANES, rank * size // LANES), :] = pack(
            first[:rank] + first[rank:] + second
        )

    pl.semaphore_wait(barrier, n_dp - 1 + group - 1)

    def send_p(i):
        pltpu.make_async_remote_copy(
            pbuf.at[dp], pbuf.at[dp], psend, precv,
            device_id=(line_peer(i), tn, sc), device_id_type=MESH,
        ).start()

    def send_v(i):
        pltpu.make_async_remote_copy(
            vbuf.at[dp], vbuf.at[dp], vsend, vrecv,
            device_id=(line_peer(i), tn, sc), device_id_type=MESH,
        ).start()

    each(n_dp - 1, send_p)
    in_vg.wait()
    each(n_dp - 1, send_v)

    in_m.wait()
    in_qr.wait()
    in_vm.wait()
    q_root_left = left_parts(qr_v[...])
    q_root_t = left_parts(qr_v[...].T)

    @pl.when(in_plane)
    def _():
        m_hi, m_lo = split(m_v[...])
        for p in range(planes):
            mhi_v[p] = m_hi[:, p * span : (p + 1) * span]
            mlo_v[p] = m_lo[:, p * span : (p + 1) * span]
        squares = jnp.zeros((8, LANES), F32)
        for c in range(chunks):
            old = 0.9 * m_v[:, c * LANES : (c + 1) * LANES]
            squares = squares + jnp.sum((old * old).reshape(rows // 8, 8, LANES), axis=0)
        msq_v[...] = squares

    others = pl.ds(0, n_dp - 1)
    pltpu.make_async_copy(pbuf.at[others], pbuf.at[others], precv).wait()
    pf = unpack(total_of(pbuf, n_dp), rank, rows)
    pf_hi, pf_lo = split(pf)
    pf_both = jnp.concatenate([pf_hi, pf_lo], axis=0)

    for i in range(planes):
        p = jnp.where(upper, planes - 1 - i, i)
        first = mm(pf_both, hi_v[p])
        second = mm(pf_hi, lo_v[p])
        part = first[:rank] + first[rank:] + second
        for j in range(per_plane):
            k = p * per_plane + j
            block = part[:, j * LANES : (j + 1) * LANES]
            here = jnp.logical_and(owns, mine == k)

            @pl.when(here)
            def _():
                rbuf[me] = block

            @pl.when(jnp.logical_not(here))
            def _():
                qpart[k] = block
                pltpu.make_async_remote_copy(
                    qpart.at[k], rbuf.at[me], rsend, rrecv,
                    device_id=(own.first + p, j, sc), device_id_type=MESH,
                ).start()

    pf_v[...] = pf
    left_t = mm(q_root_left, right_parts(pf)) / n_dp
    left = left_parts(left_t.T)
    pltpu.make_async_copy(vbuf.at[others], vbuf.at[others], vrecv).wait()
    v_new = 0.9 * vm_v[...] + total_of(vbuf, n_dp) / n_dp
    vmo_v[...] = v_new
    v_square = jnp.sum(v_new * v_new)

    def give_product(j):
        return pltpu.make_async_remote_copy(
            wsend.at[j], wbuf.at[tn], wsend_sem.at[j], wrecv,
            device_id=(dp, j, sc), device_id_type=MESH,
        )

    def give_gram(j):
        return pltpu.make_async_remote_copy(
            gbuf.at[tn], gbuf.at[tn], gsend_sem.at[j], grecv,
            device_id=(dp, j, sc), device_id_type=MESH,
        )

    @pl.when(in_plane)
    def _():
        largest = jnp.max(jnp.max(jnp.abs(left_t), axis=1, keepdims=True), axis=0, keepdims=True)
        unit = left_t / jnp.where(largest > 0, largest, 1.0)
        u_hi, u_lo = split(unit)
        first = mm(jnp.concatenate([u_hi, u_lo], axis=0), mhi_v[plane])
        second = mm(u_hi, mlo_v[plane])
        product = first[:rank] + first[rank:] + second
        for j in range(per_plane):
            block = product[:, j * LANES : (j + 1) * LANES]

            @pl.when(tn == j)
            def _():
                wbuf[tn] = block

            @pl.when(tn != j)
            def _():
                wsend[j] = block
                give_product(j).start()

        gram = mm(left_parts(unit), jnp.concatenate([u_hi, u_lo, u_hi], axis=1), ((1,), (1,)))
        gbuf[tn, 0:gram_rows, :] = pack(gram)
        row = lax.broadcasted_iota(jnp.int32, (8, LANES), 0)
        lane = lax.broadcasted_iota(jnp.int32, (8, LANES), 1)
        squares = jnp.sum(msq_v[...], axis=0, keepdims=True)
        squares = squares + jnp.where(lane == 0, v_square, 0.0)
        gbuf[tn, gram_rows : gram_rows + 8, :] = jnp.where(
            row == 0, largest, jnp.where(row == 1, squares, 0.0)
        )
        for j in range(per_plane):

            @pl.when(tn != j)
            def _():
                give_gram(j).start()

    half = 2 if n_t % 2 == 0 else 1

    def far_tensor(j):
        outer = lax.rem(n_t // half - 1 - tn // half + j // half + n_t, n_t // half)
        inner = lax.rem(half - 1 - lax.rem(tn, half) + j % half + half, half)
        return outer * half + inner

    def far_dp(i):
        return jnp.where(upper, n_dp - 1 - i, i)

    @pl.when(owns)
    def _():
        rest = pl.ds(0, n_t - 1)
        pltpu.make_async_copy(wbuf.at[rest], wbuf.at[rest], wrecv).wait()
        pltpu.make_async_copy(gbuf.at[rest], gbuf.at[rest], grecv).wait()
        squares = jnp.zeros((1, LANES), F32)
        for t in range(n_t):
            gl_v[t] = left_parts(unpack(gbuf[t, 0:gram_rows, :], rank, rank))
            squares = squares + gbuf[t, gram_rows + 1 : gram_rows + 2, :]

        whole = pl.ds(0, n - 1)
        pltpu.make_async_copy(rbuf.at[whole], rbuf.at[whole], rrecv).wait()
        q_sum = total_of(rbuf, n)
        qfull[mine] = q_sum

        def send_sum(i):
            to_dp = far_dp(i // n_t)
            to_tensor = far_tensor(i % n_t)

            @pl.when(to_dp * n_t + to_tensor != me)
            def _():
                pltpu.make_async_remote_copy(
                    qfull.at[mine], qfull.at[mine], asend, arecv.at[mine],
                    device_id=(to_dp, to_tensor, sc), device_id_type=MESH,
                ).start()

        each(n, send_sum)

        terms = jnp.zeros((rank, LANES), F32)
        for t in range(n_t):
            scaled = q_sum * gbuf[t, gram_rows : gram_rows + 1, :]
            terms = terms + scaled * (1.8 * wbuf[t] + mm(gl_v[t], right_parts(scaled)))
        at = sc * chunks + mine
        tiles[at] = jnp.sum(terms, axis=0, keepdims=True) + jnp.where(mine == 0, squares, 0.0)

        def send_row(i):
            to_dp = far_dp(i // group)
            to_tensor = far_tensor((i // n_s) % n_t)
            to_section = lax.rem(sc + 1 + i % n_s, n_s)

            @pl.when(jnp.logical_or(to_dp * n_t + to_tensor != me, to_section != sc))
            def _():
                pltpu.make_async_remote_copy(
                    tiles.at[at], tiles.at[at], tsend, trecv,
                    device_id=(to_dp, to_tensor, to_section), device_id_type=MESH,
                ).start()

        if n * n_s <= 2 * UNROLL:
            for i in range(n * n_s):
                send_row(i)
        else:
            each(n * n_s, send_row)

    for i in range(planes):
        p = jnp.where(upper, i, planes - 1 - i)
        for j in range(per_plane):
            k = p * per_plane + j

            @pl.when(jnp.logical_not(jnp.logical_and(owns, mine == k)))
            def _():
                pltpu.make_async_copy(qfull.at[k], qfull.at[k], arecv.at[k]).wait()

            cols = pl.ds(pl.multiple_of(k * LANES, LANES), LANES)
            right = right_parts(qfull[k])
            approx = mm(left, right)
            mo_v[:, cols] = 0.9 * m_v[:, cols] + approx
            eo_v[:, cols] = e_v[:, cols] - approx
            qf_v[:, cols] = mm(q_root_t, right)
    in_w.wait()
    in_vp.wait()

    count = n_s * chunks

    @pl.when(owns)
    def _():
        got = pl.ds(0, count - 1)
        pltpu.make_async_copy(tiles.at[got], tiles.at[got], trecv).wait()

    @pl.when(jnp.logical_not(owns))
    def _():
        got = pl.ds(0, count)
        pltpu.make_async_copy(tiles.at[got], tiles.at[got], trecv).wait()

    tot_v[...] = total_of(tiles, count)

    pltpu.make_async_copy(pbuf.at[others], pbuf.at[others], psend).wait()
    pltpu.make_async_copy(vbuf.at[others], vbuf.at[others], vsend).wait()

    @pl.when(in_plane)
    def _():
        for j in range(per_plane):

            @pl.when(tn != j)
            def _():
                give_product(j).wait_send()
                give_gram(j).wait_send()

    @pl.when(owns)
    def _():
        got = pl.ds(0, chunks - 1)
        pltpu.make_async_copy(qfull.at[got], qfull.at[got], rsend).wait()
        whole = pl.ds(0, n - 1)
        pltpu.make_async_copy(rbuf.at[whole], rbuf.at[whole], asend).wait()
        sent = tiles.at[pl.ds(0, n * n_s - 1)]
        pltpu.make_async_copy(sent, sent, tsend).wait()

    @pl.when(jnp.logical_not(owns))
    def _():
        pltpu.make_async_copy(qfull, qfull, rsend).wait()


def finish(
    entries,
    eo_v, pf_v, qf_v, mo_v, w_v, vmo_v, vp_v, tot_v,
    eo_hbm, pf_hbm, qf_hbm, mo_hbm, wo_hbm, vmo_hbm, vpo_hbm,
    wo_v, vpo_v, sems,
):
    copies = []

    def write(src, dst):
        copy = pltpu.make_async_copy(src, dst, sems.at[len(copies)])
        copy.start()
        copies.append(copy)

    write(eo_v, eo_hbm)
    write(mo_v, mo_hbm)
    write(qf_v, qf_hbm)
    write(pf_v, pf_hbm)
    write(vmo_v, vmo_hbm)
    total = jnp.maximum(jnp.sum(tot_v[...], axis=1, keepdims=True), 0.0)
    scale = 0.05 / jnp.sqrt(total / entries + 1e-06)
    rows = w_v.shape[0]
    step = rows // WRITES
    for i in range(WRITES):
        at = pl.ds(i * step, step)
        wo_v[at, :] = w_v[at, :] - scale * mo_v[at, :]
        write(wo_v.at[at], wo_hbm.at[at])
    vpo_v[...] = vp_v[...] - scale.reshape(1, 1, 1) * vmo_v[...]
    write(vpo_v, vpo_hbm)
    for copy in copies:
        copy.wait()


def shards(
    sizes,
    grads, errors, q_prev, p_root, q_root, momentum, weights, vec_grads, vec_momentum, vec_params,
):
    n_dp, n_t, n_s = sizes
    rows, width = errors.shape[2:]
    rank = q_prev.shape[2]
    vecs, entries = vec_params.shape[1:]
    n = n_dp * n_t
    own = Owners(n_dp, n_t, width)
    span = own.per_plane * LANES
    n_blocks = len(row_blocks(rows))
    big = (rows, width)
    vec = (vecs, 1, entries)
    packed = (packed_rows(rank, rows), LANES)
    chunk = (rank, LANES)
    any_space = pl.BlockSpec(memory_space=pl.ANY)
    in_vmem = pl.BlockSpec(memory_space=pltpu.VMEM)
    dma = pltpu.SemaphoreType.DMA
    vmem = pltpu.VMEM
    args = (
        grads[0, 0],
        errors[0, 0],
        q_prev[0].T,
        p_root[0],
        q_root[0],
        momentum[0],
        weights[0],
        vec_grads[0, 0][:, None, :],
        vec_momentum[0][:, None, :],
        vec_params[0][:, None, :],
    )
    shapes = (big, (rank, rows), (rank, width), big, big, vec, vec)
    outs = pl.pallas_call(
        functools.partial(kernel, sizes),
        out_shape=tuple(vmem(shape, F32) for shape in shapes + ((1, LANES),)),
        in_specs=[any_space] * 10,
        out_specs=(in_vmem,) * 8,
        scratch_shapes=[
            vmem(big, BF16),
            vmem(big, F32),
            vmem((rank, width), F32),
            vmem((rank, rank), F32),
            vmem((rank, rank), F32),
            vmem(big, F32),
            vmem(vec, F32),
            vmem((own.planes, rows, span), BF16),
            vmem((own.planes, rows, span), BF16),
            vmem((own.planes, rows, span), BF16),
            vmem((own.planes, rows, span), BF16),
            vmem((8, LANES), F32),
            vmem((n_dp,) + packed, F32),
            vmem((n_dp,) + vec, F32),
            vmem((n_t, packed_rows(rank, rank) + 8, LANES), F32),
            vmem((own.per_plane,) + chunk, F32),
            vmem((n_t,) + chunk, F32),
            vmem((n_t, rank, 3 * rank), BF16),
            vmem((own.count,) + chunk, F32),
            vmem((n,) + chunk, F32),
            vmem((own.count,) + chunk, F32),
            vmem((n * n_s, 1, LANES), F32),
            dma((9 + 2 * n_blocks,)),
            dma(()), dma(()), dma(()), dma(()),
            dma((own.per_plane,)), dma(()), dma((own.per_plane,)), dma(()),
            dma(()), dma(()), dma(()), dma((own.count,)), dma(()), dma(()),
        ],
        compiler_params=pltpu.CompilerParams(
            collective_id=0, has_side_effects=True, vmem_limit_bytes=48 * 1024 * 1024
        ),
    )(*(pltpu.with_memory_space_constraint(arg, pltpu.HBM) for arg in args))
    outs = pl.pallas_call(
        functools.partial(finish, n_s * (width * width + vecs * width)),
        out_shape=tuple(pltpu.HBM(shape, F32) for shape in shapes),
        in_specs=[in_vmem] * 8,
        out_specs=(any_space,) * 7,
        scratch_shapes=[vmem(big, F32), vmem(vec, F32), dma((6 + WRITES,))],
    )(*(pltpu.with_memory_space_constraint(out, pltpu.VMEM) for out in outs))
    errors_out, p_factor, q_factor, momentum_out, weights_out, vec_momentum_out, vec_params_out = outs
    return (
        errors_out[None, None],
        p_factor.T[None],
        q_factor.T[None],
        momentum_out[None],
        weights_out[None],
        vec_momentum_out[:, 0][None],
        vec_params_out[:, 0][None],
    )


def solution(mesh):
    sizes = (mesh.shape["dp"], mesh.shape["tensor"], mesh.shape["section"])
    in_specs = (
        P("dp", "section", "tensor", None),
        P("dp", "section", "tensor", None),
        P("section", None, None),
        P("section", None, None),
        P("section", None, None),
        P("section", "tensor", None),
        P("section", "tensor", None),
        P("dp", "section", None, "tensor"),
        P("section", None, "tensor"),
        P("section", None, "tensor"),
    )
    out_specs = (
        P("dp", "section", "tensor", None),
        P("section", "tensor", None),
        P("section", None, None),
        P("section", "tensor", None),
        P("section", "tensor", None),
        P("section", None, "tensor"),
        P("section", None, "tensor"),
    )
    return jax.shard_map(
        functools.partial(shards, sizes),
        mesh=mesh, in_specs=in_specs, out_specs=out_specs, check_vma=False,
    )
```

```python
import functools

import jax
import jax.numpy as jnp
from jax import lax
from jax.experimental import pallas as pl
from jax.experimental.pallas import tpu as pltpu
from jax.sharding import PartitionSpec as P

F32 = jnp.float32
BF16 = jnp.bfloat16
MESH = pl.DeviceIdType.MESH
LANES = 128
UNROLL = 32
WRITES = 4


def split(x):
    high = x.astype(BF16)
    return high, (x - high.astype(F32)).astype(BF16)


def mm(a, b, dims=((1,), (0,))):
    return lax.dot_general(a, b, (dims, ((), ())), preferred_element_type=F32)


def left_parts(x):
    high, low = split(x)
    return jnp.concatenate([high, high, low], axis=1)


def right_parts(x):
    high, low = split(x)
    return jnp.concatenate([high, low, high], axis=0)


def each(count, body):
    if count <= UNROLL:
        for i in range(count):
            body(i)
    else:
        lax.fori_loop(0, count, lambda i, c: (body(i), c)[1], 0)


def total_of(ref, count):
    if count <= UNROLL:
        total = ref[0]
        for i in range(1, count):
            total = total + ref[i]
        return total
    return lax.fori_loop(1, count, lambda i, acc: acc + ref[i], ref[0])


def row_blocks(rows):
    return [(r, min(LANES, rows - r)) for r in range(0, rows, LANES)]


def packed_rows(rank, rows):
    return rank * rows // LANES


def pack(part):
    rank, size = part.shape
    count = LANES // size
    step = rank // count
    return jnp.concatenate([part[i * step : (i + 1) * step] for i in range(count)], axis=1)


def unpack(x, rank, rows):
    parts = []
    for start, size in row_blocks(rows):
        count = LANES // size
        step = rank // count
        block = x[rank * start // LANES :][:step]
        parts.append(
            jnp.concatenate([block[:, i * size : (i + 1) * size] for i in range(count)], axis=0)
        )
    return jnp.concatenate(parts, axis=1)


class Owners:
    def __init__(self, n_dp, n_t, width):
        self.count = width // LANES
        self.planes = -(-self.count // n_t)
        self.per_plane = self.count // self.planes
        self.first = (n_dp - self.planes) // 2


def kernel(
    sizes,
    g_hbm, e_hbm, qt_hbm, pr_hbm, qr_hbm, m_hbm, w_hbm, vg_hbm, vm_hbm, vp_hbm,
    eo_v, pf_v, qf_v, mo_v, w_v, vmo_v, vp_v, tot_v,
    g_v, e_v, qt_v, pr_v, qr_v, m_v, vm_v,
    hi_v, lo_v, mhi_v, mlo_v, msq_v, pbuf, vbuf, gbuf, wsend, wbuf, qpart, rbuf, qfull, tiles,
    in_sem, psend, precv, vsend, vrecv, gsend_sem, grecv, wsend_sem, wrecv,
    rsend, rrecv, asend, arecv, tsend, trecv,
):
    n_dp, n_t, n_s = sizes
    n = n_dp * n_t
    group = n_t * n_s
    dp, tn, sc = lax.axis_index("dp"), lax.axis_index("tensor"), lax.axis_index("section")
    me = dp * n_t + tn
    rank, width = qt_v.shape
    rows = e_v.shape[0]
    own = Owners(n_dp, n_t, width)
    chunks, per_plane, planes = own.count, own.per_plane, own.planes
    span = per_plane * LANES
    gram_rows = packed_rows(rank, rank)
    plane = dp - own.first
    mine = plane * per_plane + tn
    in_plane = jnp.logical_and(plane >= 0, plane < planes)
    owns = jnp.logical_and(in_plane, tn < per_plane)
    upper = 2 * dp < n_dp

    def load(i, src, dst):
        copy = pltpu.make_async_copy(src, dst, in_sem.at[i])
        copy.start()
        return copy

    blocks = row_blocks(rows)
    in_q = load(0, qt_hbm, qt_v)
    in_pr = load(1, pr_hbm, pr_v)
    in_g, in_e = [], []
    for b, (start, size) in enumerate(blocks):
        at = pl.ds(start, size)
        in_g.append(load(9 + 2 * b, g_hbm.at[at], g_v.at[at]))
        in_e.append(load(10 + 2 * b, e_hbm.at[at], e_v.at[at]))
    in_vg = load(2, vg_hbm, vbuf.at[dp])
    in_qr = load(3, qr_hbm, qr_v)
    in_vm = load(4, vm_hbm, vm_v)
    in_m = load(5, m_hbm, m_v)
    in_vp = load(6, vp_hbm, vp_v)
    in_w = load(7, w_hbm, w_v)

    barrier = pltpu.get_barrier_semaphore()
    slot = sc * n_t + tn

    def line_peer(i):
        up, down = n_dp - 1 - i, i
        return jnp.where(
            upper, jnp.where(up > dp, up, up - 1), jnp.where(down < dp, down, down + 1)
        )

    def greet_line(i):
        pl.semaphore_signal(
            barrier, inc=1, device_id=(line_peer(i), tn, sc), device_id_type=MESH
        )

    def greet_plane(i):
        peer = lax.rem(slot + 1 + i, group)
        pl.semaphore_signal(
            barrier, inc=1, device_id=(dp, lax.rem(peer, n_t), peer // n_t), device_id_type=MESH
        )

    each(n_dp - 1, greet_line)
    each(group - 1, greet_plane)

    in_q.wait()
    in_pr.wait()
    q_hi, q_lo = split(mm(left_parts(pr_v[...].T), right_parts(qt_v[...])))
    q_both = jnp.concatenate([q_hi, q_lo], axis=0)
    for b, (start, size) in enumerate(blocks):
        at = pl.ds(start, size)
        in_g[b].wait()
        in_e[b].wait()
        merged = g_v[at, :].astype(F32) + e_v[at, :]
        e_v[at, :] = merged
        m_hi, m_lo = split(merged)
        for p in range(planes):
            hi_v[p, at, :] = m_hi[:, p * span : (p + 1) * span]
            lo_v[p, at, :] = m_lo[:, p * span : (p + 1) * span]
        first = mm(q_both, m_hi, ((1,), (1,)))
        second = mm(q_hi, m_lo, ((1,), (1,)))
        pbuf[dp, pl.ds(rank * start // LANES, rank * size // LANES), :] = pack(
            first[:rank] + first[rank:] + second
        )

    pl.semaphore_wait(barrier, n_dp - 1 + group - 1)

    def send_p(i):
        pltpu.make_async_remote_copy(
            pbuf.at[dp], pbuf.at[dp], psend, precv,
            device_id=(line_peer(i), tn, sc), device_id_type=MESH,
        ).start()

    def send_v(i):
        pltpu.make_async_remote_copy(
            vbuf.at[dp], vbuf.at[dp], vsend, vrecv,
            device_id=(line_peer(i), tn, sc), device_id_type=MESH,
        ).start()

    each(n_dp - 1, send_p)
    in_vg.wait()
    each(n_dp - 1, send_v)

    in_m.wait()
    in_qr.wait()
    in_vm.wait()
    q_root_left = left_parts(qr_v[...])
    q_root_t = left_parts(qr_v[...].T)

    @pl.when(in_plane)
    def _():
        m_hi, m_lo = split(m_v[...])
        for p in range(planes):
            mhi_v[p] = m_hi[:, p * span : (p + 1) * span]
            mlo_v[p] = m_lo[:, p * span : (p + 1) * span]
        squares = jnp.zeros((8, LANES), F32)
        for c in range(chunks):
            old = 0.9 * m_v[:, c * LANES : (c + 1) * LANES]
            squares = squares + jnp.sum((old * old).reshape(rows // 8, 8, LANES), axis=0)
        msq_v[...] = squares

    others = pl.ds(0, n_dp - 1)
    pltpu.make_async_copy(pbuf.at[others], pbuf.at[others], precv).wait()
    pf = unpack(total_of(pbuf, n_dp), rank, rows)
    pf_hi, pf_lo = split(pf)
    pf_both = jnp.concatenate([pf_hi, pf_lo], axis=0)

    for i in range(planes):
        p = jnp.where(upper, planes - 1 - i, i)
        first = mm(pf_both, hi_v[p])
        second = mm(pf_hi, lo_v[p])
        part = first[:rank] + first[rank:] + second
        for j in range(per_plane):
            k = p * per_plane + j
            block = part[:, j * LANES : (j + 1) * LANES]
            here = jnp.logical_and(owns, mine == k)

            @pl.when(here)
            def _():
                rbuf[me] = block

            @pl.when(jnp.logical_not(here))
            def _():
                qpart[k] = block
                pltpu.make_async_remote_copy(
                    qpart.at[k], rbuf.at[me], rsend, rrecv,
                    device_id=(own.first + p, j, sc), device_id_type=MESH,
                ).start()

    def give_product(j):
        return pltpu.make_async_remote_copy(
            wsend.at[j], wbuf.at[tn], wsend_sem.at[j], wrecv,
            device_id=(dp, j, sc), device_id_type=MESH,
        )

    def give_gram(j):
        return pltpu.make_async_remote_copy(
            gbuf.at[tn], gbuf.at[tn], gsend_sem.at[j], grecv,
            device_id=(dp, j, sc), device_id_type=MESH,
        )

    @pl.when(in_plane)
    def _():
        largest = jnp.max(jnp.max(jnp.abs(pf), axis=1, keepdims=True), axis=0, keepdims=True)
        unit = pf / jnp.where(largest > 0, largest, 1.0)
        u_hi, u_lo = split(unit)
        first = mm(jnp.concatenate([u_hi, u_lo], axis=0), mhi_v[plane])
        second = mm(u_hi, mlo_v[plane])
        product = first[:rank] + first[rank:] + second
        for j in range(per_plane):
            block = product[:, j * LANES : (j + 1) * LANES]

            @pl.when(tn == j)
            def _():
                wbuf[tn] = block

            @pl.when(tn != j)
            def _():
                wsend[j] = block
                give_product(j).start()

        gram = mm(left_parts(unit), jnp.concatenate([u_hi, u_lo, u_hi], axis=1), ((1,), (1,)))
        gbuf[tn, 0:gram_rows, :] = pack(gram)
        pltpu.make_async_copy(vbuf.at[others], vbuf.at[others], vrecv).wait()
        v_new = 0.9 * vm_v[...] + total_of(vbuf, n_dp) / n_dp
        v_row = jnp.sum(v_new * v_new, axis=0)
        squares = jnp.sum(msq_v[...], axis=0, keepdims=True)
        for start, size in row_blocks(v_row.shape[1]):
            piece = v_row[:, start : start + size]
            if size < LANES:
                piece = jnp.concatenate([piece, jnp.zeros((1, LANES - size), F32)], axis=1)
            squares = squares + piece
        row = lax.broadcasted_iota(jnp.int32, (8, LANES), 0)
        gbuf[tn, gram_rows : gram_rows + 8, :] = jnp.where(
            row == 0, largest, jnp.where(row == 1, squares, 0.0)
        )
        for j in range(per_plane):

            @pl.when(tn != j)
            def _():
                give_gram(j).start()

    @pl.when(jnp.logical_not(in_plane))
    def _():
        pltpu.make_async_copy(vbuf.at[others], vbuf.at[others], vrecv).wait()

    pf_v[...] = pf
    left_t = mm(q_root_left, right_parts(pf)) / n_dp
    left = left_parts(left_t.T)
    vmo_v[...] = 0.9 * vm_v[...] + total_of(vbuf, n_dp) / n_dp

    half = 2 if n_t % 2 == 0 else 1

    def far_tensor(j):
        outer = lax.rem(tn // half + 1 + j // half, n_t // half)
        inner = lax.rem(lax.rem(tn, half) + 1 + j % half, half)
        return outer * half + inner

    @pl.when(owns)
    def _():
        whole = pl.ds(0, n - 1)
        pltpu.make_async_copy(rbuf.at[whole], rbuf.at[whole], rrecv).wait()
        q_sum = total_of(rbuf, n)
        qfull[mine] = q_sum

        def send_sum(to_dp, to_tensor):
            pltpu.make_async_remote_copy(
                qfull.at[mine], qfull.at[mine], asend, arecv.at[mine],
                device_id=(to_dp, to_tensor, sc), device_id_type=MESH,
            ).start()

        each((n_dp - 1) * n_t, lambda i: send_sum(line_peer(i // n_t), far_tensor(i % n_t)))
        each(n_t - 1, lambda j: send_sum(dp, far_tensor(j)))

        factor = mm(q_root_t, right_parts(q_sum)) / n_dp
        rest = pl.ds(0, n_t - 1)
        pltpu.make_async_copy(wbuf.at[rest], wbuf.at[rest], wrecv).wait()
        pltpu.make_async_copy(gbuf.at[rest], gbuf.at[rest], grecv).wait()
        squares = jnp.zeros((1, LANES), F32)
        terms = jnp.zeros((rank, LANES), F32)
        for t in range(n_t):
            gram = left_parts(unpack(gbuf[t, 0:gram_rows, :], rank, rank))
            squares = squares + gbuf[t, gram_rows + 1 : gram_rows + 2, :]
            scaled = factor * gbuf[t, gram_rows : gram_rows + 1, :]
            terms = terms + scaled * (1.8 * wbuf[t] + mm(gram, right_parts(scaled)))
        at = sc * chunks + mine
        tiles[at] = jnp.sum(terms, axis=0, keepdims=True) + jnp.where(mine == 0, squares, 0.0)

        def send_row(to_dp, to_tensor, to_section):
            pltpu.make_async_remote_copy(
                tiles.at[at], tiles.at[at], tsend, trecv,
                device_id=(to_dp, to_tensor, to_section), device_id_type=MESH,
            ).start()

        def section_of(i):
            return lax.rem(sc + 1 + i, n_s)

        def send_far_row(i):
            send_row(line_peer(i // group), far_tensor((i // n_s) % n_t), section_of(i % n_s))

        def send_near_row(i):
            send_row(dp, far_tensor(i // n_s), section_of(i % n_s))

        each((n_dp - 1) * group, send_far_row)
        each(group - 1, send_near_row)

    for i in range(planes):
        p = jnp.where(upper, i, planes - 1 - i)
        for j in range(per_plane):
            k = p * per_plane + j

            @pl.when(jnp.logical_not(jnp.logical_and(owns, mine == k)))
            def _():
                pltpu.make_async_copy(qfull.at[k], qfull.at[k], arecv.at[k]).wait()

            cols = pl.ds(pl.multiple_of(k * LANES, LANES), LANES)
            right = right_parts(qfull[k])
            approx = mm(left, right)
            mo_v[:, cols] = 0.9 * m_v[:, cols] + approx
            eo_v[:, cols] = e_v[:, cols] - approx
            qf_v[:, cols] = mm(q_root_t, right)
    in_w.wait()
    in_vp.wait()

    count = n_s * chunks

    @pl.when(owns)
    def _():
        got = pl.ds(0, count - 1)
        pltpu.make_async_copy(tiles.at[got], tiles.at[got], trecv).wait()

    @pl.when(jnp.logical_not(owns))
    def _():
        got = pl.ds(0, count)
        pltpu.make_async_copy(tiles.at[got], tiles.at[got], trecv).wait()

    tot_v[...] = total_of(tiles, count)

    pltpu.make_async_copy(pbuf.at[others], pbuf.at[others], psend).wait()
    pltpu.make_async_copy(vbuf.at[others], vbuf.at[others], vsend).wait()

    @pl.when(in_plane)
    def _():
        for j in range(per_plane):

            @pl.when(tn != j)
            def _():
                give_product(j).wait_send()
                give_gram(j).wait_send()

    @pl.when(owns)
    def _():
        got = pl.ds(0, chunks - 1)
        pltpu.make_async_copy(qfull.at[got], qfull.at[got], rsend).wait()
        whole = pl.ds(0, n - 1)
        pltpu.make_async_copy(rbuf.at[whole], rbuf.at[whole], asend).wait()
        sent = tiles.at[pl.ds(0, n * n_s - 1)]
        pltpu.make_async_copy(sent, sent, tsend).wait()

    @pl.when(jnp.logical_not(owns))
    def _():
        pltpu.make_async_copy(qfull, qfull, rsend).wait()


def finish(
    entries,
    eo_v, pf_v, qf_v, mo_v, w_v, vmo_v, vp_v, tot_v,
    eo_hbm, pf_hbm, qf_hbm, mo_hbm, wo_hbm, vmo_hbm, vpo_hbm,
    wo_v, vpo_v, sems,
):
    copies = []

    def write(src, dst):
        copy = pltpu.make_async_copy(src, dst, sems.at[len(copies)])
        copy.start()
        copies.append(copy)

    write(eo_v, eo_hbm)
    write(mo_v, mo_hbm)
    write(qf_v, qf_hbm)
    write(pf_v, pf_hbm)
    write(vmo_v, vmo_hbm)
    total = jnp.maximum(jnp.sum(tot_v[...], axis=1, keepdims=True), 0.0)
    scale = 0.05 / jnp.sqrt(total / entries + 1e-06)
    rows = w_v.shape[0]
    step = rows // WRITES
    for i in range(WRITES):
        at = pl.ds(i * step, step)
        wo_v[at, :] = w_v[at, :] - scale * mo_v[at, :]
        write(wo_v.at[at], wo_hbm.at[at])
    vpo_v[...] = vp_v[...] - scale.reshape(1, 1, 1) * vmo_v[...]
    write(vpo_v, vpo_hbm)
    for copy in copies:
        copy.wait()


def shards(
    sizes,
    grads, errors, q_prev, p_root, q_root, momentum, weights, vec_grads, vec_momentum, vec_params,
):
    n_dp, n_t, n_s = sizes
    rows, width = errors.shape[2:]
    rank = q_prev.shape[2]
    vecs, entries = vec_params.shape[1:]
    n = n_dp * n_t
    own = Owners(n_dp, n_t, width)
    span = own.per_plane * LANES
    n_blocks = len(row_blocks(rows))
    big = (rows, width)
    vec = (vecs, 1, entries)
    packed = (packed_rows(rank, rows), LANES)
    chunk = (rank, LANES)
    any_space = pl.BlockSpec(memory_space=pl.ANY)
    in_vmem = pl.BlockSpec(memory_space=pltpu.VMEM)
    dma = pltpu.SemaphoreType.DMA
    vmem = pltpu.VMEM
    args = (
        grads[0, 0],
        errors[0, 0],
        q_prev[0].T,
        p_root[0],
        q_root[0],
        momentum[0],
        weights[0],
        vec_grads[0, 0][:, None, :],
        vec_momentum[0][:, None, :],
        vec_params[0][:, None, :],
    )
    shapes = (big, (rank, rows), (rank, width), big, big, vec, vec)
    outs = pl.pallas_call(
        functools.partial(kernel, sizes),
        out_shape=tuple(vmem(shape, F32) for shape in shapes + ((1, LANES),)),
        in_specs=[any_space] * 10,
        out_specs=(in_vmem,) * 8,
        scratch_shapes=[
            vmem(big, BF16),
            vmem(big, F32),
            vmem((rank, width), F32),
            vmem((rank, rank), F32),
            vmem((rank, rank), F32),
            vmem(big, F32),
            vmem(vec, F32),
            vmem((own.planes, rows, span), BF16),
            vmem((own.planes, rows, span), BF16),
            vmem((own.planes, rows, span), BF16),
            vmem((own.planes, rows, span), BF16),
            vmem((8, LANES), F32),
            vmem((n_dp,) + packed, F32),
            vmem((n_dp,) + vec, F32),
            vmem((n_t, packed_rows(rank, rank) + 8, LANES), F32),
            vmem((own.per_plane,) + chunk, F32),
            vmem((n_t,) + chunk, F32),
            vmem((own.count,) + chunk, F32),
            vmem((n,) + chunk, F32),
            vmem((own.count,) + chunk, F32),
            vmem((n * n_s, 1, LANES), F32),
            dma((9 + 2 * n_blocks,)),
            dma(()), dma(()), dma(()), dma(()),
            dma((own.per_plane,)), dma(()), dma((own.per_plane,)), dma(()),
            dma(()), dma(()), dma(()), dma((own.count,)), dma(()), dma(()),
        ],
        compiler_params=pltpu.CompilerParams(
            collective_id=0, has_side_effects=True, vmem_limit_bytes=48 * 1024 * 1024
        ),
    )(*(pltpu.with_memory_space_constraint(arg, pltpu.HBM) for arg in args))
    outs = pl.pallas_call(
        functools.partial(finish, n_s * (width * width + vecs * width)),
        out_shape=tuple(pltpu.HBM(shape, F32) for shape in shapes),
        in_specs=[in_vmem] * 8,
        out_specs=(any_space,) * 7,
        scratch_shapes=[vmem(big, F32), vmem(vec, F32), dma((6 + WRITES,))],
    )(*(pltpu.with_memory_space_constraint(out, pltpu.VMEM) for out in outs))
    errors_out, p_factor, q_factor, momentum_out, weights_out, vec_momentum_out, vec_params_out = outs
    return (
        errors_out[None, None],
        p_factor.T[None],
        q_factor.T[None],
        momentum_out[None],
        weights_out[None],
        vec_momentum_out[:, 0][None],
        vec_params_out[:, 0][None],
    )


def solution(mesh):
    sizes = (mesh.shape["dp"], mesh.shape["tensor"], mesh.shape["section"])
    in_specs = (
        P("dp", "section", "tensor", None),
        P("dp", "section", "tensor", None),
        P("section", None, None),
        P("section", None, None),
        P("section", None, None),
        P("section", "tensor", None),
        P("section", "tensor", None),
        P("dp", "section", None, "tensor"),
        P("section", None, "tensor"),
        P("section", None, "tensor"),
    )
    out_specs = (
        P("dp", "section", "tensor", None),
        P("section", "tensor", None),
        P("section", None, None),
        P("section", "tensor", None),
        P("section", "tensor", None),
        P("section", None, "tensor"),
        P("section", None, "tensor"),
    )
    return jax.shard_map(
        functools.partial(shards, sizes),
        mesh=mesh, in_specs=in_specs, out_specs=out_specs, check_vma=False,
    )
```

```python
import functools

import jax
import jax.numpy as jnp
from jax import lax
from jax.experimental import pallas as pl
from jax.experimental.pallas import tpu as pltpu
from jax.sharding import PartitionSpec as P

F32 = jnp.float32
BF16 = jnp.bfloat16
MESH = pl.DeviceIdType.MESH
LANES = 128
UNROLL = 32
HALVES = 2
PARTS = 4
USED = 96
PIECE = 32


def split(x):
    high = x.astype(BF16)
    return high, (x - high.astype(F32)).astype(BF16)


def mm(a, b, dims=((1,), (0,))):
    return lax.dot_general(a, b, (dims, ((), ())), preferred_element_type=F32)


def left_parts(x):
    high, low = split(x)
    return jnp.concatenate([high, high, low], axis=1)


def right_parts(x):
    high, low = split(x)
    return jnp.concatenate([high, low, high], axis=0)


def each(count, body):
    if count <= UNROLL:
        for i in range(count):
            body(i)
    else:
        lax.fori_loop(0, count, lambda i, c: (body(i), c)[1], 0)


def total_of(ref, count):
    if count <= UNROLL:
        total = ref[0]
        for i in range(1, count):
            total = total + ref[i]
        return total
    return lax.fori_loop(1, count, lambda i, acc: acc + ref[i], ref[0])


def row_blocks(rows):
    return [(r, min(LANES, rows - r)) for r in range(0, rows, LANES)]


def packed_rows(rank, rows):
    return rank * rows // LANES


def pack(part):
    rank, size = part.shape
    count = LANES // size
    step = rank // count
    return jnp.concatenate([part[i * step : (i + 1) * step] for i in range(count)], axis=1)


def unpack(x, rank, rows):
    parts = []
    for start, size in row_blocks(rows):
        count = LANES // size
        step = rank // count
        block = x[rank * start // LANES :][:step]
        parts.append(
            jnp.concatenate([block[:, i * size : (i + 1) * size] for i in range(count)], axis=0)
        )
    return jnp.concatenate(parts, axis=1)


def lanes_of(shape):
    return lax.broadcasted_iota(jnp.int32, shape, 1)


def chunks_of(x):
    tiles = [x[:, b * LANES : (b + 1) * LANES] for b in range(3)]
    lane = lanes_of((8, LANES))
    chunks = []
    for tile in tiles:
        tail = tile[24:]
        chunks.append(
            [
                jnp.where(lane < USED, tile[8 * p : 8 * p + 8], pltpu.roll(tail, USED - PIECE * p, 1))
                for p in range(3)
            ]
        )
    rest = last_columns(tiles)
    chunks.append(
        [jnp.where(lane < USED, rest[8 * p : 8 * p + 8], tiles[p][24:]) for p in range(3)]
    )
    return [jnp.concatenate(chunk, axis=0) for chunk in chunks]


def last_columns(tiles):
    lane = lanes_of(tiles[0].shape)
    rolled = [pltpu.roll(tile, PIECE * (b + 1), 1) for b, tile in enumerate(tiles)]
    return jnp.where(lane < PIECE, rolled[0], jnp.where(lane < 2 * PIECE, rolled[1], rolled[2]))


def chunk_tail(chunk):
    lane = lanes_of((8, LANES))
    rolled = [pltpu.roll(chunk[8 * p : 8 * p + 8], PIECE * (p + 1), 1) for p in range(3)]
    return jnp.where(lane < PIECE, rolled[0], jnp.where(lane < 2 * PIECE, rolled[1], rolled[2]))


def columns_of(chunks):
    lane = lanes_of((8, LANES))
    last = chunks[3]
    tiles = []
    for j in range(3):
        rows = [
            jnp.where(
                lane < USED,
                chunks[j][8 * p : 8 * p + 8],
                pltpu.roll(last[8 * p : 8 * p + 8], USED - PIECE * j, 1),
            )
            for p in range(3)
        ]
        rows.append(jnp.where(lane < USED, chunk_tail(chunks[j]), last[8 * j : 8 * j + 8]))
        tiles.append(jnp.concatenate(rows, axis=0))
    return jnp.concatenate(tiles, axis=1)


def near_half(n_dp):
    return jnp.where(2 * lax.axis_index("dp") < n_dp, 0, 1)


def kernel(
    sizes,
    g_hbm, e_hbm, qt_hbm, pr_hbm, qr_hbm, m_hbm, w_hbm, vg_hbm, vm_hbm, vp_hbm,
    e_v, pf_v, qf_v, m_v, w_v, vmo_v, vp_v, tot_v, left_v, qrt_v, qfar_v,
    g_v, qt_v, pr_v, qr_v, vm_v,
    hi_v, lo_v, mhi_v, mlo_v, msq_v, pbuf, vbuf, gsend, gbuf, wsend, wbuf, qpart, rbuf, qsum_v, qfull, tiles,
    in_sem, psend, precv, vsend, vrecv, gsend_sem, grecv, wsend_sem, wrecv,
    rsend, rrecv, asend, arecv, tsend, trecv,
):
    n_dp, n_t, n_s = sizes
    n = n_dp * n_t
    group = n_t * n_s
    dp, tn, sc = lax.axis_index("dp"), lax.axis_index("tensor"), lax.axis_index("section")
    me = dp * n_t + tn
    rank, width = qt_v.shape
    rows = e_v.shape[0]
    span = width // HALVES
    gram_rows = packed_rows(rank, rank)
    chunks = HALVES * PARTS
    first_plane = n_dp // 2 - 1
    plane = dp - first_plane
    keeper = n_s - 1
    mine = plane * PARTS + tn
    in_plane = jnp.logical_and(plane >= 0, plane < HALVES)
    owns = jnp.logical_and(jnp.logical_and(in_plane, tn < PARTS), sc == keeper)
    upper = 2 * dp < n_dp
    near = near_half(n_dp)
    far = 1 - near

    def load(i, src, dst):
        copy = pltpu.make_async_copy(src, dst, in_sem.at[i])
        copy.start()
        return copy

    blocks = row_blocks(rows)
    in_q = load(0, qt_hbm, qt_v)
    in_pr = load(1, pr_hbm, pr_v)
    in_g, in_e = [], []
    for b, (start, size) in enumerate(blocks):
        at = pl.ds(start, size)
        in_g.append(load(9 + 2 * b, g_hbm.at[at], g_v.at[at]))
        in_e.append(load(10 + 2 * b, e_hbm.at[at], e_v.at[at]))
    in_vg = load(2, vg_hbm, vbuf.at[dp])
    in_qr = load(3, qr_hbm, qr_v)
    in_vm = load(4, vm_hbm, vm_v)
    in_m = load(5, m_hbm, m_v)
    in_vp = load(6, vp_hbm, vp_v)
    in_w = load(7, w_hbm, w_v)

    barrier = pltpu.get_barrier_semaphore()
    slot = sc * n_t + tn

    def line_peer(i):
        up, down = n_dp - 1 - i, i
        return jnp.where(
            upper, jnp.where(up > dp, up, up - 1), jnp.where(down < dp, down, down + 1)
        )

    def greet_line(i):
        pl.semaphore_signal(
            barrier, inc=1, device_id=(line_peer(i), tn, sc), device_id_type=MESH
        )

    def greet_plane(i):
        peer = lax.rem(slot + 1 + i, group)
        pl.semaphore_signal(
            barrier, inc=1, device_id=(dp, lax.rem(peer, n_t), peer // n_t), device_id_type=MESH
        )

    each(n_dp - 1, greet_line)
    each(group - 1, greet_plane)

    in_q.wait()
    in_pr.wait()
    q_hi, q_lo = split(mm(left_parts(pr_v[...].T), right_parts(qt_v[...])))
    q_both = jnp.concatenate([q_hi, q_lo], axis=0)
    for b, (start, size) in enumerate(blocks):
        at = pl.ds(start, size)
        in_g[b].wait()
        in_e[b].wait()
        merged = g_v[at, :].astype(F32) + e_v[at, :]
        e_v[at, :] = merged
        m_hi, m_lo = split(merged)
        for p in range(HALVES):
            hi_v[p, at, :] = m_hi[:, p * span : (p + 1) * span]
            lo_v[p, at, :] = m_lo[:, p * span : (p + 1) * span]
        first = mm(q_both, m_hi, ((1,), (1,)))
        second = mm(q_hi, m_lo, ((1,), (1,)))
        pbuf[dp, pl.ds(rank * start // LANES, rank * size // LANES), :] = pack(
            first[:rank] + first[rank:] + second
        )

    pl.semaphore_wait(barrier, n_dp - 1 + group - 1)

    def send_p(i):
        pltpu.make_async_remote_copy(
            pbuf.at[dp], pbuf.at[dp], psend, precv,
            device_id=(line_peer(i), tn, sc), device_id_type=MESH,
        ).start()

    def send_v(i):
        pltpu.make_async_remote_copy(
            vbuf.at[dp], vbuf.at[dp], vsend, vrecv,
            device_id=(line_peer(i), tn, sc), device_id_type=MESH,
        ).start()

    each(n_dp - 1, send_p)
    in_vg.wait()
    each(n_dp - 1, send_v)

    in_m.wait()
    in_qr.wait()
    in_vm.wait()
    in_vp.wait()
    in_w.wait()
    q_root_left = left_parts(qr_v[...])
    q_root_t = left_parts(qr_v[...].T)
    qrt_v[...] = q_root_t

    @pl.when(in_plane)
    def _():
        old = m_v[:, pl.ds(pl.multiple_of(plane * span, LANES), span)]
        m_hi, m_lo = split(old)
        mhi_v[...] = m_hi
        mlo_v[...] = m_lo
        old = 0.9 * old
        squares = jnp.zeros((8, LANES), F32)
        for c in range(span // LANES):
            tile = old[:, c * LANES : (c + 1) * LANES]
            squares = squares + jnp.sum((tile * tile).reshape(rows // 8, 8, LANES), axis=0)
        msq_v[...] = squares

    others = pl.ds(0, n_dp - 1)
    pltpu.make_async_copy(pbuf.at[others], pbuf.at[others], precv).wait()
    pf = unpack(total_of(pbuf, n_dp), rank, rows)
    pf_hi, pf_lo = split(pf)
    pf_both = jnp.concatenate([pf_hi, pf_lo], axis=0)

    for i in range(HALVES):
        p = far if i == 0 else near
        first = mm(pf_both, hi_v[p])
        second = mm(pf_hi, lo_v[p])
        parts = chunks_of(first[:rank] + first[rank:] + second)
        for j in range(PARTS):
            k = p * PARTS + j
            here = jnp.logical_and(owns, mine == k)

            @pl.when(here)
            def _():
                rbuf[keeper, me] = parts[j]

            @pl.when(jnp.logical_not(here))
            def _():
                qpart[k] = parts[j]
                pltpu.make_async_remote_copy(
                    qpart.at[k], rbuf.at[sc, me], rsend, rrecv.at[sc],
                    device_id=(first_plane + p, j, keeper), device_id_type=MESH,
                ).start()

    left_t = mm(q_root_left, right_parts(pf)) / n_dp

    def give_product(j):
        return pltpu.make_async_remote_copy(
            wsend.at[j], wbuf.at[sc, tn], wsend_sem.at[j], wrecv.at[sc],
            device_id=(dp, j, keeper), device_id_type=MESH,
        )

    def give_gram(j):
        return pltpu.make_async_remote_copy(
            gsend, gbuf.at[sc, tn], gsend_sem.at[j], grecv.at[sc],
            device_id=(dp, j, keeper), device_id_type=MESH,
        )

    def stays(j):
        return jnp.logical_and(tn == j, sc == keeper)

    @pl.when(in_plane)
    def _():
        largest = jnp.max(jnp.max(jnp.abs(left_t), axis=1, keepdims=True), axis=0, keepdims=True)
        unit = left_t / jnp.where(largest > 0, largest, 1.0)
        u_hi, u_lo = split(unit)
        first = mm(jnp.concatenate([u_hi, u_lo], axis=0), mhi_v[...])
        second = mm(u_hi, mlo_v[...])
        product = first[:rank] + first[rank:] + second
        parts = [product[:, b * LANES : (b + 1) * LANES] for b in range(3)]
        parts.append(last_columns(parts))
        for j in range(PARTS):

            @pl.when(stays(j))
            def _():
                wbuf[keeper, tn] = parts[j]

            @pl.when(jnp.logical_not(stays(j)))
            def _():
                wsend[j] = parts[j]
                give_product(j).start()

        gram = mm(left_parts(unit), jnp.concatenate([u_hi, u_lo, u_hi], axis=1), ((1,), (1,)))
        pltpu.make_async_copy(vbuf.at[others], vbuf.at[others], vrecv).wait()
        v_new = 0.9 * vm_v[...] + total_of(vbuf, n_dp) / n_dp
        v_row = jnp.sum(v_new * v_new, axis=0)
        v_squares = jnp.zeros((1, LANES), F32)
        for start, size in row_blocks(v_row.shape[1]):
            piece = v_row[:, start : start + size]
            if size < LANES:
                piece = jnp.concatenate([piece, jnp.zeros((1, LANES - size), F32)], axis=1)
            v_squares = v_squares + piece
        squares = jnp.sum(msq_v[...], axis=0, keepdims=True)
        squares = squares + jnp.where(plane == 0, v_squares, 0.0)
        row = lax.broadcasted_iota(jnp.int32, (8, LANES), 0)
        gsend[0:gram_rows, :] = pack(gram)
        gsend[gram_rows:, :] = jnp.where(row == 0, largest, squares)

        @pl.when(owns)
        def _():
            gbuf[keeper, tn] = gsend[...]

        for j in range(PARTS):

            @pl.when(jnp.logical_not(stays(j)))
            def _():
                give_gram(j).start()

    @pl.when(jnp.logical_not(in_plane))
    def _():
        pltpu.make_async_copy(vbuf.at[others], vbuf.at[others], vrecv).wait()

    pf_v[...] = pf
    left_v[...] = left_parts(left_t.T)
    vmo_v[...] = 0.9 * vm_v[...] + total_of(vbuf, n_dp) / n_dp

    @pl.when(owns)
    def _():
        used = lanes_of((rank, LANES)) < USED
        row = jnp.zeros((1, LANES), F32)
        for turn in range(n_s):
            s = n_s - 1 - turn
            count = n - 1 if s == keeper else n
            whole = pl.ds(0, count)
            pltpu.make_async_copy(rbuf.at[s, whole], rbuf.at[s, whole], rrecv.at[s]).wait()
            q_sum = total_of(rbuf.at[s], n)
            qsum_v[s] = q_sum
            if s == keeper:
                qfull[mine] = q_sum

            def send_sum(i):
                peer = i + jnp.where(i >= me, 1, 0) if s == keeper else i
                pltpu.make_async_remote_copy(
                    qsum_v.at[s], qfull.at[mine], asend, arecv.at[plane],
                    device_id=(peer // n_t, lax.rem(peer, n_t), s), device_id_type=MESH,
                ).start()

            each(count, send_sum)

            rest = pl.ds(0, n_t - 1 if s == keeper else n_t)
            pltpu.make_async_copy(wbuf.at[s, rest], wbuf.at[s, rest], wrecv.at[s]).wait()
            pltpu.make_async_copy(gbuf.at[s, rest], gbuf.at[s, rest], grecv.at[s]).wait()
            levels = [gbuf[s, t, gram_rows : gram_rows + 1, :] for t in range(n_t)]
            level = levels[0]
            for t in range(1, n_t):
                level = jnp.maximum(level, levels[t])
            inverse = 1.0 / jnp.where(level > 0, level, 1.0)
            product = jnp.zeros((rank, LANES), F32)
            gram = jnp.zeros((gram_rows, LANES), F32)
            for t in range(n_t):
                share = levels[t] * inverse
                product = product + share * wbuf[s, t]
                gram = gram + share * share * gbuf[s, t, 0:gram_rows, :]
            product = jnp.where(used, 1.8 * product, 0.0)
            gram = left_parts(unpack(gram, rank, rank))
            scaled = jnp.concatenate([q_sum, chunk_tail(q_sum)], axis=0) * level
            scaled = jnp.where(used, scaled, 0.0)
            terms = scaled * (product + mm(gram, right_parts(scaled)))
            row = row + jnp.sum(terms, axis=0, keepdims=True)
            row = row + gbuf[s, tn, gram_rows + 1 : gram_rows + 2, :]

        tiles[mine] = row

        def send_row_to(i):
            peer = i + jnp.where(i >= me * n_s + sc, 1, 0)
            pltpu.make_async_remote_copy(
                tiles.at[mine], tiles.at[mine], tsend, trecv,
                device_id=(peer // group, lax.rem(peer // n_s, n_t), lax.rem(peer, n_s)),
                device_id_type=MESH,
            ).start()

        each(n * n_s - 1, send_row_to)

    @pl.when(owns)
    def _():
        got = pl.ds(0, PARTS - 1)
        pltpu.make_async_copy(qfull.at[got], qfull.at[got], arecv.at[near]).wait()

    @pl.when(jnp.logical_not(owns))
    def _():
        got = pl.ds(0, PARTS)
        pltpu.make_async_copy(qfull.at[got], qfull.at[got], arecv.at[near]).wait()

    right = right_parts(columns_of([qfull[near * PARTS + j] for j in range(PARTS)]))
    approx = mm(left_v[...], right)
    cols = pl.ds(pl.multiple_of(near * span, LANES), span)
    m_v[:, cols] = 0.9 * m_v[:, cols] + approx
    e_v[:, cols] = e_v[:, cols] - approx
    qf_v[:, cols] = mm(q_root_t, right)

    got = pl.ds(0, PARTS)
    pltpu.make_async_copy(qfull.at[got], qfull.at[got], arecv.at[far]).wait()
    qfar_v[...] = columns_of([qfull[far * PARTS + j] for j in range(PARTS)])

    count = chunks

    @pl.when(owns)
    def _():
        got = pl.ds(0, count - 1)
        pltpu.make_async_copy(tiles.at[got], tiles.at[got], trecv).wait()

    @pl.when(jnp.logical_not(owns))
    def _():
        got = pl.ds(0, count)
        pltpu.make_async_copy(tiles.at[got], tiles.at[got], trecv).wait()

    tot_v[...] = total_of(tiles, count)

    pltpu.make_async_copy(pbuf.at[others], pbuf.at[others], psend).wait()
    pltpu.make_async_copy(vbuf.at[others], vbuf.at[others], vsend).wait()

    @pl.when(in_plane)
    def _():
        for j in range(PARTS):

            @pl.when(jnp.logical_not(stays(j)))
            def _():
                give_product(j).wait_send()
                give_gram(j).wait_send()

    @pl.when(owns)
    def _():
        got = pl.ds(0, chunks - 1)
        pltpu.make_async_copy(qfull.at[got], qfull.at[got], rsend).wait()
        for s in range(n_s):
            whole = pl.ds(0, n - 1 if s == keeper else n)
            pltpu.make_async_copy(rbuf.at[s, whole], rbuf.at[s, whole], asend).wait()
        sent = tiles.at[pl.ds(0, n * n_s - 1)]
        pltpu.make_async_copy(sent, sent, tsend).wait()

    @pl.when(jnp.logical_not(owns))
    def _():
        pltpu.make_async_copy(qfull, qfull, rsend).wait()


def finish(
    n_dp, entries,
    e_v, pf_v, qf_v, m_v, w_v, vmo_v, vp_v, tot_v, left_v, qrt_v, qfar_v,
    eo_hbm, pf_hbm, qf_hbm, mo_hbm, wo_hbm, vmo_hbm, vpo_hbm,
    eo_v, mo_v, wo_v, qff_v, vpo_v, sems,
):
    copies = []
    span = qfar_v.shape[1]
    near = pl.multiple_of(near_half(n_dp) * span, LANES)
    far = pl.multiple_of(span - near, LANES)
    cols = pl.ds(near, span)

    def write(src, dst):
        copy = pltpu.make_async_copy(src, dst, sems.at[len(copies)])
        copy.start()
        copies.append(copy)

    write(e_v.at[:, cols], eo_hbm.at[:, cols])
    write(m_v.at[:, cols], mo_hbm.at[:, cols])
    write(qf_v.at[:, cols], qf_hbm.at[:, cols])
    write(pf_v, pf_hbm)
    write(vmo_v, vmo_hbm)
    total = jnp.maximum(jnp.sum(tot_v[...], axis=1, keepdims=True), 0.0)
    scale = 0.05 / jnp.sqrt(total / entries + 1e-06)
    for c in range(span // LANES):
        here = pl.ds(c * LANES, LANES)
        cols = pl.ds(pl.multiple_of(far + c * LANES, LANES), LANES)
        right = right_parts(qfar_v[:, here])
        approx = mm(left_v[...], right)
        new = 0.9 * m_v[:, cols] + approx
        eo_v[:, here] = e_v[:, cols] - approx
        write(eo_v.at[:, here], eo_hbm.at[:, cols])
        mo_v[:, here] = new
        write(mo_v.at[:, here], mo_hbm.at[:, cols])
        wo_v[:, cols] = w_v[:, cols] - scale * new
        write(wo_v.at[:, cols], wo_hbm.at[:, cols])
        qff_v[:, here] = mm(qrt_v[...], right)
        write(qff_v.at[:, here], qf_hbm.at[:, cols])
    cols = pl.ds(near, span)
    wo_v[:, cols] = w_v[:, cols] - scale * m_v[:, cols]
    write(wo_v.at[:, cols], wo_hbm.at[:, cols])
    vpo_v[...] = vp_v[...] - scale.reshape(1, 1, 1) * vmo_v[...]
    write(vpo_v, vpo_hbm)
    for copy in copies:
        copy.wait()


def shards(
    sizes,
    grads, errors, q_prev, p_root, q_root, momentum, weights, vec_grads, vec_momentum, vec_params,
):
    n_dp, n_t, n_s = sizes
    rows, width = errors.shape[2:]
    rank = q_prev.shape[2]
    vecs, entries = vec_params.shape[1:]
    n = n_dp * n_t
    chunks = HALVES * PARTS
    span = width // HALVES
    n_blocks = len(row_blocks(rows))
    big = (rows, width)
    vec = (vecs, 1, entries)
    packed = (packed_rows(rank, rows), LANES)
    square = (rank, LANES)
    chunk = (rank * USED // LANES, LANES)
    any_space = pl.BlockSpec(memory_space=pl.ANY)
    in_vmem = pl.BlockSpec(memory_space=pltpu.VMEM)
    dma = pltpu.SemaphoreType.DMA
    vmem = pltpu.VMEM
    args = (
        grads[0, 0],
        errors[0, 0],
        q_prev[0].T,
        p_root[0],
        q_root[0],
        momentum[0],
        weights[0],
        vec_grads[0, 0][:, None, :],
        vec_momentum[0][:, None, :],
        vec_params[0][:, None, :],
    )
    shapes = (big, (rank, rows), (rank, width), big, big, vec, vec)
    kept = tuple(vmem(shape, F32) for shape in shapes + ((1, LANES),)) + (
        vmem((rows, 3 * rank), BF16),
        vmem((rank, 3 * rank), BF16),
        vmem((rank, span), F32),
    )
    outs = pl.pallas_call(
        functools.partial(kernel, sizes),
        out_shape=kept,
        in_specs=[any_space] * 10,
        out_specs=(in_vmem,) * len(kept),
        scratch_shapes=[
            vmem(big, BF16),
            vmem((rank, width), F32),
            vmem((rank, rank), F32),
            vmem((rank, rank), F32),
            vmem(vec, F32),
            vmem((HALVES, rows, span), BF16),
            vmem((HALVES, rows, span), BF16),
            vmem((rows, span), BF16),
            vmem((rows, span), BF16),
            vmem((8, LANES), F32),
            vmem((n_dp,) + packed, F32),
            vmem((n_dp,) + vec, F32),
            vmem((packed_rows(rank, rank) + 8, LANES), F32),
            vmem((n_s, n_t, packed_rows(rank, rank) + 8, LANES), F32),
            vmem((PARTS,) + square, F32),
            vmem((n_s, n_t) + square, F32),
            vmem((chunks,) + chunk, F32),
            vmem((n_s, n) + chunk, F32),
            vmem((n_s,) + chunk, F32),
            vmem((chunks,) + chunk, F32),
            vmem((n * n_s, 1, LANES), F32),
            dma((9 + 2 * n_blocks,)),
            dma(()), dma(()), dma(()), dma(()),
            dma((PARTS,)), dma((n_s,)), dma((PARTS,)), dma((n_s,)),
            dma(()), dma((n_s,)), dma(()), dma((HALVES,)), dma(()), dma(()),
        ],
        compiler_params=pltpu.CompilerParams(
            collective_id=0, has_side_effects=True, vmem_limit_bytes=48 * 1024 * 1024
        ),
    )(*(pltpu.with_memory_space_constraint(arg, pltpu.HBM) for arg in args))
    outs = pl.pallas_call(
        functools.partial(finish, n_dp, n_s * (width * width + vecs * width)),
        out_shape=tuple(pltpu.HBM(shape, F32) for shape in shapes),
        in_specs=[in_vmem] * len(kept),
        out_specs=(any_space,) * 7,
        scratch_shapes=[
            vmem((rows, span), F32),
            vmem((rows, span), F32),
            vmem(big, F32),
            vmem((rank, span), F32),
            vmem(vec, F32),
            dma((7 + 4 * (span // LANES),)),
        ],
    )(*(pltpu.with_memory_space_constraint(out, pltpu.VMEM) for out in outs))
    errors_out, p_factor, q_factor, momentum_out, weights_out, vec_momentum_out, vec_params_out = outs
    return (
        errors_out[None, None],
        p_factor.T[None],
        q_factor.T[None],
        momentum_out[None],
        weights_out[None],
        vec_momentum_out[:, 0][None],
        vec_params_out[:, 0][None],
    )


def solution(mesh):
    sizes = (mesh.shape["dp"], mesh.shape["tensor"], mesh.shape["section"])
    in_specs = (
        P("dp", "section", "tensor", None),
        P("dp", "section", "tensor", None),
        P("section", None, None),
        P("section", None, None),
        P("section", None, None),
        P("section", "tensor", None),
        P("section", "tensor", None),
        P("dp", "section", None, "tensor"),
        P("section", None, "tensor"),
        P("section", None, "tensor"),
    )
    out_specs = (
        P("dp", "section", "tensor", None),
        P("section", "tensor", None),
        P("section", None, None),
        P("section", "tensor", None),
        P("section", "tensor", None),
        P("section", None, "tensor"),
        P("section", None, "tensor"),
    )
    return jax.shard_map(
        functools.partial(shards, sizes),
        mesh=mesh, in_specs=in_specs, out_specs=out_specs, check_vma=False,
    )
```

```python
import functools

import jax
import jax.numpy as jnp
from jax import lax
from jax.experimental import pallas as pl
from jax.experimental.pallas import tpu as pltpu
from jax.sharding import PartitionSpec as P

F32 = jnp.float32
BF16 = jnp.bfloat16
MESH = pl.DeviceIdType.MESH
LANES = 128
UNROLL = 32
HALVES = 2
PARTS = 4
USED = 96
PIECE = 32


def split(x):
    high = x.astype(BF16)
    return high, (x - high.astype(F32)).astype(BF16)


def mm(a, b, dims=((1,), (0,))):
    return lax.dot_general(a, b, (dims, ((), ())), preferred_element_type=F32)


def left_parts(x):
    high, low = split(x)
    return jnp.concatenate([high, high, low], axis=1)


def right_parts(x):
    high, low = split(x)
    return jnp.concatenate([high, low, high], axis=0)


def each(count, body):
    if count <= UNROLL:
        for i in range(count):
            body(i)
    else:
        lax.fori_loop(0, count, lambda i, c: (body(i), c)[1], 0)


def total_of(ref, count):
    if count <= UNROLL:
        total = ref[0]
        for i in range(1, count):
            total = total + ref[i]
        return total
    return lax.fori_loop(1, count, lambda i, acc: acc + ref[i], ref[0])


def row_blocks(rows):
    return [(r, min(LANES, rows - r)) for r in range(0, rows, LANES)]


def packed_rows(rank, rows):
    return rank * rows // LANES


def pack(part):
    rank, size = part.shape
    count = LANES // size
    step = rank // count
    return jnp.concatenate([part[i * step : (i + 1) * step] for i in range(count)], axis=1)


def unpack(x, rank, rows):
    parts = []
    for start, size in row_blocks(rows):
        count = LANES // size
        step = rank // count
        block = x[rank * start // LANES :][:step]
        parts.append(
            jnp.concatenate([block[:, i * size : (i + 1) * size] for i in range(count)], axis=0)
        )
    return jnp.concatenate(parts, axis=1)


def lanes_of(shape):
    return lax.broadcasted_iota(jnp.int32, shape, 1)


def chunks_of(x):
    tiles = [x[:, b * LANES : (b + 1) * LANES] for b in range(3)]
    lane = lanes_of((8, LANES))
    chunks = []
    for tile in tiles:
        tail = tile[24:]
        chunks.append(
            [
                jnp.where(lane < USED, tile[8 * p : 8 * p + 8], pltpu.roll(tail, USED - PIECE * p, 1))
                for p in range(3)
            ]
        )
    rest = last_columns(tiles)
    chunks.append(
        [jnp.where(lane < USED, rest[8 * p : 8 * p + 8], tiles[p][24:]) for p in range(3)]
    )
    return [jnp.concatenate(chunk, axis=0) for chunk in chunks]


def last_columns(tiles):
    lane = lanes_of(tiles[0].shape)
    rolled = [pltpu.roll(tile, PIECE * (b + 1), 1) for b, tile in enumerate(tiles)]
    return jnp.where(lane < PIECE, rolled[0], jnp.where(lane < 2 * PIECE, rolled[1], rolled[2]))


def chunk_tail(chunk):
    lane = lanes_of((8, LANES))
    rolled = [pltpu.roll(chunk[8 * p : 8 * p + 8], PIECE * (p + 1), 1) for p in range(3)]
    return jnp.where(lane < PIECE, rolled[0], jnp.where(lane < 2 * PIECE, rolled[1], rolled[2]))


def columns_of(chunks):
    lane = lanes_of((8, LANES))
    last = chunks[3]
    tiles = []
    for j in range(3):
        rows = [
            jnp.where(
                lane < USED,
                chunks[j][8 * p : 8 * p + 8],
                pltpu.roll(last[8 * p : 8 * p + 8], USED - PIECE * j, 1),
            )
            for p in range(3)
        ]
        rows.append(jnp.where(lane < USED, chunk_tail(chunks[j]), last[8 * j : 8 * j + 8]))
        tiles.append(jnp.concatenate(rows, axis=0))
    return jnp.concatenate(tiles, axis=1)


def near_half(n_dp):
    return jnp.where(2 * lax.axis_index("dp") < n_dp, 0, 1)


def kernel(
    sizes,
    g_hbm, e_hbm, qt_hbm, pr_hbm, qr_hbm, m_hbm, w_hbm, vg_hbm, vm_hbm, vp_hbm,
    e_v, pf_v, qf_v, m_v, w_v, vmo_v, vp_v, tot_v, left_v, qrt_v, qfar_v,
    g_v, qt_v, pr_v, qr_v, vm_v,
    hi_v, lo_v, mhi_v, mlo_v, msq_v, pbuf, vbuf, gsend, gbuf, wsend, wbuf, qpart, rbuf, qsum_v, qfull, tiles,
    in_sem, psend, precv, vsend, vrecv, gsend_sem, grecv, wsend_sem, wrecv,
    rsend, rrecv, asend, arecv, tsend, trecv,
):
    n_dp, n_t, n_s = sizes
    n = n_dp * n_t
    group = n_t * n_s
    dp, tn, sc = lax.axis_index("dp"), lax.axis_index("tensor"), lax.axis_index("section")
    me = dp * n_t + tn
    rank, width = qt_v.shape
    rows = e_v.shape[0]
    span = width // HALVES
    gram_rows = packed_rows(rank, rank)
    chunks = HALVES * PARTS
    first_plane = n_dp // 2 - 1
    plane = dp - first_plane
    keeper = n_s - 1
    mine = plane * PARTS + tn
    in_plane = jnp.logical_and(plane >= 0, plane < HALVES)
    owns = jnp.logical_and(jnp.logical_and(in_plane, tn < PARTS), sc == keeper)
    upper = 2 * dp < n_dp
    near = near_half(n_dp)
    far = 1 - near

    def load(i, src, dst):
        copy = pltpu.make_async_copy(src, dst, in_sem.at[i])
        copy.start()
        return copy

    blocks = row_blocks(rows)
    in_q = load(0, qt_hbm, qt_v)
    in_pr = load(1, pr_hbm, pr_v)
    in_g, in_e = [], []
    for b, (start, size) in enumerate(blocks):
        at = pl.ds(start, size)
        in_g.append(load(9 + 2 * b, g_hbm.at[at], g_v.at[at]))
        in_e.append(load(10 + 2 * b, e_hbm.at[at], e_v.at[at]))
    in_vg = load(2, vg_hbm, vbuf.at[dp])
    in_qr = load(3, qr_hbm, qr_v)
    in_vm = load(4, vm_hbm, vm_v)
    in_m = load(5, m_hbm, m_v)
    in_vp = load(6, vp_hbm, vp_v)
    in_w = load(7, w_hbm, w_v)

    barrier = pltpu.get_barrier_semaphore()
    slot = sc * n_t + tn

    def line_peer(i):
        up, down = n_dp - 1 - i, i
        return jnp.where(
            upper, jnp.where(up > dp, up, up - 1), jnp.where(down < dp, down, down + 1)
        )

    def greet_line(i):
        pl.semaphore_signal(
            barrier, inc=1, device_id=(line_peer(i), tn, sc), device_id_type=MESH
        )

    def greet_plane(i):
        peer = lax.rem(slot + 1 + i, group)
        pl.semaphore_signal(
            barrier, inc=1, device_id=(dp, lax.rem(peer, n_t), peer // n_t), device_id_type=MESH
        )

    each(n_dp - 1, greet_line)
    each(group - 1, greet_plane)

    in_q.wait()
    in_pr.wait()
    q_hi, q_lo = split(mm(left_parts(pr_v[...].T), right_parts(qt_v[...])))
    q_both = jnp.concatenate([q_hi, q_lo], axis=0)
    for b, (start, size) in enumerate(blocks):
        at = pl.ds(start, size)
        in_g[b].wait()
        in_e[b].wait()
        merged = g_v[at, :].astype(F32) + e_v[at, :]
        e_v[at, :] = merged
        m_hi, m_lo = split(merged)
        for p in range(HALVES):
            hi_v[p, at, :] = m_hi[:, p * span : (p + 1) * span]
            lo_v[p, at, :] = m_lo[:, p * span : (p + 1) * span]
        first = mm(q_both, m_hi, ((1,), (1,)))
        second = mm(q_hi, m_lo, ((1,), (1,)))
        pbuf[dp, pl.ds(rank * start // LANES, rank * size // LANES), :] = pack(
            first[:rank] + first[rank:] + second
        )

    pl.semaphore_wait(barrier, n_dp - 1 + group - 1)

    def send_p(i):
        pltpu.make_async_remote_copy(
            pbuf.at[dp], pbuf.at[dp], psend, precv,
            device_id=(line_peer(i), tn, sc), device_id_type=MESH,
        ).start()

    def send_v(i):
        pltpu.make_async_remote_copy(
            vbuf.at[dp], vbuf.at[dp], vsend, vrecv,
            device_id=(line_peer(i), tn, sc), device_id_type=MESH,
        ).start()

    each(n_dp - 1, send_p)
    in_vg.wait()
    each(n_dp - 1, send_v)

    in_m.wait()
    in_qr.wait()
    in_vm.wait()
    in_vp.wait()
    in_w.wait()
    q_root_left = left_parts(qr_v[...])
    q_root_t = left_parts(qr_v[...].T)
    qrt_v[...] = q_root_t

    old = m_v[:, pl.ds(pl.multiple_of(near * span, LANES), span)]
    m_hi, m_lo = split(old)
    mhi_v[...] = m_hi
    mlo_v[...] = m_lo
    old = 0.9 * old
    squares = jnp.zeros((8, LANES), F32)
    for c in range(span // LANES):
        tile = old[:, c * LANES : (c + 1) * LANES]
        squares = squares + jnp.sum((tile * tile).reshape(rows // 8, 8, LANES), axis=0)
    msq_v[...] = squares

    others = pl.ds(0, n_dp - 1)
    pltpu.make_async_copy(pbuf.at[others], pbuf.at[others], precv).wait()
    pf = unpack(total_of(pbuf, n_dp), rank, rows)
    pf_hi, pf_lo = split(pf)
    pf_both = jnp.concatenate([pf_hi, pf_lo], axis=0)

    def q_parts(p):
        first = mm(pf_both, hi_v[p])
        second = mm(pf_hi, lo_v[p])
        return chunks_of(first[:rank] + first[rank:] + second)

    def send_q(k, owner_dp, j):
        pltpu.make_async_remote_copy(
            qpart.at[k], rbuf.at[sc, me], rsend, rrecv.at[sc],
            device_id=(owner_dp, j, keeper), device_id_type=MESH,
        ).start()

    parts = q_parts(far)
    for j in range(PARTS):
        qpart[far * PARTS + j] = parts[j]
    left_t = mm(q_root_left, right_parts(pf)) / n_dp
    largest = jnp.max(jnp.max(jnp.abs(left_t), axis=1, keepdims=True), axis=0, keepdims=True)
    unit = left_t / jnp.where(largest > 0, largest, 1.0)
    u_hi, u_lo = split(unit)
    for j in range(PARTS):
        send_q(far * PARTS + j, first_plane + far, j)

    parts = q_parts(near)
    first = mm(jnp.concatenate([u_hi, u_lo], axis=0), mhi_v[...])
    second = mm(u_hi, mlo_v[...])
    product = first[:rank] + first[rank:] + second
    products = chunks_of(product)
    gram = mm(left_parts(unit), jnp.concatenate([u_hi, u_lo, u_hi], axis=1), ((1,), (1,)))
    gsend[0:gram_rows, :] = pack(gram)
    for j in range(PARTS):
        qpart[near * PARTS + j] = parts[j]
        wsend[j] = products[j]
    def give_product(j):
        return pltpu.make_async_remote_copy(
            wsend.at[j], wbuf.at[sc, tn], wsend_sem.at[j], wrecv.at[sc],
            device_id=(dp, j, keeper), device_id_type=MESH,
        )

    def give_gram(j):
        return pltpu.make_async_remote_copy(
            gsend, gbuf.at[sc, tn], gsend_sem.at[j], grecv.at[sc],
            device_id=(dp, j, keeper), device_id_type=MESH,
        )

    def stays(j):
        return jnp.logical_and(tn == j, sc == keeper)

    @pl.when(in_plane)
    def _():
        for j in range(PARTS):

            @pl.when(stays(j))
            def _():
                wbuf[keeper, tn] = wsend[j]

            @pl.when(jnp.logical_not(stays(j)))
            def _():
                give_product(j).start()

        pltpu.make_async_copy(vbuf.at[others], vbuf.at[others], vrecv).wait()
        v_new = 0.9 * vm_v[...] + total_of(vbuf, n_dp) / n_dp
        v_row = jnp.sum(v_new * v_new, axis=0)
        v_squares = jnp.zeros((1, LANES), F32)
        for start, size in row_blocks(v_row.shape[1]):
            piece = v_row[:, start : start + size]
            if size < LANES:
                piece = jnp.concatenate([piece, jnp.zeros((1, LANES - size), F32)], axis=1)
            v_squares = v_squares + piece
        squares = jnp.sum(msq_v[...], axis=0, keepdims=True)
        squares = squares + jnp.where(plane == 0, v_squares, 0.0)
        row = lax.broadcasted_iota(jnp.int32, (8, LANES), 0)
        gsend[gram_rows:, :] = jnp.where(row == 0, largest, squares)

        @pl.when(owns)
        def _():
            gbuf[keeper, tn] = gsend[...]

        for j in range(PARTS):

            @pl.when(jnp.logical_not(stays(j)))
            def _():
                give_gram(j).start()

    for j in range(PARTS):
        here = jnp.logical_and(owns, tn == j)

        @pl.when(here)
        def _():
            rbuf[keeper, me] = qpart[near * PARTS + j]

        @pl.when(jnp.logical_not(here))
        def _():
            send_q(near * PARTS + j, first_plane + near, j)

    @pl.when(jnp.logical_not(in_plane))
    def _():
        pltpu.make_async_copy(vbuf.at[others], vbuf.at[others], vrecv).wait()

    pf_v[...] = pf
    left_v[...] = left_parts(left_t.T)
    vmo_v[...] = 0.9 * vm_v[...] + total_of(vbuf, n_dp) / n_dp

    @pl.when(owns)
    def _():
        used = lanes_of((rank, LANES)) < USED

        def prepare(s):
            rest = pl.ds(0, n_t - 1 if s == keeper else n_t)
            pltpu.make_async_copy(wbuf.at[s, rest], wbuf.at[s, rest], wrecv.at[s]).wait()
            pltpu.make_async_copy(gbuf.at[s, rest], gbuf.at[s, rest], grecv.at[s]).wait()
            levels = [gbuf[s, t, gram_rows : gram_rows + 1, :] for t in range(n_t)]
            level = levels[0]
            for t in range(1, n_t):
                level = jnp.maximum(level, levels[t])
            inverse = 1.0 / jnp.where(level > 0, level, 1.0)
            product = jnp.zeros((rank * USED // LANES, LANES), F32)
            gram = jnp.zeros((gram_rows, LANES), F32)
            for t in range(n_t):
                share = levels[t] * inverse
                product = product + share * wbuf[s, t]
                gram = gram + share * share * gbuf[s, t, 0:gram_rows, :]
            product = jnp.concatenate([product, chunk_tail(product)], axis=0)
            product = jnp.where(used, 1.8 * product, 0.0)
            gram = left_parts(unpack(gram, rank, rank))
            return product, gram, level, gbuf[s, tn, gram_rows + 1 : gram_rows + 2, :]

        def row_of(q_sum, prepared):
            product, gram, level, squares = prepared
            scaled = jnp.concatenate([q_sum, chunk_tail(q_sum)], axis=0) * level
            scaled = jnp.where(used, scaled, 0.0)
            terms = scaled * (product + mm(gram, right_parts(scaled)))
            return jnp.sum(terms, axis=0, keepdims=True) + squares

        def summed(s):
            whole = pl.ds(0, n - 1 if s == keeper else n)
            pltpu.make_async_copy(rbuf.at[s, whole], rbuf.at[s, whole], rrecv.at[s]).wait()
            q_sum = total_of(rbuf.at[s], n)
            qsum_v[s] = q_sum
            return q_sum

        def send_sum(s, i):
            peer = i + jnp.where(i >= me, 1, 0) if s == keeper else i
            pltpu.make_async_remote_copy(
                qsum_v.at[s], qfull.at[mine], asend, arecv.at[plane],
                device_id=(peer // n_t, lax.rem(peer, n_t), s), device_id_type=MESH,
            ).start()

        def send_row(i):
            peer = i + jnp.where(i >= me * n_s + sc, 1, 0)
            pltpu.make_async_remote_copy(
                tiles.at[mine], tiles.at[mine], tsend, trecv,
                device_id=(peer // group, lax.rem(peer // n_s, n_t), lax.rem(peer, n_s)),
                device_id_type=MESH,
            ).start()

        q_sum = summed(keeper)
        qfull[mine] = q_sum
        each(n - 1, lambda i: send_sum(keeper, i))
        row = row_of(q_sum, prepare(keeper))
        for s in range(keeper):
            prepared = prepare(s)
            q_sum = summed(s)
            row = row + row_of(q_sum, prepared)
            if s < keeper - 1:
                each(n, lambda i: send_sum(s, i))
        tiles[mine] = row
        each(n * n_s - 1, send_row)
        each(n, lambda i: send_sum(keeper - 1, i))

    pltpu.make_async_copy(pbuf.at[others], pbuf.at[others], psend).wait()
    pltpu.make_async_copy(vbuf.at[others], vbuf.at[others], vsend).wait()

    @pl.when(in_plane)
    def _():
        for j in range(PARTS):

            @pl.when(jnp.logical_not(stays(j)))
            def _():
                give_product(j).wait_send()
                give_gram(j).wait_send()

    @pl.when(owns)
    def _():
        got = pl.ds(0, chunks - 1)
        pltpu.make_async_copy(qfull.at[got], qfull.at[got], rsend).wait()

    @pl.when(jnp.logical_not(owns))
    def _():
        pltpu.make_async_copy(qfull, qfull, rsend).wait()

    @pl.when(owns)
    def _():
        got = pl.ds(0, PARTS - 1)
        pltpu.make_async_copy(qfull.at[got], qfull.at[got], arecv.at[near]).wait()

    @pl.when(jnp.logical_not(owns))
    def _():
        got = pl.ds(0, PARTS)
        pltpu.make_async_copy(qfull.at[got], qfull.at[got], arecv.at[near]).wait()

    right = right_parts(columns_of([qfull[near * PARTS + j] for j in range(PARTS)]))
    approx = mm(left_v[...], right)
    cols = pl.ds(pl.multiple_of(near * span, LANES), span)
    m_v[:, cols] = 0.9 * m_v[:, cols] + approx
    e_v[:, cols] = e_v[:, cols] - approx
    qf_v[:, cols] = mm(q_root_t, right)

    got = pl.ds(0, PARTS)
    pltpu.make_async_copy(qfull.at[got], qfull.at[got], arecv.at[far]).wait()
    qfar_v[...] = columns_of([qfull[far * PARTS + j] for j in range(PARTS)])

    count = chunks

    @pl.when(owns)
    def _():
        got = pl.ds(0, count - 1)
        pltpu.make_async_copy(tiles.at[got], tiles.at[got], trecv).wait()

    @pl.when(jnp.logical_not(owns))
    def _():
        got = pl.ds(0, count)
        pltpu.make_async_copy(tiles.at[got], tiles.at[got], trecv).wait()

    tot_v[...] = total_of(tiles, count)

    @pl.when(owns)
    def _():
        for s in range(n_s):
            whole = pl.ds(0, n - 1 if s == keeper else n)
            pltpu.make_async_copy(rbuf.at[s, whole], rbuf.at[s, whole], asend).wait()
        sent = tiles.at[pl.ds(0, n * n_s - 1)]
        pltpu.make_async_copy(sent, sent, tsend).wait()


def finish(
    n_dp, entries,
    e_v, pf_v, qf_v, m_v, w_v, vmo_v, vp_v, tot_v, left_v, qrt_v, qfar_v,
    eo_hbm, pf_hbm, qf_hbm, mo_hbm, wo_hbm, vmo_hbm, vpo_hbm,
    eo_v, mo_v, wo_v, qff_v, vpo_v, sems,
):
    copies = []
    span = qfar_v.shape[1]
    near = pl.multiple_of(near_half(n_dp) * span, LANES)
    far = pl.multiple_of(span - near, LANES)
    cols = pl.ds(near, span)

    def write(src, dst):
        copy = pltpu.make_async_copy(src, dst, sems.at[len(copies)])
        copy.start()
        copies.append(copy)

    write(e_v.at[:, cols], eo_hbm.at[:, cols])
    write(m_v.at[:, cols], mo_hbm.at[:, cols])
    write(qf_v.at[:, cols], qf_hbm.at[:, cols])
    write(pf_v, pf_hbm)
    write(vmo_v, vmo_hbm)
    total = jnp.maximum(jnp.sum(tot_v[...], axis=1, keepdims=True), 0.0)
    scale = 0.05 / jnp.sqrt(total / entries + 1e-06)
    for c in range(span // LANES):
        here = pl.ds(c * LANES, LANES)
        cols = pl.ds(pl.multiple_of(far + c * LANES, LANES), LANES)
        right = right_parts(qfar_v[:, here])
        approx = mm(left_v[...], right)
        new = 0.9 * m_v[:, cols] + approx
        eo_v[:, here] = e_v[:, cols] - approx
        write(eo_v.at[:, here], eo_hbm.at[:, cols])
        mo_v[:, here] = new
        write(mo_v.at[:, here], mo_hbm.at[:, cols])
        wo_v[:, cols] = w_v[:, cols] - scale * new
        write(wo_v.at[:, cols], wo_hbm.at[:, cols])
        qff_v[:, here] = mm(qrt_v[...], right)
        write(qff_v.at[:, here], qf_hbm.at[:, cols])
    cols = pl.ds(near, span)
    wo_v[:, cols] = w_v[:, cols] - scale * m_v[:, cols]
    write(wo_v.at[:, cols], wo_hbm.at[:, cols])
    vpo_v[...] = vp_v[...] - scale.reshape(1, 1, 1) * vmo_v[...]
    write(vpo_v, vpo_hbm)
    for copy in copies:
        copy.wait()


def shards(
    sizes,
    grads, errors, q_prev, p_root, q_root, momentum, weights, vec_grads, vec_momentum, vec_params,
):
    n_dp, n_t, n_s = sizes
    rows, width = errors.shape[2:]
    rank = q_prev.shape[2]
    vecs, entries = vec_params.shape[1:]
    n = n_dp * n_t
    chunks = HALVES * PARTS
    span = width // HALVES
    n_blocks = len(row_blocks(rows))
    big = (rows, width)
    vec = (vecs, 1, entries)
    packed = (packed_rows(rank, rows), LANES)
    chunk = (rank * USED // LANES, LANES)
    any_space = pl.BlockSpec(memory_space=pl.ANY)
    in_vmem = pl.BlockSpec(memory_space=pltpu.VMEM)
    dma = pltpu.SemaphoreType.DMA
    vmem = pltpu.VMEM
    args = (
        grads[0, 0],
        errors[0, 0],
        q_prev[0].T,
        p_root[0],
        q_root[0],
        momentum[0],
        weights[0],
        vec_grads[0, 0][:, None, :],
        vec_momentum[0][:, None, :],
        vec_params[0][:, None, :],
    )
    shapes = (big, (rank, rows), (rank, width), big, big, vec, vec)
    kept = tuple(vmem(shape, F32) for shape in shapes + ((1, LANES),)) + (
        vmem((rows, 3 * rank), BF16),
        vmem((rank, 3 * rank), BF16),
        vmem((rank, span), F32),
    )
    outs = pl.pallas_call(
        functools.partial(kernel, sizes),
        out_shape=kept,
        in_specs=[any_space] * 10,
        out_specs=(in_vmem,) * len(kept),
        scratch_shapes=[
            vmem(big, BF16),
            vmem((rank, width), F32),
            vmem((rank, rank), F32),
            vmem((rank, rank), F32),
            vmem(vec, F32),
            vmem((HALVES, rows, span), BF16),
            vmem((HALVES, rows, span), BF16),
            vmem((rows, span), BF16),
            vmem((rows, span), BF16),
            vmem((8, LANES), F32),
            vmem((n_dp,) + packed, F32),
            vmem((n_dp,) + vec, F32),
            vmem((packed_rows(rank, rank) + 8, LANES), F32),
            vmem((n_s, n_t, packed_rows(rank, rank) + 8, LANES), F32),
            vmem((PARTS,) + chunk, F32),
            vmem((n_s, n_t) + chunk, F32),
            vmem((chunks,) + chunk, F32),
            vmem((n_s, n) + chunk, F32),
            vmem((n_s,) + chunk, F32),
            vmem((chunks,) + chunk, F32),
            vmem((n * n_s, 1, LANES), F32),
            dma((9 + 2 * n_blocks,)),
            dma(()), dma(()), dma(()), dma(()),
            dma((PARTS,)), dma((n_s,)), dma((PARTS,)), dma((n_s,)),
            dma(()), dma((n_s,)), dma(()), dma((HALVES,)), dma(()), dma(()),
        ],
        compiler_params=pltpu.CompilerParams(
            collective_id=0, has_side_effects=True, vmem_limit_bytes=48 * 1024 * 1024
        ),
    )(*(pltpu.with_memory_space_constraint(arg, pltpu.HBM) for arg in args))
    outs = pl.pallas_call(
        functools.partial(finish, n_dp, n_s * (width * width + vecs * width)),
        out_shape=tuple(pltpu.HBM(shape, F32) for shape in shapes),
        in_specs=[in_vmem] * len(kept),
        out_specs=(any_space,) * 7,
        scratch_shapes=[
            vmem((rows, span), F32),
            vmem((rows, span), F32),
            vmem(big, F32),
            vmem((rank, span), F32),
            vmem(vec, F32),
            dma((7 + 4 * (span // LANES),)),
        ],
    )(*(pltpu.with_memory_space_constraint(out, pltpu.VMEM) for out in outs))
    errors_out, p_factor, q_factor, momentum_out, weights_out, vec_momentum_out, vec_params_out = outs
    return (
        errors_out[None, None],
        p_factor.T[None],
        q_factor.T[None],
        momentum_out[None],
        weights_out[None],
        vec_momentum_out[:, 0][None],
        vec_params_out[:, 0][None],
    )


def solution(mesh):
    sizes = (mesh.shape["dp"], mesh.shape["tensor"], mesh.shape["section"])
    in_specs = (
        P("dp", "section", "tensor", None),
        P("dp", "section", "tensor", None),
        P("section", None, None),
        P("section", None, None),
        P("section", None, None),
        P("section", "tensor", None),
        P("section", "tensor", None),
        P("dp", "section", None, "tensor"),
        P("section", None, "tensor"),
        P("section", None, "tensor"),
    )
    out_specs = (
        P("dp", "section", "tensor", None),
        P("section", "tensor", None),
        P("section", None, None),
        P("section", "tensor", None),
        P("section", "tensor", None),
        P("section", None, "tensor"),
        P("section", None, "tensor"),
    )
    return jax.shard_map(
        functools.partial(shards, sizes),
        mesh=mesh, in_specs=in_specs, out_specs=out_specs, check_vma=False,
    )
```

```python
import functools

import jax
import jax.numpy as jnp
from jax import lax
from jax.experimental import pallas as pl
from jax.experimental.pallas import tpu as pltpu
from jax.sharding import PartitionSpec as P

F32 = jnp.float32
BF16 = jnp.bfloat16
MESH = pl.DeviceIdType.MESH
LANES = 128
UNROLL = 32
HALVES = 2
PARTS = 4
USED = 96
PIECE = 32


def split(x):
    high = x.astype(BF16)
    return high, (x - high.astype(F32)).astype(BF16)


def mm(a, b, dims=((1,), (0,))):
    return lax.dot_general(a, b, (dims, ((), ())), preferred_element_type=F32)


def left_parts(x):
    high, low = split(x)
    return jnp.concatenate([high, high, low], axis=1)


def right_parts(x):
    high, low = split(x)
    return jnp.concatenate([high, low, high], axis=0)


def each(count, body):
    if count <= UNROLL:
        for i in range(count):
            body(i)
    else:
        lax.fori_loop(0, count, lambda i, c: (body(i), c)[1], 0)


def total_of(ref, count):
    if count <= UNROLL:
        total = ref[0]
        for i in range(1, count):
            total = total + ref[i]
        return total
    return lax.fori_loop(1, count, lambda i, acc: acc + ref[i], ref[0])


def row_blocks(rows):
    return [(r, min(LANES, rows - r)) for r in range(0, rows, LANES)]


def packed_rows(rank, rows):
    return rank * rows // LANES


def pack(part):
    rank, size = part.shape
    count = LANES // size
    step = rank // count
    return jnp.concatenate([part[i * step : (i + 1) * step] for i in range(count)], axis=1)


def unpack(x, rank, rows):
    parts = []
    for start, size in row_blocks(rows):
        count = LANES // size
        step = rank // count
        block = x[rank * start // LANES :][:step]
        parts.append(
            jnp.concatenate([block[:, i * size : (i + 1) * size] for i in range(count)], axis=0)
        )
    return jnp.concatenate(parts, axis=1)


def lanes_of(shape):
    return lax.broadcasted_iota(jnp.int32, shape, 1)


def chunks_of(x):
    tiles = [x[:, b * LANES : (b + 1) * LANES] for b in range(3)]
    lane = lanes_of((8, LANES))
    chunks = []
    for tile in tiles:
        tail = tile[24:]
        chunks.append(
            [
                jnp.where(lane < USED, tile[8 * p : 8 * p + 8], pltpu.roll(tail, USED - PIECE * p, 1))
                for p in range(3)
            ]
        )
    rest = last_columns(tiles)
    chunks.append(
        [jnp.where(lane < USED, rest[8 * p : 8 * p + 8], tiles[p][24:]) for p in range(3)]
    )
    return [jnp.concatenate(chunk, axis=0) for chunk in chunks]


def last_columns(tiles):
    lane = lanes_of(tiles[0].shape)
    rolled = [pltpu.roll(tile, PIECE * (b + 1), 1) for b, tile in enumerate(tiles)]
    return jnp.where(lane < PIECE, rolled[0], jnp.where(lane < 2 * PIECE, rolled[1], rolled[2]))


def chunk_tail(chunk):
    lane = lanes_of((8, LANES))
    rolled = [pltpu.roll(chunk[8 * p : 8 * p + 8], PIECE * (p + 1), 1) for p in range(3)]
    return jnp.where(lane < PIECE, rolled[0], jnp.where(lane < 2 * PIECE, rolled[1], rolled[2]))


def columns_of(chunks):
    lane = lanes_of((8, LANES))
    last = chunks[3]
    tiles = []
    for j in range(3):
        rows = [
            jnp.where(
                lane < USED,
                chunks[j][8 * p : 8 * p + 8],
                pltpu.roll(last[8 * p : 8 * p + 8], USED - PIECE * j, 1),
            )
            for p in range(3)
        ]
        rows.append(jnp.where(lane < USED, chunk_tail(chunks[j]), last[8 * j : 8 * j + 8]))
        tiles.append(jnp.concatenate(rows, axis=0))
    return jnp.concatenate(tiles, axis=1)


def near_half(n_dp):
    return jnp.where(2 * lax.axis_index("dp") < n_dp, 0, 1)


def kernel(
    sizes,
    g_hbm, e_hbm, qt_hbm, pr_hbm, qr_hbm, m_hbm, w_hbm, vg_hbm, vm_hbm, vp_hbm,
    e_v, pf_v, qf_v, m_v, w_v, vmo_v, vp_v, tot_v, left_v, qrt_v, qfar_v,
    g_v, qt_v, pr_v, qr_v, vm_v,
    hi_v, lo_v, mhi_v, mlo_v, msq_v, pbuf, vbuf, gsend, gbuf, wsend, wbuf, qpart, rbuf, qsum_v, qfull, tiles,
    in_sem, psend, precv, vsend, vrecv, gsend_sem, grecv, wsend_sem, wrecv,
    rsend, rrecv, asend, arecv, tsend, trecv,
):
    n_dp, n_t, n_s = sizes
    n = n_dp * n_t
    group = n_t * n_s
    dp, tn, sc = lax.axis_index("dp"), lax.axis_index("tensor"), lax.axis_index("section")
    me = dp * n_t + tn
    rank, width = qt_v.shape
    rows = e_v.shape[0]
    span = width // HALVES
    gram_rows = packed_rows(rank, rank)
    chunks = HALVES * PARTS
    first_plane = n_dp // 2 - 1
    plane = dp - first_plane
    keeper = n_s - 1
    mine = plane * PARTS + tn
    in_plane = jnp.logical_and(plane >= 0, plane < HALVES)
    owns = jnp.logical_and(jnp.logical_and(in_plane, tn < PARTS), sc == keeper)
    upper = 2 * dp < n_dp
    near = near_half(n_dp)
    far = 1 - near

    def load(i, src, dst):
        copy = pltpu.make_async_copy(src, dst, in_sem.at[i])
        copy.start()
        return copy

    blocks = row_blocks(rows)
    in_q = load(0, qt_hbm, qt_v)
    in_pr = load(1, pr_hbm, pr_v)
    in_g, in_e = [], []
    for b, (start, size) in enumerate(blocks):
        at = pl.ds(start, size)
        in_g.append(load(9 + 2 * b, g_hbm.at[at], g_v.at[at]))
        in_e.append(load(10 + 2 * b, e_hbm.at[at], e_v.at[at]))
    in_vg = load(2, vg_hbm, vbuf.at[dp])
    in_qr = load(3, qr_hbm, qr_v)
    in_vm = load(4, vm_hbm, vm_v)
    in_m = load(5, m_hbm, m_v)
    in_vp = load(6, vp_hbm, vp_v)
    in_w = load(7, w_hbm, w_v)

    barrier = pltpu.get_barrier_semaphore()
    slot = sc * n_t + tn

    def line_peer(i):
        up, down = n_dp - 1 - i, i
        return jnp.where(
            upper, jnp.where(up > dp, up, up - 1), jnp.where(down < dp, down, down + 1)
        )

    def greet_line(i):
        pl.semaphore_signal(
            barrier, inc=1, device_id=(line_peer(i), tn, sc), device_id_type=MESH
        )

    def greet_plane(i):
        peer = lax.rem(slot + 1 + i, group)
        pl.semaphore_signal(
            barrier, inc=1, device_id=(dp, lax.rem(peer, n_t), peer // n_t), device_id_type=MESH
        )

    each(n_dp - 1, greet_line)
    each(group - 1, greet_plane)

    in_q.wait()
    in_pr.wait()
    q_hi, q_lo = split(mm(left_parts(pr_v[...].T), right_parts(qt_v[...])))
    q_both = jnp.concatenate([q_hi, q_lo], axis=0)
    for b, (start, size) in enumerate(blocks):
        at = pl.ds(start, size)
        in_g[b].wait()
        in_e[b].wait()
        merged = g_v[at, :].astype(F32) + e_v[at, :]
        e_v[at, :] = merged
        m_hi, m_lo = split(merged)
        for p in range(HALVES):
            hi_v[p, at, :] = m_hi[:, p * span : (p + 1) * span]
            lo_v[p, at, :] = m_lo[:, p * span : (p + 1) * span]
        first = mm(q_both, m_hi, ((1,), (1,)))
        second = mm(q_hi, m_lo, ((1,), (1,)))
        pbuf[dp, pl.ds(rank * start // LANES, rank * size // LANES), :] = pack(
            first[:rank] + first[rank:] + second
        )

    pl.semaphore_wait(barrier, n_dp - 1 + group - 1)

    def send_p(i):
        pltpu.make_async_remote_copy(
            pbuf.at[dp], pbuf.at[dp], psend, precv,
            device_id=(line_peer(i), tn, sc), device_id_type=MESH,
        ).start()

    def send_v(i):
        pltpu.make_async_remote_copy(
            vbuf.at[dp], vbuf.at[dp], vsend, vrecv,
            device_id=(line_peer(i), tn, sc), device_id_type=MESH,
        ).start()

    each(n_dp - 1, send_p)
    in_vg.wait()
    each(n_dp - 1, send_v)

    in_m.wait()
    in_qr.wait()
    in_vm.wait()
    in_vp.wait()
    in_w.wait()
    q_root_left = left_parts(qr_v[...])
    q_root_t = left_parts(qr_v[...].T)
    qrt_v[...] = q_root_t

    old = m_v[:, pl.ds(pl.multiple_of(near * span, LANES), span)]
    m_hi, m_lo = split(old)
    mhi_v[...] = m_hi
    mlo_v[...] = m_lo
    old = 0.9 * old
    squares = jnp.zeros((8, LANES), F32)
    for c in range(span // LANES):
        tile = old[:, c * LANES : (c + 1) * LANES]
        squares = squares + jnp.sum((tile * tile).reshape(rows // 8, 8, LANES), axis=0)
    msq_v[...] = squares

    others = pl.ds(0, n_dp - 1)
    pltpu.make_async_copy(pbuf.at[others], pbuf.at[others], precv).wait()
    pf = unpack(total_of(pbuf, n_dp), rank, rows)
    pf_hi, pf_lo = split(pf)
    pf_both = jnp.concatenate([pf_hi, pf_lo], axis=0)

    def q_parts(p):
        first = mm(pf_both, hi_v[p])
        second = mm(pf_hi, lo_v[p])
        return chunks_of(first[:rank] + first[rank:] + second)

    def send_q(k, owner_dp, j):
        pltpu.make_async_remote_copy(
            qpart.at[k], rbuf.at[sc, me], rsend, rrecv.at[sc],
            device_id=(owner_dp, j, keeper), device_id_type=MESH,
        ).start()

    parts = q_parts(far)
    for j in range(PARTS):
        qpart[far * PARTS + j] = parts[j]
    left_t = mm(q_root_left, right_parts(pf)) / n_dp
    largest = jnp.max(jnp.max(jnp.abs(left_t), axis=1, keepdims=True), axis=0, keepdims=True)
    unit = left_t / jnp.where(largest > 0, largest, 1.0)
    u_hi, u_lo = split(unit)
    for j in range(PARTS):
        send_q(far * PARTS + j, first_plane + far, j)

    parts = q_parts(near)
    first = mm(jnp.concatenate([u_hi, u_lo], axis=0), mhi_v[...])
    second = mm(u_hi, mlo_v[...])
    product = first[:rank] + first[rank:] + second
    products = chunks_of(product)
    gram = mm(left_parts(unit), jnp.concatenate([u_hi, u_lo, u_hi], axis=1), ((1,), (1,)))
    gsend[0:gram_rows, :] = pack(gram)
    for j in range(PARTS):
        qpart[near * PARTS + j] = parts[j]
        wsend[j] = products[j]
    def give_product(j):
        return pltpu.make_async_remote_copy(
            wsend.at[j], wbuf.at[sc, tn], wsend_sem.at[j], wrecv.at[sc],
            device_id=(dp, j, keeper), device_id_type=MESH,
        )

    def give_gram(j):
        return pltpu.make_async_remote_copy(
            gsend, gbuf.at[sc, tn], gsend_sem.at[j], grecv.at[sc],
            device_id=(dp, j, keeper), device_id_type=MESH,
        )

    def stays(j):
        return jnp.logical_and(tn == j, sc == keeper)

    @pl.when(in_plane)
    def _():
        for j in range(PARTS):

            @pl.when(stays(j))
            def _():
                wbuf[keeper, tn] = wsend[j]

            @pl.when(jnp.logical_not(stays(j)))
            def _():
                give_product(j).start()

        pltpu.make_async_copy(vbuf.at[others], vbuf.at[others], vrecv).wait()
        v_new = 0.9 * vm_v[...] + total_of(vbuf, n_dp) / n_dp
        v_row = jnp.sum(v_new * v_new, axis=0)
        v_squares = jnp.zeros((1, LANES), F32)
        for start, size in row_blocks(v_row.shape[1]):
            piece = v_row[:, start : start + size]
            if size < LANES:
                piece = jnp.concatenate([piece, jnp.zeros((1, LANES - size), F32)], axis=1)
            v_squares = v_squares + piece
        squares = jnp.sum(msq_v[...], axis=0, keepdims=True)
        squares = squares + jnp.where(plane == 0, v_squares, 0.0)
        row = lax.broadcasted_iota(jnp.int32, (8, LANES), 0)
        gsend[gram_rows:, :] = jnp.where(row == 0, largest, squares)

        @pl.when(owns)
        def _():
            gbuf[keeper, tn] = gsend[...]

        for j in range(PARTS):

            @pl.when(jnp.logical_not(stays(j)))
            def _():
                give_gram(j).start()

    for j in range(PARTS):
        here = jnp.logical_and(owns, tn == j)

        @pl.when(here)
        def _():
            rbuf[keeper, me] = qpart[near * PARTS + j]

        @pl.when(jnp.logical_not(here))
        def _():
            send_q(near * PARTS + j, first_plane + near, j)

    @pl.when(jnp.logical_not(in_plane))
    def _():
        pltpu.make_async_copy(vbuf.at[others], vbuf.at[others], vrecv).wait()

    pf_v[...] = pf
    left_v[...] = left_parts(left_t.T)
    vmo_v[...] = 0.9 * vm_v[...] + total_of(vbuf, n_dp) / n_dp

    @pl.when(owns)
    def _():
        used = lanes_of((rank, LANES)) < USED

        def prepare(s):
            rest = pl.ds(0, n_t - 1 if s == keeper else n_t)
            pltpu.make_async_copy(wbuf.at[s, rest], wbuf.at[s, rest], wrecv.at[s]).wait()
            pltpu.make_async_copy(gbuf.at[s, rest], gbuf.at[s, rest], grecv.at[s]).wait()
            levels = [gbuf[s, t, gram_rows : gram_rows + 1, :] for t in range(n_t)]
            level = levels[0]
            for t in range(1, n_t):
                level = jnp.maximum(level, levels[t])
            inverse = 1.0 / jnp.where(level > 0, level, 1.0)
            product = jnp.zeros((rank * USED // LANES, LANES), F32)
            gram = jnp.zeros((gram_rows, LANES), F32)
            for t in range(n_t):
                share = levels[t] * inverse
                product = product + share * wbuf[s, t]
                gram = gram + share * share * gbuf[s, t, 0:gram_rows, :]
            product = jnp.concatenate([product, chunk_tail(product)], axis=0)
            product = jnp.where(used, 1.8 * product, 0.0)
            gram = left_parts(unpack(gram, rank, rank))
            return product, gram, level, gbuf[s, tn, gram_rows + 1 : gram_rows + 2, :]

        def row_of(q_sum, prepared):
            product, gram, level, squares = prepared
            scaled = jnp.concatenate([q_sum, chunk_tail(q_sum)], axis=0) * level
            scaled = jnp.where(used, scaled, 0.0)
            terms = scaled * (product + mm(gram, right_parts(scaled)))
            return jnp.sum(terms, axis=0, keepdims=True) + squares

        def summed(s):
            whole = pl.ds(0, n - 1 if s == keeper else n)
            pltpu.make_async_copy(rbuf.at[s, whole], rbuf.at[s, whole], rrecv.at[s]).wait()
            q_sum = total_of(rbuf.at[s], n)
            qsum_v[s] = q_sum
            return q_sum

        def send_sum(s, i):
            peer = i + jnp.where(i >= me, 1, 0) if s == keeper else i
            pltpu.make_async_remote_copy(
                qsum_v.at[s], qfull.at[mine], asend, arecv.at[plane],
                device_id=(peer // n_t, lax.rem(peer, n_t), s), device_id_type=MESH,
            ).start()

        def send_row(i):
            peer = i + jnp.where(i >= me * n_s + sc, 1, 0)
            pltpu.make_async_remote_copy(
                tiles.at[mine], tiles.at[mine], tsend, trecv,
                device_id=(peer // group, lax.rem(peer // n_s, n_t), lax.rem(peer, n_s)),
                device_id_type=MESH,
            ).start()

        q_sum = summed(keeper)
        qfull[mine] = q_sum
        each(n - 1, lambda i: send_sum(keeper, i))
        row = row_of(q_sum, prepare(keeper))
        for s in range(keeper):
            prepared = prepare(s)
            q_sum = summed(s)
            send_sum(s, 0)
            row = row + row_of(q_sum, prepared)
            if s < keeper - 1:
                each(n - 1, lambda i: send_sum(s, 1 + i))
        tiles[mine] = row
        each(n * n_s - 1, send_row)
        each(n - 1, lambda i: send_sum(keeper - 1, 1 + i))

    pltpu.make_async_copy(pbuf.at[others], pbuf.at[others], psend).wait()
    pltpu.make_async_copy(vbuf.at[others], vbuf.at[others], vsend).wait()

    @pl.when(in_plane)
    def _():
        for j in range(PARTS):

            @pl.when(jnp.logical_not(stays(j)))
            def _():
                give_product(j).wait_send()
                give_gram(j).wait_send()

    @pl.when(owns)
    def _():
        got = pl.ds(0, chunks - 1)
        pltpu.make_async_copy(qfull.at[got], qfull.at[got], rsend).wait()

    @pl.when(jnp.logical_not(owns))
    def _():
        pltpu.make_async_copy(qfull, qfull, rsend).wait()

    @pl.when(owns)
    def _():
        got = pl.ds(0, PARTS - 1)
        pltpu.make_async_copy(qfull.at[got], qfull.at[got], arecv.at[near]).wait()

    @pl.when(jnp.logical_not(owns))
    def _():
        got = pl.ds(0, PARTS)
        pltpu.make_async_copy(qfull.at[got], qfull.at[got], arecv.at[near]).wait()

    right = right_parts(columns_of([qfull[near * PARTS + j] for j in range(PARTS)]))
    approx = mm(left_v[...], right)
    cols = pl.ds(pl.multiple_of(near * span, LANES), span)
    m_v[:, cols] = 0.9 * m_v[:, cols] + approx
    e_v[:, cols] = e_v[:, cols] - approx
    qf_v[:, cols] = mm(q_root_t, right)

    got = pl.ds(0, PARTS)
    pltpu.make_async_copy(qfull.at[got], qfull.at[got], arecv.at[far]).wait()
    qfar_v[...] = columns_of([qfull[far * PARTS + j] for j in range(PARTS)])

    count = chunks

    @pl.when(owns)
    def _():
        got = pl.ds(0, count - 1)
        pltpu.make_async_copy(tiles.at[got], tiles.at[got], trecv).wait()

    @pl.when(jnp.logical_not(owns))
    def _():
        got = pl.ds(0, count)
        pltpu.make_async_copy(tiles.at[got], tiles.at[got], trecv).wait()

    tot_v[...] = total_of(tiles, count)

    @pl.when(owns)
    def _():
        for s in range(n_s):
            whole = pl.ds(0, n - 1 if s == keeper else n)
            pltpu.make_async_copy(rbuf.at[s, whole], rbuf.at[s, whole], asend).wait()
        sent = tiles.at[pl.ds(0, n * n_s - 1)]
        pltpu.make_async_copy(sent, sent, tsend).wait()


def finish(
    n_dp, entries,
    e_v, pf_v, qf_v, m_v, w_v, vmo_v, vp_v, tot_v, left_v, qrt_v, qfar_v,
    eo_hbm, pf_hbm, qf_hbm, mo_hbm, wo_hbm, vmo_hbm, vpo_hbm,
    eo_v, mo_v, wo_v, qff_v, vpo_v, sems,
):
    copies = []
    span = qfar_v.shape[1]
    near = pl.multiple_of(near_half(n_dp) * span, LANES)
    far = pl.multiple_of(span - near, LANES)
    cols = pl.ds(near, span)

    def write(src, dst):
        copy = pltpu.make_async_copy(src, dst, sems.at[len(copies)])
        copy.start()
        copies.append(copy)

    write(e_v.at[:, cols], eo_hbm.at[:, cols])
    write(m_v.at[:, cols], mo_hbm.at[:, cols])
    write(qf_v.at[:, cols], qf_hbm.at[:, cols])
    write(pf_v, pf_hbm)
    write(vmo_v, vmo_hbm)
    total = jnp.maximum(jnp.sum(tot_v[...], axis=1, keepdims=True), 0.0)
    scale = 0.05 / jnp.sqrt(total / entries + 1e-06)
    for c in range(span // LANES):
        here = pl.ds(c * LANES, LANES)
        cols = pl.ds(pl.multiple_of(far + c * LANES, LANES), LANES)
        right = right_parts(qfar_v[:, here])
        approx = mm(left_v[...], right)
        new = 0.9 * m_v[:, cols] + approx
        eo_v[:, here] = e_v[:, cols] - approx
        write(eo_v.at[:, here], eo_hbm.at[:, cols])
        mo_v[:, here] = new
        write(mo_v.at[:, here], mo_hbm.at[:, cols])
        wo_v[:, cols] = w_v[:, cols] - scale * new
        write(wo_v.at[:, cols], wo_hbm.at[:, cols])
        qff_v[:, here] = mm(qrt_v[...], right)
        write(qff_v.at[:, here], qf_hbm.at[:, cols])
    cols = pl.ds(near, span)
    wo_v[:, cols] = w_v[:, cols] - scale * m_v[:, cols]
    write(wo_v.at[:, cols], wo_hbm.at[:, cols])
    vpo_v[...] = vp_v[...] - scale.reshape(1, 1, 1) * vmo_v[...]
    write(vpo_v, vpo_hbm)
    for copy in copies:
        copy.wait()


def shards(
    sizes,
    grads, errors, q_prev, p_root, q_root, momentum, weights, vec_grads, vec_momentum, vec_params,
):
    n_dp, n_t, n_s = sizes
    rows, width = errors.shape[2:]
    rank = q_prev.shape[2]
    vecs, entries = vec_params.shape[1:]
    n = n_dp * n_t
    chunks = HALVES * PARTS
    span = width // HALVES
    n_blocks = len(row_blocks(rows))
    big = (rows, width)
    vec = (vecs, 1, entries)
    packed = (packed_rows(rank, rows), LANES)
    chunk = (rank * USED // LANES, LANES)
    any_space = pl.BlockSpec(memory_space=pl.ANY)
    in_vmem = pl.BlockSpec(memory_space=pltpu.VMEM)
    dma = pltpu.SemaphoreType.DMA
    vmem = pltpu.VMEM
    args = (
        grads[0, 0],
        errors[0, 0],
        q_prev[0].T,
        p_root[0],
        q_root[0],
        momentum[0],
        weights[0],
        vec_grads[0, 0][:, None, :],
        vec_momentum[0][:, None, :],
        vec_params[0][:, None, :],
    )
    shapes = (big, (rank, rows), (rank, width), big, big, vec, vec)
    kept = tuple(vmem(shape, F32) for shape in shapes + ((1, LANES),)) + (
        vmem((rows, 3 * rank), BF16),
        vmem((rank, 3 * rank), BF16),
        vmem((rank, span), F32),
    )
    outs = pl.pallas_call(
        functools.partial(kernel, sizes),
        out_shape=kept,
        in_specs=[any_space] * 10,
        out_specs=(in_vmem,) * len(kept),
        scratch_shapes=[
            vmem(big, BF16),
            vmem((rank, width), F32),
            vmem((rank, rank), F32),
            vmem((rank, rank), F32),
            vmem(vec, F32),
            vmem((HALVES, rows, span), BF16),
            vmem((HALVES, rows, span), BF16),
            vmem((rows, span), BF16),
            vmem((rows, span), BF16),
            vmem((8, LANES), F32),
            vmem((n_dp,) + packed, F32),
            vmem((n_dp,) + vec, F32),
            vmem((packed_rows(rank, rank) + 8, LANES), F32),
            vmem((n_s, n_t, packed_rows(rank, rank) + 8, LANES), F32),
            vmem((PARTS,) + chunk, F32),
            vmem((n_s, n_t) + chunk, F32),
            vmem((chunks,) + chunk, F32),
            vmem((n_s, n) + chunk, F32),
            vmem((n_s,) + chunk, F32),
            vmem((chunks,) + chunk, F32),
            vmem((n * n_s, 1, LANES), F32),
            dma((9 + 2 * n_blocks,)),
            dma(()), dma(()), dma(()), dma(()),
            dma((PARTS,)), dma((n_s,)), dma((PARTS,)), dma((n_s,)),
            dma(()), dma((n_s,)), dma(()), dma((HALVES,)), dma(()), dma(()),
        ],
        compiler_params=pltpu.CompilerParams(
            collective_id=0, has_side_effects=True, vmem_limit_bytes=48 * 1024 * 1024
        ),
    )(*(pltpu.with_memory_space_constraint(arg, pltpu.HBM) for arg in args))
    outs = pl.pallas_call(
        functools.partial(finish, n_dp, n_s * (width * width + vecs * width)),
        out_shape=tuple(pltpu.HBM(shape, F32) for shape in shapes),
        in_specs=[in_vmem] * len(kept),
        out_specs=(any_space,) * 7,
        scratch_shapes=[
            vmem((rows, span), F32),
            vmem((rows, span), F32),
            vmem(big, F32),
            vmem((rank, span), F32),
            vmem(vec, F32),
            dma((7 + 4 * (span // LANES),)),
        ],
    )(*(pltpu.with_memory_space_constraint(out, pltpu.VMEM) for out in outs))
    errors_out, p_factor, q_factor, momentum_out, weights_out, vec_momentum_out, vec_params_out = outs
    return (
        errors_out[None, None],
        p_factor.T[None],
        q_factor.T[None],
        momentum_out[None],
        weights_out[None],
        vec_momentum_out[:, 0][None],
        vec_params_out[:, 0][None],
    )


def solution(mesh):
    sizes = (mesh.shape["dp"], mesh.shape["tensor"], mesh.shape["section"])
    in_specs = (
        P("dp", "section", "tensor", None),
        P("dp", "section", "tensor", None),
        P("section", None, None),
        P("section", None, None),
        P("section", None, None),
        P("section", "tensor", None),
        P("section", "tensor", None),
        P("dp", "section", None, "tensor"),
        P("section", None, "tensor"),
        P("section", None, "tensor"),
    )
    out_specs = (
        P("dp", "section", "tensor", None),
        P("section", "tensor", None),
        P("section", None, None),
        P("section", "tensor", None),
        P("section", "tensor", None),
        P("section", None, "tensor"),
        P("section", None, "tensor"),
    )
    return jax.shard_map(
        functools.partial(shards, sizes),
        mesh=mesh, in_specs=in_specs, out_specs=out_specs, check_vma=False,
    )
```

```python
import functools

import jax
import jax.numpy as jnp
from jax import lax
from jax.experimental import pallas as pl
from jax.experimental.pallas import tpu as pltpu
from jax.sharding import PartitionSpec as P

F32 = jnp.float32
BF16 = jnp.bfloat16
MESH = pl.DeviceIdType.MESH
LANES = 128
UNROLL = 32
HALVES = 2
PARTS = 4
USED = 96
PIECE = 32


def split(x):
    high = x.astype(BF16)
    return high, (x - high.astype(F32)).astype(BF16)


def mm(a, b, dims=((1,), (0,))):
    return lax.dot_general(a, b, (dims, ((), ())), preferred_element_type=F32)


def left_parts(x):
    high, low = split(x)
    return jnp.concatenate([high, high, low], axis=1)


def right_parts(x):
    high, low = split(x)
    return jnp.concatenate([high, low, high], axis=0)


def each(count, body):
    if count <= UNROLL:
        for i in range(count):
            body(i)
    else:
        lax.fori_loop(0, count, lambda i, c: (body(i), c)[1], 0)


def total_of(ref, count):
    if count <= UNROLL:
        total = ref[0]
        for i in range(1, count):
            total = total + ref[i]
        return total
    return lax.fori_loop(1, count, lambda i, acc: acc + ref[i], ref[0])


def row_blocks(rows):
    return [(r, min(LANES, rows - r)) for r in range(0, rows, LANES)]


def packed_rows(rank, rows):
    return rank * rows // LANES


def pack(part):
    rank, size = part.shape
    count = LANES // size
    step = rank // count
    return jnp.concatenate([part[i * step : (i + 1) * step] for i in range(count)], axis=1)


def unpack(x, rank, rows):
    parts = []
    for start, size in row_blocks(rows):
        count = LANES // size
        step = rank // count
        block = x[rank * start // LANES :][:step]
        parts.append(
            jnp.concatenate([block[:, i * size : (i + 1) * size] for i in range(count)], axis=0)
        )
    return jnp.concatenate(parts, axis=1)


def lanes_of(shape):
    return lax.broadcasted_iota(jnp.int32, shape, 1)


def chunks_of(x):
    tiles = [x[:, b * LANES : (b + 1) * LANES] for b in range(3)]
    lane = lanes_of((8, LANES))
    chunks = []
    for tile in tiles:
        tail = tile[24:]
        chunks.append(
            [
                jnp.where(lane < USED, tile[8 * p : 8 * p + 8], pltpu.roll(tail, USED - PIECE * p, 1))
                for p in range(3)
            ]
        )
    rest = last_columns(tiles)
    chunks.append(
        [jnp.where(lane < USED, rest[8 * p : 8 * p + 8], tiles[p][24:]) for p in range(3)]
    )
    return [jnp.concatenate(chunk, axis=0) for chunk in chunks]


def last_columns(tiles):
    lane = lanes_of(tiles[0].shape)
    rolled = [pltpu.roll(tile, PIECE * (b + 1), 1) for b, tile in enumerate(tiles)]
    return jnp.where(lane < PIECE, rolled[0], jnp.where(lane < 2 * PIECE, rolled[1], rolled[2]))


def chunk_tail(chunk):
    lane = lanes_of((8, LANES))
    rolled = [pltpu.roll(chunk[8 * p : 8 * p + 8], PIECE * (p + 1), 1) for p in range(3)]
    return jnp.where(lane < PIECE, rolled[0], jnp.where(lane < 2 * PIECE, rolled[1], rolled[2]))


def columns_of(chunks):
    lane = lanes_of((8, LANES))
    last = chunks[3]
    tiles = []
    for j in range(3):
        rows = [
            jnp.where(
                lane < USED,
                chunks[j][8 * p : 8 * p + 8],
                pltpu.roll(last[8 * p : 8 * p + 8], USED - PIECE * j, 1),
            )
            for p in range(3)
        ]
        rows.append(jnp.where(lane < USED, chunk_tail(chunks[j]), last[8 * j : 8 * j + 8]))
        tiles.append(jnp.concatenate(rows, axis=0))
    return jnp.concatenate(tiles, axis=1)


def near_half(n_dp):
    return jnp.where(2 * lax.axis_index("dp") < n_dp, 0, 1)


def kernel(
    sizes,
    g_hbm, e_hbm, qt_hbm, pr_hbm, qr_hbm, m_hbm, w_hbm, vg_hbm, vm_hbm, vp_hbm,
    e_v, pf_v, qf_v, m_v, w_v, vmo_v, vp_v, tot_v, left_v, qrt_v, qfar_v,
    g_v, qt_v, pr_v, qr_v, vm_v,
    hi_v, lo_v, mhi_v, mlo_v, msq_v, pbuf, vbuf, gsend, gbuf, wsend, wbuf, qpart, rbuf, qsum_v, qfull, tiles,
    in_sem, psend, precv, vsend, vrecv, gsend_sem, grecv, wsend_sem, wrecv,
    rsend, rrecv, asend, arecv, tsend, trecv,
):
    n_dp, n_t, n_s = sizes
    n = n_dp * n_t
    group = n_t * n_s
    dp, tn, sc = lax.axis_index("dp"), lax.axis_index("tensor"), lax.axis_index("section")
    me = dp * n_t + tn
    rank, width = qt_v.shape
    rows = e_v.shape[0]
    span = width // HALVES
    gram_rows = packed_rows(rank, rank)
    chunks = HALVES * PARTS
    first_plane = n_dp // 2 - 1
    plane = dp - first_plane
    keeper = n_s - 1
    final = HALVES * PARTS - 1
    corner = jnp.logical_and(dp == 0, tn == 0)
    mine = jnp.where(corner, final, plane * PARTS + tn)
    in_plane = jnp.logical_and(plane >= 0, plane < HALVES)
    regular = jnp.logical_and(jnp.logical_and(in_plane, tn < PARTS), mine < final)
    owns = jnp.logical_and(jnp.logical_or(regular, corner), sc == keeper)
    upper = 2 * dp < n_dp
    near = near_half(n_dp)
    far = 1 - near

    def load(i, src, dst):
        copy = pltpu.make_async_copy(src, dst, in_sem.at[i])
        copy.start()
        return copy

    blocks = row_blocks(rows)
    in_q = load(0, qt_hbm, qt_v)
    in_pr = load(1, pr_hbm, pr_v)
    in_g, in_e = [], []
    for b, (start, size) in enumerate(blocks):
        at = pl.ds(start, size)
        in_g.append(load(9 + 2 * b, g_hbm.at[at], g_v.at[at]))
        in_e.append(load(10 + 2 * b, e_hbm.at[at], e_v.at[at]))
    in_vg = load(2, vg_hbm, vbuf.at[dp])
    in_qr = load(3, qr_hbm, qr_v)
    in_vm = load(4, vm_hbm, vm_v)
    in_m = load(5, m_hbm, m_v)
    in_vp = load(6, vp_hbm, vp_v)
    in_w = load(7, w_hbm, w_v)

    barrier = pltpu.get_barrier_semaphore()
    slot = sc * n_t + tn

    def line_peer(i):
        up, down = n_dp - 1 - i, i
        return jnp.where(
            upper, jnp.where(up > dp, up, up - 1), jnp.where(down < dp, down, down + 1)
        )

    def greet_line(i):
        pl.semaphore_signal(
            barrier, inc=1, device_id=(line_peer(i), tn, sc), device_id_type=MESH
        )

    def greet_plane(i):
        peer = lax.rem(slot + 1 + i, group)
        pl.semaphore_signal(
            barrier, inc=1, device_id=(dp, lax.rem(peer, n_t), peer // n_t), device_id_type=MESH
        )

    each(n_dp - 1, greet_line)
    each(group - 1, greet_plane)

    in_q.wait()
    in_pr.wait()
    q_hi, q_lo = split(mm(left_parts(pr_v[...].T), right_parts(qt_v[...])))
    q_both = jnp.concatenate([q_hi, q_lo], axis=0)
    for b, (start, size) in enumerate(blocks):
        at = pl.ds(start, size)
        in_g[b].wait()
        in_e[b].wait()
        merged = g_v[at, :].astype(F32) + e_v[at, :]
        e_v[at, :] = merged
        m_hi, m_lo = split(merged)
        for p in range(HALVES):
            hi_v[p, at, :] = m_hi[:, p * span : (p + 1) * span]
            lo_v[p, at, :] = m_lo[:, p * span : (p + 1) * span]
        first = mm(q_both, m_hi, ((1,), (1,)))
        second = mm(q_hi, m_lo, ((1,), (1,)))
        pbuf[dp, pl.ds(rank * start // LANES, rank * size // LANES), :] = pack(
            first[:rank] + first[rank:] + second
        )

    pl.semaphore_wait(barrier, n_dp - 1 + group - 1)

    def send_p(i):
        pltpu.make_async_remote_copy(
            pbuf.at[dp], pbuf.at[dp], psend, precv,
            device_id=(line_peer(i), tn, sc), device_id_type=MESH,
        ).start()

    def send_v(i):
        pltpu.make_async_remote_copy(
            vbuf.at[dp], vbuf.at[dp], vsend, vrecv,
            device_id=(line_peer(i), tn, sc), device_id_type=MESH,
        ).start()

    each(n_dp - 1, send_p)
    in_vg.wait()
    each(n_dp - 1, send_v)

    in_m.wait()
    in_qr.wait()
    in_vm.wait()
    in_vp.wait()
    in_w.wait()
    q_root_left = left_parts(qr_v[...])
    q_root_t = left_parts(qr_v[...].T)
    qrt_v[...] = q_root_t

    old = m_v[:, pl.ds(pl.multiple_of(near * span, LANES), span)]
    m_hi, m_lo = split(old)
    mhi_v[...] = m_hi
    mlo_v[...] = m_lo
    old = 0.9 * old
    squares = jnp.zeros((8, LANES), F32)
    for c in range(span // LANES):
        tile = old[:, c * LANES : (c + 1) * LANES]
        squares = squares + jnp.sum((tile * tile).reshape(rows // 8, 8, LANES), axis=0)
    msq_v[...] = squares

    others = pl.ds(0, n_dp - 1)
    pltpu.make_async_copy(pbuf.at[others], pbuf.at[others], precv).wait()
    pf = unpack(total_of(pbuf, n_dp), rank, rows)
    pf_hi, pf_lo = split(pf)
    pf_both = jnp.concatenate([pf_hi, pf_lo], axis=0)

    def q_parts(p):
        first = mm(pf_both, hi_v[p])
        second = mm(pf_hi, lo_v[p])
        return chunks_of(first[:rank] + first[rank:] + second)

    def owner(half, j):
        if j < PARTS - 1:
            return first_plane + half, j, keeper
        moved = half == HALVES - 1
        return jnp.where(moved, 0, first_plane + half), jnp.where(moved, 0, j), keeper

    def send_q(half, j):
        k = half * PARTS + j
        here = jnp.logical_and(owns, mine == k)

        @pl.when(here)
        def _():
            rbuf[keeper, me] = qpart[k]

        @pl.when(jnp.logical_not(here))
        def _():
            pltpu.make_async_remote_copy(
                qpart.at[k], rbuf.at[sc, me], rsend, rrecv.at[sc],
                device_id=owner(half, j), device_id_type=MESH,
            ).start()

    parts = q_parts(far)
    for j in range(PARTS):
        qpart[far * PARTS + j] = parts[j]
    left_t = mm(q_root_left, right_parts(pf)) / n_dp
    largest = jnp.max(jnp.max(jnp.abs(left_t), axis=1, keepdims=True), axis=0, keepdims=True)
    unit = left_t / jnp.where(largest > 0, largest, 1.0)
    u_hi, u_lo = split(unit)
    for j in range(PARTS):
        send_q(far, j)

    parts = q_parts(near)
    first = mm(jnp.concatenate([u_hi, u_lo], axis=0), mhi_v[...])
    second = mm(u_hi, mlo_v[...])
    product = first[:rank] + first[rank:] + second
    products = chunks_of(product)
    gram = mm(left_parts(unit), jnp.concatenate([u_hi, u_lo, u_hi], axis=1), ((1,), (1,)))
    gsend[0:gram_rows, :] = pack(gram)
    for j in range(PARTS):
        qpart[near * PARTS + j] = parts[j]
        wsend[j] = products[j]
    def give_product(j):
        return pltpu.make_async_remote_copy(
            wsend.at[j], wbuf.at[sc, tn], wsend_sem.at[j], wrecv.at[sc],
            device_id=owner(plane, j), device_id_type=MESH,
        )

    def give_gram(j):
        return pltpu.make_async_remote_copy(
            gsend, gbuf.at[sc, tn], gsend_sem.at[j], grecv.at[sc],
            device_id=owner(plane, j), device_id_type=MESH,
        )

    def stays(j):
        return jnp.logical_and(owns, tn == j)

    @pl.when(in_plane)
    def _():
        for j in range(PARTS):

            @pl.when(stays(j))
            def _():
                wbuf[keeper, tn] = wsend[j]

            @pl.when(jnp.logical_not(stays(j)))
            def _():
                give_product(j).start()

        pltpu.make_async_copy(vbuf.at[others], vbuf.at[others], vrecv).wait()
        v_new = 0.9 * vm_v[...] + total_of(vbuf, n_dp) / n_dp
        v_row = jnp.sum(v_new * v_new, axis=0)
        v_squares = jnp.zeros((1, LANES), F32)
        for start, size in row_blocks(v_row.shape[1]):
            piece = v_row[:, start : start + size]
            if size < LANES:
                piece = jnp.concatenate([piece, jnp.zeros((1, LANES - size), F32)], axis=1)
            v_squares = v_squares + piece
        squares = jnp.sum(msq_v[...], axis=0, keepdims=True)
        squares = squares + jnp.where(plane == 0, v_squares, 0.0)
        row = lax.broadcasted_iota(jnp.int32, (8, LANES), 0)
        gsend[gram_rows:, :] = jnp.where(row == 0, largest, squares)

        @pl.when(owns)
        def _():
            gbuf[keeper, tn] = gsend[...]

        for j in range(PARTS):

            @pl.when(jnp.logical_not(stays(j)))
            def _():
                give_gram(j).start()

    for j in range(PARTS):
        send_q(near, j)

    @pl.when(jnp.logical_not(in_plane))
    def _():
        pltpu.make_async_copy(vbuf.at[others], vbuf.at[others], vrecv).wait()

    pf_v[...] = pf
    left_v[...] = left_parts(left_t.T)
    vmo_v[...] = 0.9 * vm_v[...] + total_of(vbuf, n_dp) / n_dp

    @pl.when(owns)
    def _():
        used = lanes_of((rank, LANES)) < USED

        def prepare(s):
            def arrived(count):
                rest = pl.ds(0, count)
                pltpu.make_async_copy(wbuf.at[s, rest], wbuf.at[s, rest], wrecv.at[s]).wait()
                pltpu.make_async_copy(gbuf.at[s, rest], gbuf.at[s, rest], grecv.at[s]).wait()

            if s == keeper:
                pl.when(corner)(lambda: arrived(n_t))
                pl.when(jnp.logical_not(corner))(lambda: arrived(n_t - 1))
            else:
                arrived(n_t)
            levels = [gbuf[s, t, gram_rows : gram_rows + 1, :] for t in range(n_t)]
            level = levels[0]
            for t in range(1, n_t):
                level = jnp.maximum(level, levels[t])
            inverse = 1.0 / jnp.where(level > 0, level, 1.0)
            product = jnp.zeros((rank * USED // LANES, LANES), F32)
            gram = jnp.zeros((gram_rows, LANES), F32)
            for t in range(n_t):
                share = levels[t] * inverse
                product = product + share * wbuf[s, t]
                gram = gram + share * share * gbuf[s, t, 0:gram_rows, :]
            product = jnp.concatenate([product, chunk_tail(product)], axis=0)
            product = jnp.where(used, 1.8 * product, 0.0)
            gram = left_parts(unpack(gram, rank, rank))
            return product, gram, level, gbuf[s, lax.rem(mine, PARTS), gram_rows + 1 : gram_rows + 2, :]

        def row_of(q_sum, prepared):
            product, gram, level, squares = prepared
            scaled = jnp.concatenate([q_sum, chunk_tail(q_sum)], axis=0) * level
            scaled = jnp.where(used, scaled, 0.0)
            terms = scaled * (product + mm(gram, right_parts(scaled)))
            return jnp.sum(terms, axis=0, keepdims=True) + squares

        def summed(s):
            whole = pl.ds(0, n - 1 if s == keeper else n)
            pltpu.make_async_copy(rbuf.at[s, whole], rbuf.at[s, whole], rrecv.at[s]).wait()
            q_sum = total_of(rbuf.at[s], n)
            qsum_v[s] = q_sum
            return q_sum

        def send_sum(s, i):
            peer = i + jnp.where(i >= me, 1, 0) if s == keeper else i
            pltpu.make_async_remote_copy(
                qsum_v.at[s], qfull.at[mine], asend, arecv.at[mine // PARTS],
                device_id=(peer // n_t, lax.rem(peer, n_t), s), device_id_type=MESH,
            ).start()

        def send_row(i):
            peer = i + jnp.where(i >= me * n_s + sc, 1, 0)
            pltpu.make_async_remote_copy(
                tiles.at[mine], tiles.at[mine], tsend, trecv,
                device_id=(peer // group, lax.rem(peer // n_s, n_t), lax.rem(peer, n_s)),
                device_id_type=MESH,
            ).start()

        q_sum = summed(keeper)
        qfull[mine] = q_sum
        each(n - 1, lambda i: send_sum(keeper, i))
        row = row_of(q_sum, prepare(keeper))
        for s in range(keeper):
            prepared = prepare(s)
            q_sum = summed(s)
            send_sum(s, 0)
            row = row + row_of(q_sum, prepared)
            if s < keeper - 1:
                each(n - 1, lambda i: send_sum(s, 1 + i))
        tiles[mine] = row
        each(n * n_s - 1, send_row)
        each(n - 1, lambda i: send_sum(keeper - 1, 1 + i))

    pltpu.make_async_copy(pbuf.at[others], pbuf.at[others], psend).wait()
    pltpu.make_async_copy(vbuf.at[others], vbuf.at[others], vsend).wait()

    @pl.when(in_plane)
    def _():
        for j in range(PARTS):

            @pl.when(jnp.logical_not(stays(j)))
            def _():
                give_product(j).wait_send()
                give_gram(j).wait_send()

    @pl.when(owns)
    def _():
        got = pl.ds(0, chunks - 1)
        pltpu.make_async_copy(qfull.at[got], qfull.at[got], rsend).wait()

    @pl.when(jnp.logical_not(owns))
    def _():
        pltpu.make_async_copy(qfull, qfull, rsend).wait()

    def gathered(half):
        own_half = jnp.logical_and(owns, mine // PARTS == half)

        @pl.when(own_half)
        def _():
            got = pl.ds(0, PARTS - 1)
            pltpu.make_async_copy(qfull.at[got], qfull.at[got], arecv.at[half]).wait()

        @pl.when(jnp.logical_not(own_half))
        def _():
            got = pl.ds(0, PARTS)
            pltpu.make_async_copy(qfull.at[got], qfull.at[got], arecv.at[half]).wait()

    gathered(near)
    right = right_parts(columns_of([qfull[near * PARTS + j] for j in range(PARTS)]))
    approx = mm(left_v[...], right)
    cols = pl.ds(pl.multiple_of(near * span, LANES), span)
    m_v[:, cols] = 0.9 * m_v[:, cols] + approx
    e_v[:, cols] = e_v[:, cols] - approx
    qf_v[:, cols] = mm(q_root_t, right)

    gathered(far)
    qfar_v[...] = columns_of([qfull[far * PARTS + j] for j in range(PARTS)])

    count = chunks

    @pl.when(owns)
    def _():
        got = pl.ds(0, count - 1)
        pltpu.make_async_copy(tiles.at[got], tiles.at[got], trecv).wait()

    @pl.when(jnp.logical_not(owns))
    def _():
        got = pl.ds(0, count)
        pltpu.make_async_copy(tiles.at[got], tiles.at[got], trecv).wait()

    tot_v[...] = total_of(tiles, count)

    @pl.when(owns)
    def _():
        for s in range(n_s):
            whole = pl.ds(0, n - 1 if s == keeper else n)
            pltpu.make_async_copy(rbuf.at[s, whole], rbuf.at[s, whole], asend).wait()
        sent = tiles.at[pl.ds(0, n * n_s - 1)]
        pltpu.make_async_copy(sent, sent, tsend).wait()


def finish(
    n_dp, entries,
    e_v, pf_v, qf_v, m_v, w_v, vmo_v, vp_v, tot_v, left_v, qrt_v, qfar_v,
    eo_hbm, pf_hbm, qf_hbm, mo_hbm, wo_hbm, vmo_hbm, vpo_hbm,
    eo_v, mo_v, wo_v, qff_v, vpo_v, sems,
):
    copies = []
    span = qfar_v.shape[1]
    near = pl.multiple_of(near_half(n_dp) * span, LANES)
    far = pl.multiple_of(span - near, LANES)
    cols = pl.ds(near, span)

    def write(src, dst):
        copy = pltpu.make_async_copy(src, dst, sems.at[len(copies)])
        copy.start()
        copies.append(copy)

    write(e_v.at[:, cols], eo_hbm.at[:, cols])
    write(m_v.at[:, cols], mo_hbm.at[:, cols])
    write(qf_v.at[:, cols], qf_hbm.at[:, cols])
    write(pf_v, pf_hbm)
    write(vmo_v, vmo_hbm)
    total = jnp.maximum(jnp.sum(tot_v[...], axis=1, keepdims=True), 0.0)
    scale = 0.05 / jnp.sqrt(total / entries + 1e-06)
    for c in range(span // LANES):
        here = pl.ds(c * LANES, LANES)
        cols = pl.ds(pl.multiple_of(far + c * LANES, LANES), LANES)
        right = right_parts(qfar_v[:, here])
        approx = mm(left_v[...], right)
        new = 0.9 * m_v[:, cols] + approx
        eo_v[:, here] = e_v[:, cols] - approx
        write(eo_v.at[:, here], eo_hbm.at[:, cols])
        mo_v[:, here] = new
        write(mo_v.at[:, here], mo_hbm.at[:, cols])
        wo_v[:, cols] = w_v[:, cols] - scale * new
        write(wo_v.at[:, cols], wo_hbm.at[:, cols])
        qff_v[:, here] = mm(qrt_v[...], right)
        write(qff_v.at[:, here], qf_hbm.at[:, cols])
    cols = pl.ds(near, span)
    wo_v[:, cols] = w_v[:, cols] - scale * m_v[:, cols]
    write(wo_v.at[:, cols], wo_hbm.at[:, cols])
    vpo_v[...] = vp_v[...] - scale.reshape(1, 1, 1) * vmo_v[...]
    write(vpo_v, vpo_hbm)
    for copy in copies:
        copy.wait()


def shards(
    sizes,
    grads, errors, q_prev, p_root, q_root, momentum, weights, vec_grads, vec_momentum, vec_params,
):
    n_dp, n_t, n_s = sizes
    rows, width = errors.shape[2:]
    rank = q_prev.shape[2]
    vecs, entries = vec_params.shape[1:]
    n = n_dp * n_t
    chunks = HALVES * PARTS
    span = width // HALVES
    n_blocks = len(row_blocks(rows))
    big = (rows, width)
    vec = (vecs, 1, entries)
    packed = (packed_rows(rank, rows), LANES)
    chunk = (rank * USED // LANES, LANES)
    any_space = pl.BlockSpec(memory_space=pl.ANY)
    in_vmem = pl.BlockSpec(memory_space=pltpu.VMEM)
    dma = pltpu.SemaphoreType.DMA
    vmem = pltpu.VMEM
    args = (
        grads[0, 0],
        errors[0, 0],
        q_prev[0].T,
        p_root[0],
        q_root[0],
        momentum[0],
        weights[0],
        vec_grads[0, 0][:, None, :],
        vec_momentum[0][:, None, :],
        vec_params[0][:, None, :],
    )
    shapes = (big, (rank, rows), (rank, width), big, big, vec, vec)
    kept = tuple(vmem(shape, F32) for shape in shapes + ((1, LANES),)) + (
        vmem((rows, 3 * rank), BF16),
        vmem((rank, 3 * rank), BF16),
        vmem((rank, span), F32),
    )
    outs = pl.pallas_call(
        functools.partial(kernel, sizes),
        out_shape=kept,
        in_specs=[any_space] * 10,
        out_specs=(in_vmem,) * len(kept),
        scratch_shapes=[
            vmem(big, BF16),
            vmem((rank, width), F32),
            vmem((rank, rank), F32),
            vmem((rank, rank), F32),
            vmem(vec, F32),
            vmem((HALVES, rows, span), BF16),
            vmem((HALVES, rows, span), BF16),
            vmem((rows, span), BF16),
            vmem((rows, span), BF16),
            vmem((8, LANES), F32),
            vmem((n_dp,) + packed, F32),
            vmem((n_dp,) + vec, F32),
            vmem((packed_rows(rank, rank) + 8, LANES), F32),
            vmem((n_s, n_t, packed_rows(rank, rank) + 8, LANES), F32),
            vmem((PARTS,) + chunk, F32),
            vmem((n_s, n_t) + chunk, F32),
            vmem((chunks,) + chunk, F32),
            vmem((n_s, n) + chunk, F32),
            vmem((n_s,) + chunk, F32),
            vmem((chunks,) + chunk, F32),
            vmem((n * n_s, 1, LANES), F32),
            dma((9 + 2 * n_blocks,)),
            dma(()), dma(()), dma(()), dma(()),
            dma((PARTS,)), dma((n_s,)), dma((PARTS,)), dma((n_s,)),
            dma(()), dma((n_s,)), dma(()), dma((HALVES,)), dma(()), dma(()),
        ],
        compiler_params=pltpu.CompilerParams(
            collective_id=0, has_side_effects=True, vmem_limit_bytes=48 * 1024 * 1024
        ),
    )(*(pltpu.with_memory_space_constraint(arg, pltpu.HBM) for arg in args))
    outs = pl.pallas_call(
        functools.partial(finish, n_dp, n_s * (width * width + vecs * width)),
        out_shape=tuple(pltpu.HBM(shape, F32) for shape in shapes),
        in_specs=[in_vmem] * len(kept),
        out_specs=(any_space,) * 7,
        scratch_shapes=[
            vmem((rows, span), F32),
            vmem((rows, span), F32),
            vmem(big, F32),
            vmem((rank, span), F32),
            vmem(vec, F32),
            dma((7 + 4 * (span // LANES),)),
        ],
    )(*(pltpu.with_memory_space_constraint(out, pltpu.VMEM) for out in outs))
    errors_out, p_factor, q_factor, momentum_out, weights_out, vec_momentum_out, vec_params_out = outs
    return (
        errors_out[None, None],
        p_factor.T[None],
        q_factor.T[None],
        momentum_out[None],
        weights_out[None],
        vec_momentum_out[:, 0][None],
        vec_params_out[:, 0][None],
    )


def solution(mesh):
    sizes = (mesh.shape["dp"], mesh.shape["tensor"], mesh.shape["section"])
    in_specs = (
        P("dp", "section", "tensor", None),
        P("dp", "section", "tensor", None),
        P("section", None, None),
        P("section", None, None),
        P("section", None, None),
        P("section", "tensor", None),
        P("section", "tensor", None),
        P("dp", "section", None, "tensor"),
        P("section", None, "tensor"),
        P("section", None, "tensor"),
    )
    out_specs = (
        P("dp", "section", "tensor", None),
        P("section", "tensor", None),
        P("section", None, None),
        P("section", "tensor", None),
        P("section", "tensor", None),
        P("section", None, "tensor"),
        P("section", None, "tensor"),
    )
    return jax.shard_map(
        functools.partial(shards, sizes),
        mesh=mesh, in_specs=in_specs, out_specs=out_specs, check_vma=False,
    )
```

```python
import functools

import jax
import jax.numpy as jnp
from jax import lax
from jax.experimental import pallas as pl
from jax.experimental.pallas import tpu as pltpu
from jax.sharding import PartitionSpec as P

F32 = jnp.float32
BF16 = jnp.bfloat16
MESH = pl.DeviceIdType.MESH
LANES = 128
UNROLL = 32
HALVES = 2
PARTS = 4
USED = 96
PIECE = 32


def split(x):
    high = x.astype(BF16)
    return high, (x - high.astype(F32)).astype(BF16)


def mm(a, b, dims=((1,), (0,))):
    return lax.dot_general(a, b, (dims, ((), ())), preferred_element_type=F32)


def left_parts(x):
    high, low = split(x)
    return jnp.concatenate([high, high, low], axis=1)


def right_parts(x):
    high, low = split(x)
    return jnp.concatenate([high, low, high], axis=0)


def each(count, body):
    if count <= UNROLL:
        for i in range(count):
            body(i)
    else:
        lax.fori_loop(0, count, lambda i, c: (body(i), c)[1], 0)


def total_of(ref, count):
    if count <= UNROLL:
        total = ref[0]
        for i in range(1, count):
            total = total + ref[i]
        return total
    return lax.fori_loop(1, count, lambda i, acc: acc + ref[i], ref[0])


def row_blocks(rows):
    return [(r, min(LANES, rows - r)) for r in range(0, rows, LANES)]


def packed_rows(rank, rows):
    return rank * rows // LANES


def pack(part):
    rank, size = part.shape
    count = LANES // size
    step = rank // count
    return jnp.concatenate([part[i * step : (i + 1) * step] for i in range(count)], axis=1)


def unpack(x, rank, rows):
    parts = []
    for start, size in row_blocks(rows):
        count = LANES // size
        step = rank // count
        block = x[rank * start // LANES :][:step]
        parts.append(
            jnp.concatenate([block[:, i * size : (i + 1) * size] for i in range(count)], axis=0)
        )
    return jnp.concatenate(parts, axis=1)


def lanes_of(shape):
    return lax.broadcasted_iota(jnp.int32, shape, 1)


def chunks_of(x):
    tiles = [x[:, b * LANES : (b + 1) * LANES] for b in range(3)]
    lane = lanes_of((8, LANES))
    chunks = []
    for tile in tiles:
        tail = tile[24:]
        chunks.append(
            [
                jnp.where(lane < USED, tile[8 * p : 8 * p + 8], pltpu.roll(tail, USED - PIECE * p, 1))
                for p in range(3)
            ]
        )
    rest = last_columns(tiles)
    chunks.append(
        [jnp.where(lane < USED, rest[8 * p : 8 * p + 8], tiles[p][24:]) for p in range(3)]
    )
    return [jnp.concatenate(chunk, axis=0) for chunk in chunks]


def last_columns(tiles):
    lane = lanes_of(tiles[0].shape)
    rolled = [pltpu.roll(tile, PIECE * (b + 1), 1) for b, tile in enumerate(tiles)]
    return jnp.where(lane < PIECE, rolled[0], jnp.where(lane < 2 * PIECE, rolled[1], rolled[2]))


def chunk_tail(chunk):
    lane = lanes_of((8, LANES))
    rolled = [pltpu.roll(chunk[8 * p : 8 * p + 8], PIECE * (p + 1), 1) for p in range(3)]
    return jnp.where(lane < PIECE, rolled[0], jnp.where(lane < 2 * PIECE, rolled[1], rolled[2]))


def columns_of(chunks):
    lane = lanes_of((8, LANES))
    last = chunks[3]
    tiles = []
    for j in range(3):
        rows = [
            jnp.where(
                lane < USED,
                chunks[j][8 * p : 8 * p + 8],
                pltpu.roll(last[8 * p : 8 * p + 8], USED - PIECE * j, 1),
            )
            for p in range(3)
        ]
        rows.append(jnp.where(lane < USED, chunk_tail(chunks[j]), last[8 * j : 8 * j + 8]))
        tiles.append(jnp.concatenate(rows, axis=0))
    return jnp.concatenate(tiles, axis=1)


def near_half(n_dp):
    return jnp.where(2 * lax.axis_index("dp") < n_dp, 0, 1)


def kernel(
    sizes,
    g_hbm, e_hbm, qt_hbm, pr_hbm, qr_hbm, m_hbm, w_hbm, vg_hbm, vm_hbm, vp_hbm,
    e_v, pf_v, qf_v, m_v, w_v, vmo_v, vp_v, tot_v, left_v, qrt_v, qfar_v,
    g_v, qt_v, pr_v, qr_v, vm_v,
    hi_v, lo_v, mhi_v, mlo_v, msq_v, pbuf, vbuf, gsend, gbuf, wsend, wbuf, qpart, rbuf, qsum_v, qfull, tiles,
    in_sem, psend, precv, vsend, vrecv, gsend_sem, grecv, wsend_sem, wrecv,
    rsend, rrecv, asend, arecv, tsend, trecv,
):
    n_dp, n_t, n_s = sizes
    n = n_dp * n_t
    group = n_t * n_s
    dp, tn, sc = lax.axis_index("dp"), lax.axis_index("tensor"), lax.axis_index("section")
    me = dp * n_t + tn
    rank, width = qt_v.shape
    rows = e_v.shape[0]
    span = width // HALVES
    gram_rows = packed_rows(rank, rank)
    chunks = HALVES * PARTS
    first_plane = n_dp // 2 - 1
    plane = dp - first_plane
    keeper = n_s - 1
    mine = plane * PARTS + tn
    in_plane = jnp.logical_and(plane >= 0, plane < HALVES)
    owns = jnp.logical_and(jnp.logical_and(in_plane, tn < PARTS), sc == keeper)
    upper = 2 * dp < n_dp
    near = near_half(n_dp)
    far = 1 - near

    def load(i, src, dst):
        copy = pltpu.make_async_copy(src, dst, in_sem.at[i])
        copy.start()
        return copy

    blocks = row_blocks(rows)
    in_q = load(0, qt_hbm, qt_v)
    in_pr = load(1, pr_hbm, pr_v)
    in_g, in_e = [], []
    for b, (start, size) in enumerate(blocks):
        at = pl.ds(start, size)
        in_g.append(load(9 + 2 * b, g_hbm.at[at], g_v.at[at]))
        in_e.append(load(10 + 2 * b, e_hbm.at[at], e_v.at[at]))
    in_vg = load(2, vg_hbm, vbuf.at[dp])
    in_qr = load(3, qr_hbm, qr_v)
    in_vm = load(4, vm_hbm, vm_v)
    in_m = load(5, m_hbm, m_v)
    in_vp = load(6, vp_hbm, vp_v)
    in_w = load(7, w_hbm, w_v)

    barrier = pltpu.get_barrier_semaphore()
    slot = sc * n_t + tn

    def line_peer(i):
        up, down = n_dp - 1 - i, i
        return jnp.where(
            upper, jnp.where(up > dp, up, up - 1), jnp.where(down < dp, down, down + 1)
        )

    def greet_line(i):
        pl.semaphore_signal(
            barrier, inc=1, device_id=(line_peer(i), tn, sc), device_id_type=MESH
        )

    def greet_plane(i):
        peer = lax.rem(slot + 1 + i, group)
        pl.semaphore_signal(
            barrier, inc=1, device_id=(dp, lax.rem(peer, n_t), peer // n_t), device_id_type=MESH
        )

    each(n_dp - 1, greet_line)
    each(group - 1, greet_plane)

    in_q.wait()
    in_pr.wait()
    q_hi, q_lo = split(mm(left_parts(pr_v[...].T), right_parts(qt_v[...])))
    q_both = jnp.concatenate([q_hi, q_lo], axis=0)
    for b, (start, size) in enumerate(blocks):
        at = pl.ds(start, size)
        in_g[b].wait()
        in_e[b].wait()
        merged = g_v[at, :].astype(F32) + e_v[at, :]
        e_v[at, :] = merged
        m_hi, m_lo = split(merged)
        for p in range(HALVES):
            hi_v[p, at, :] = m_hi[:, p * span : (p + 1) * span]
            lo_v[p, at, :] = m_lo[:, p * span : (p + 1) * span]
        first = mm(q_both, m_hi, ((1,), (1,)))
        second = mm(q_hi, m_lo, ((1,), (1,)))
        pbuf[dp, pl.ds(rank * start // LANES, rank * size // LANES), :] = pack(
            first[:rank] + first[rank:] + second
        )

    pl.semaphore_wait(barrier, n_dp - 1 + group - 1)

    def send_p(i):
        pltpu.make_async_remote_copy(
            pbuf.at[dp], pbuf.at[dp], psend, precv,
            device_id=(line_peer(i), tn, sc), device_id_type=MESH,
        ).start()

    def send_v(i):
        pltpu.make_async_remote_copy(
            vbuf.at[dp], vbuf.at[dp], vsend, vrecv,
            device_id=(line_peer(i), tn, sc), device_id_type=MESH,
        ).start()

    each(n_dp - 1, send_p)
    in_vg.wait()
    each(n_dp - 1, send_v)

    in_m.wait()
    in_qr.wait()
    in_vm.wait()
    in_vp.wait()
    in_w.wait()
    q_root_left = left_parts(qr_v[...])
    q_root_t = left_parts(qr_v[...].T)
    qrt_v[...] = q_root_t

    old = m_v[:, pl.ds(pl.multiple_of(near * span, LANES), span)]
    m_hi, m_lo = split(old)
    mhi_v[...] = m_hi
    mlo_v[...] = m_lo
    old = 0.9 * old
    squares = jnp.zeros((8, LANES), F32)
    for c in range(span // LANES):
        tile = old[:, c * LANES : (c + 1) * LANES]
        squares = squares + jnp.sum((tile * tile).reshape(rows // 8, 8, LANES), axis=0)
    msq_v[...] = squares

    others = pl.ds(0, n_dp - 1)
    pltpu.make_async_copy(pbuf.at[others], pbuf.at[others], precv).wait()
    pf = unpack(total_of(pbuf, n_dp), rank, rows)
    pf_hi, pf_lo = split(pf)
    pf_both = jnp.concatenate([pf_hi, pf_lo], axis=0)

    def q_parts(p):
        first = mm(pf_both, hi_v[p])
        second = mm(pf_hi, lo_v[p])
        return chunks_of(first[:rank] + first[rank:] + second)

    def send_q(k, owner_dp, j):
        pltpu.make_async_remote_copy(
            qpart.at[k], rbuf.at[sc, me], rsend, rrecv.at[sc],
            device_id=(owner_dp, j, keeper), device_id_type=MESH,
        ).start()

    parts = q_parts(far)
    for j in range(PARTS):
        qpart[far * PARTS + j] = parts[j]
    left_t = mm(q_root_left, right_parts(pf)) / n_dp
    largest = jnp.max(jnp.max(jnp.abs(left_t), axis=1, keepdims=True), axis=0, keepdims=True)
    unit = left_t / jnp.where(largest > 0, largest, 1.0)
    u_hi, u_lo = split(unit)
    for j in range(PARTS):
        send_q(far * PARTS + j, first_plane + far, j)

    parts = q_parts(near)
    first = mm(jnp.concatenate([u_hi, u_lo], axis=0), mhi_v[...])
    second = mm(u_hi, mlo_v[...])
    product = first[:rank] + first[rank:] + second
    products = chunks_of(product)
    gram = mm(left_parts(unit), jnp.concatenate([u_hi, u_lo, u_hi], axis=1), ((1,), (1,)))
    gsend[0:gram_rows, :] = pack(gram)
    for j in range(PARTS):
        qpart[near * PARTS + j] = parts[j]
        wsend[j] = products[j]
    def give_product(j):
        return pltpu.make_async_remote_copy(
            wsend.at[j], wbuf.at[sc, tn], wsend_sem.at[j], wrecv.at[sc],
            device_id=(dp, j, keeper), device_id_type=MESH,
        )

    def give_gram(j):
        return pltpu.make_async_remote_copy(
            gsend, gbuf.at[sc, tn], gsend_sem.at[j], grecv.at[sc],
            device_id=(dp, j, keeper), device_id_type=MESH,
        )

    def stays(j):
        return jnp.logical_and(tn == j, sc == keeper)

    @pl.when(in_plane)
    def _():
        for j in range(PARTS):

            @pl.when(stays(j))
            def _():
                wbuf[keeper, tn] = wsend[j]

            @pl.when(jnp.logical_not(stays(j)))
            def _():
                give_product(j).start()

        pltpu.make_async_copy(vbuf.at[others], vbuf.at[others], vrecv).wait()
        v_new = 0.9 * vm_v[...] + total_of(vbuf, n_dp) / n_dp
        v_row = jnp.sum(v_new * v_new, axis=0)
        v_squares = jnp.zeros((1, LANES), F32)
        for start, size in row_blocks(v_row.shape[1]):
            piece = v_row[:, start : start + size]
            if size < LANES:
                piece = jnp.concatenate([piece, jnp.zeros((1, LANES - size), F32)], axis=1)
            v_squares = v_squares + piece
        squares = jnp.sum(msq_v[...], axis=0, keepdims=True)
        squares = squares + jnp.where(plane == 0, v_squares, 0.0)
        row = lax.broadcasted_iota(jnp.int32, (8, LANES), 0)
        gsend[gram_rows:, :] = jnp.where(row == 0, largest, squares)

        @pl.when(owns)
        def _():
            gbuf[keeper, tn] = gsend[...]

        for j in range(PARTS):

            @pl.when(jnp.logical_not(stays(j)))
            def _():
                give_gram(j).start()

    for j in range(PARTS):
        here = jnp.logical_and(owns, tn == j)

        @pl.when(here)
        def _():
            rbuf[keeper, me] = qpart[near * PARTS + j]

        @pl.when(jnp.logical_not(here))
        def _():
            send_q(near * PARTS + j, first_plane + near, j)

    @pl.when(jnp.logical_not(in_plane))
    def _():
        pltpu.make_async_copy(vbuf.at[others], vbuf.at[others], vrecv).wait()

    pf_v[...] = pf
    left_v[...] = left_parts(left_t.T)
    vmo_v[...] = 0.9 * vm_v[...] + total_of(vbuf, n_dp) / n_dp

    @pl.when(owns)
    def _():
        used = lanes_of((rank, LANES)) < USED

        def prepare(s):
            rest = pl.ds(0, n_t - 1 if s == keeper else n_t)
            pltpu.make_async_copy(wbuf.at[s, rest], wbuf.at[s, rest], wrecv.at[s]).wait()
            pltpu.make_async_copy(gbuf.at[s, rest], gbuf.at[s, rest], grecv.at[s]).wait()
            levels = [gbuf[s, t, gram_rows : gram_rows + 1, :] for t in range(n_t)]
            level = levels[0]
            for t in range(1, n_t):
                level = jnp.maximum(level, levels[t])
            inverse = 1.0 / jnp.where(level > 0, level, 1.0)
            product = jnp.zeros((rank * USED // LANES, LANES), F32)
            gram = jnp.zeros((gram_rows, LANES), F32)
            for t in range(n_t):
                share = levels[t] * inverse
                product = product + share * wbuf[s, t]
                gram = gram + share * share * gbuf[s, t, 0:gram_rows, :]
            product = jnp.concatenate([product, chunk_tail(product)], axis=0)
            product = jnp.where(used, 1.8 * product, 0.0)
            gram = left_parts(unpack(gram, rank, rank))
            return product, gram, level, gbuf[s, tn, gram_rows + 1 : gram_rows + 2, :]

        def row_of(q_sum, prepared):
            product, gram, level, squares = prepared
            scaled = jnp.concatenate([q_sum, chunk_tail(q_sum)], axis=0) * level
            scaled = jnp.where(used, scaled, 0.0)
            terms = scaled * (product + mm(gram, right_parts(scaled)))
            return jnp.sum(terms, axis=0, keepdims=True) + squares

        def summed(s):
            whole = pl.ds(0, n - 1 if s == keeper else n)
            pltpu.make_async_copy(rbuf.at[s, whole], rbuf.at[s, whole], rrecv.at[s]).wait()
            q_sum = total_of(rbuf.at[s], n)
            qsum_v[s] = q_sum
            return q_sum

        def send_sum(s, i):
            peer = i + jnp.where(i >= me, 1, 0) if s == keeper else i
            pltpu.make_async_remote_copy(
                qsum_v.at[s], qfull.at[mine], asend, arecv.at[plane],
                device_id=(peer // n_t, lax.rem(peer, n_t), s), device_id_type=MESH,
            ).start()

        def send_row(i):
            peer = i + jnp.where(i >= me * n_s + sc, 1, 0)
            pltpu.make_async_remote_copy(
                tiles.at[mine], tiles.at[mine], tsend, trecv,
                device_id=(peer // group, lax.rem(peer // n_s, n_t), lax.rem(peer, n_s)),
                device_id_type=MESH,
            ).start()

        q_sum = summed(keeper)
        qfull[mine] = q_sum
        each(n - 1, lambda i: send_sum(keeper, i))
        row = row_of(q_sum, prepare(keeper))
        for s in range(keeper):
            prepared = prepare(s)
            q_sum = summed(s)
            send_sum(s, 0)
            row = row + row_of(q_sum, prepared)
            if s < keeper - 1:
                each(n - 1, lambda i: send_sum(s, 1 + i))
        tiles[mine] = row
        each(n * n_s - 1, send_row)
        each(n - 1, lambda i: send_sum(keeper - 1, 1 + i))

    pltpu.make_async_copy(pbuf.at[others], pbuf.at[others], psend).wait()
    pltpu.make_async_copy(vbuf.at[others], vbuf.at[others], vsend).wait()

    @pl.when(in_plane)
    def _():
        for j in range(PARTS):

            @pl.when(jnp.logical_not(stays(j)))
            def _():
                give_product(j).wait_send()
                give_gram(j).wait_send()

    @pl.when(owns)
    def _():
        got = pl.ds(0, chunks - 1)
        pltpu.make_async_copy(qfull.at[got], qfull.at[got], rsend).wait()

    @pl.when(jnp.logical_not(owns))
    def _():
        pltpu.make_async_copy(qfull, qfull, rsend).wait()

    @pl.when(owns)
    def _():
        got = pl.ds(0, PARTS - 1)
        pltpu.make_async_copy(qfull.at[got], qfull.at[got], arecv.at[near]).wait()

    @pl.when(jnp.logical_not(owns))
    def _():
        got = pl.ds(0, PARTS)
        pltpu.make_async_copy(qfull.at[got], qfull.at[got], arecv.at[near]).wait()

    right = right_parts(columns_of([qfull[near * PARTS + j] for j in range(PARTS)]))
    approx = mm(left_v[...], right)
    cols = pl.ds(pl.multiple_of(near * span, LANES), span)
    m_v[:, cols] = 0.9 * m_v[:, cols] + approx
    e_v[:, cols] = e_v[:, cols] - approx
    qf_v[:, cols] = mm(q_root_t, right)

    got = pl.ds(0, PARTS)
    pltpu.make_async_copy(qfull.at[got], qfull.at[got], arecv.at[far]).wait()
    qfar_v[...] = columns_of([qfull[far * PARTS + j] for j in range(PARTS)])

    count = chunks

    @pl.when(owns)
    def _():
        got = pl.ds(0, count - 1)
        pltpu.make_async_copy(tiles.at[got], tiles.at[got], trecv).wait()

    @pl.when(jnp.logical_not(owns))
    def _():
        got = pl.ds(0, count)
        pltpu.make_async_copy(tiles.at[got], tiles.at[got], trecv).wait()

    tot_v[...] = total_of(tiles, count)

    @pl.when(owns)
    def _():
        for s in range(n_s):
            whole = pl.ds(0, n - 1 if s == keeper else n)
            pltpu.make_async_copy(rbuf.at[s, whole], rbuf.at[s, whole], asend).wait()
        sent = tiles.at[pl.ds(0, n * n_s - 1)]
        pltpu.make_async_copy(sent, sent, tsend).wait()


def finish(
    n_dp, entries,
    e_v, pf_v, qf_v, m_v, w_v, vmo_v, vp_v, tot_v, left_v, qrt_v, qfar_v,
    eo_hbm, pf_hbm, qf_hbm, mo_hbm, wo_hbm, vmo_hbm, vpo_hbm,
    eo_v, mo_v, wo_v, qff_v, vpo_v, sems,
):
    copies = []
    span = qfar_v.shape[1]
    near = pl.multiple_of(near_half(n_dp) * span, LANES)
    far = pl.multiple_of(span - near, LANES)
    cols = pl.ds(near, span)

    def write(src, dst):
        copy = pltpu.make_async_copy(src, dst, sems.at[len(copies)])
        copy.start()
        copies.append(copy)

    write(e_v.at[:, cols], eo_hbm.at[:, cols])
    write(m_v.at[:, cols], mo_hbm.at[:, cols])
    write(qf_v.at[:, cols], qf_hbm.at[:, cols])
    write(pf_v, pf_hbm)
    write(vmo_v, vmo_hbm)
    total = jnp.maximum(jnp.sum(tot_v[...], axis=1, keepdims=True), 0.0)
    scale = 0.05 / jnp.sqrt(total / entries + 1e-06)
    for here, cols in [(pl.ds(0, span), pl.ds(far, span))]:
        right = right_parts(qfar_v[:, here])
        approx = mm(left_v[...], right)
        new = 0.9 * m_v[:, cols] + approx
        eo_v[:, here] = e_v[:, cols] - approx
        write(eo_v.at[:, here], eo_hbm.at[:, cols])
        mo_v[:, here] = new
        write(mo_v.at[:, here], mo_hbm.at[:, cols])
        wo_v[:, cols] = w_v[:, cols] - scale * new
        write(wo_v.at[:, cols], wo_hbm.at[:, cols])
        qff_v[:, here] = mm(qrt_v[...], right)
        write(qff_v.at[:, here], qf_hbm.at[:, cols])
    cols = pl.ds(near, span)
    wo_v[:, cols] = w_v[:, cols] - scale * m_v[:, cols]
    write(wo_v.at[:, cols], wo_hbm.at[:, cols])
    vpo_v[...] = vp_v[...] - scale.reshape(1, 1, 1) * vmo_v[...]
    write(vpo_v, vpo_hbm)
    for copy in copies:
        copy.wait()


def shards(
    sizes,
    grads, errors, q_prev, p_root, q_root, momentum, weights, vec_grads, vec_momentum, vec_params,
):
    n_dp, n_t, n_s = sizes
    rows, width = errors.shape[2:]
    rank = q_prev.shape[2]
    vecs, entries = vec_params.shape[1:]
    n = n_dp * n_t
    chunks = HALVES * PARTS
    span = width // HALVES
    n_blocks = len(row_blocks(rows))
    big = (rows, width)
    vec = (vecs, 1, entries)
    packed = (packed_rows(rank, rows), LANES)
    chunk = (rank * USED // LANES, LANES)
    any_space = pl.BlockSpec(memory_space=pl.ANY)
    in_vmem = pl.BlockSpec(memory_space=pltpu.VMEM)
    dma = pltpu.SemaphoreType.DMA
    vmem = pltpu.VMEM
    args = (
        grads[0, 0],
        errors[0, 0],
        q_prev[0].T,
        p_root[0],
        q_root[0],
        momentum[0],
        weights[0],
        vec_grads[0, 0][:, None, :],
        vec_momentum[0][:, None, :],
        vec_params[0][:, None, :],
    )
    shapes = (big, (rank, rows), (rank, width), big, big, vec, vec)
    kept = tuple(vmem(shape, F32) for shape in shapes + ((1, LANES),)) + (
        vmem((rows, 3 * rank), BF16),
        vmem((rank, 3 * rank), BF16),
        vmem((rank, span), F32),
    )
    outs = pl.pallas_call(
        functools.partial(kernel, sizes),
        out_shape=kept,
        in_specs=[any_space] * 10,
        out_specs=(in_vmem,) * len(kept),
        scratch_shapes=[
            vmem(big, BF16),
            vmem((rank, width), F32),
            vmem((rank, rank), F32),
            vmem((rank, rank), F32),
            vmem(vec, F32),
            vmem((HALVES, rows, span), BF16),
            vmem((HALVES, rows, span), BF16),
            vmem((rows, span), BF16),
            vmem((rows, span), BF16),
            vmem((8, LANES), F32),
            vmem((n_dp,) + packed, F32),
            vmem((n_dp,) + vec, F32),
            vmem((packed_rows(rank, rank) + 8, LANES), F32),
            vmem((n_s, n_t, packed_rows(rank, rank) + 8, LANES), F32),
            vmem((PARTS,) + chunk, F32),
            vmem((n_s, n_t) + chunk, F32),
            vmem((chunks,) + chunk, F32),
            vmem((n_s, n) + chunk, F32),
            vmem((n_s,) + chunk, F32),
            vmem((chunks,) + chunk, F32),
            vmem((n * n_s, 1, LANES), F32),
            dma((9 + 2 * n_blocks,)),
            dma(()), dma(()), dma(()), dma(()),
            dma((PARTS,)), dma((n_s,)), dma((PARTS,)), dma((n_s,)),
            dma(()), dma((n_s,)), dma(()), dma((HALVES,)), dma(()), dma(()),
        ],
        compiler_params=pltpu.CompilerParams(
            collective_id=0, has_side_effects=True, vmem_limit_bytes=48 * 1024 * 1024
        ),
    )(*(pltpu.with_memory_space_constraint(arg, pltpu.HBM) for arg in args))
    outs = pl.pallas_call(
        functools.partial(finish, n_dp, n_s * (width * width + vecs * width)),
        out_shape=tuple(pltpu.HBM(shape, F32) for shape in shapes),
        in_specs=[in_vmem] * len(kept),
        out_specs=(any_space,) * 7,
        scratch_shapes=[
            vmem((rows, span), F32),
            vmem((rows, span), F32),
            vmem(big, F32),
            vmem((rank, span), F32),
            vmem(vec, F32),
            dma((11,)),
        ],
    )(*(pltpu.with_memory_space_constraint(out, pltpu.VMEM) for out in outs))
    errors_out, p_factor, q_factor, momentum_out, weights_out, vec_momentum_out, vec_params_out = outs
    return (
        errors_out[None, None],
        p_factor.T[None],
        q_factor.T[None],
        momentum_out[None],
        weights_out[None],
        vec_momentum_out[:, 0][None],
        vec_params_out[:, 0][None],
    )


def solution(mesh):
    sizes = (mesh.shape["dp"], mesh.shape["tensor"], mesh.shape["section"])
    in_specs = (
        P("dp", "section", "tensor", None),
        P("dp", "section", "tensor", None),
        P("section", None, None),
        P("section", None, None),
        P("section", None, None),
        P("section", "tensor", None),
        P("section", "tensor", None),
        P("dp", "section", None, "tensor"),
        P("section", None, "tensor"),
        P("section", None, "tensor"),
    )
    out_specs = (
        P("dp", "section", "tensor", None),
        P("section", "tensor", None),
        P("section", None, None),
        P("section", "tensor", None),
        P("section", "tensor", None),
        P("section", None, "tensor"),
        P("section", None, "tensor"),
    )
    return jax.shard_map(
        functools.partial(shards, sizes),
        mesh=mesh, in_specs=in_specs, out_specs=out_specs, check_vma=False,
    )
```
